32 devices in a mesh: group: 2 (over y), gene: 4 (over z), lat: 2 (over x), sub: 2 (over core).
Axes of the slice: x: 2, y: 2, z: 4, core: 2. Of those that a mesh axis runs over, the one named last changes fastest.
Arguments:
- cell_index: int32 [2048], P(('group', 'lat', 'sub')), parts along dimension 0, may hold values from 0 to 511
- coords_table: float32 [4, 2048], P('group', ('lat', 'sub')), parts along dimension 0, may hold values from 0 to 1
- expr_table: bfloat16 [4096, 16384], P(('group', 'lat', 'sub'), 'gene'), parts along dimension 0, may hold values from -6 to 6
- inducing: float32 [4, 64, 8192], P('group', 'lat', 'sub'), parts along dimension 0, may hold values from 0 to 1
- ind_weights: float32 [128, 8192], P(('group', 'lat'), 'sub'), parts along dimension 0, may hold values from -0.6 to 0.6
- lengthscale: float32 [128], P(('group', 'lat')), parts along dimension 0, may hold values from 0.02 to 0.1
- variance: float32 [128], P(('group', 'lat')), parts along dimension 0, may hold values from 0.5 to 2
- mixing: bfloat16 [128, 16384], P('group', 'gene'), parts along dimension 0, may hold values from -0.75 to 0.75
- noise_prec: float32 [32768], P(('group', 'gene')), parts along dimension 0, may hold values from 0.5 to 4
Outputs:
- grad_mixing: float32 [128, 16384], P('group', 'gene'), parts along dimension 0
- grad_inducing: float32 [128, 8192], P(('group', 'lat'), 'sub'), parts along dimension 0
The draws below stay inside these ranges and needn't reach their ends.
There are 2 independent parts, one for each index of `group`. The reference program is written for one: setup_inputs(seed, part) draws one part's arguments, and reference() takes and returns one part's arrays. A program takes and returns all parts, laid end to end along the dimension named above; each array names one. Nothing has to cross between parts.
Inputs may be any that keep to these rules, and one draw needn't show every extreme that they name: Entry n indexes a row inside block n // 256 of the tables: cell n is table row (n // 256) * 512 + cell_index[n]; cells may repeat.
All inputs are finite; a program needn't handle non-finite values.
Results may differ from the reference program's by a relative error of at most 0.00075.
Values may be sent and summed in bfloat16 or wider, within the bound.
A program may use at most 64 MiB of HBM per device.

```python
import math
import jax
import jax.numpy as jnp
from jax import lax

G = 16384
Q = 64
M = 8192
BAT_DEV = 256
TAB_DEV = 512
BATCH = 1024
TABLE = 2048


def plant(result, own_key, least, largest):
    place = [jax.random.randint(jax.random.fold_in(own_key, axis), (), 0, length) for axis, length in enumerate(result.shape)]
    main_axis = result.shape.index(max(result.shape))
    next_to = place[:main_axis] + [(place[main_axis] + 1) % result.shape[main_axis]] + place[main_axis + 1:]
    return result.at[tuple(place)].set(least).at[tuple(next_to)].set(largest)


def levels(own_key, extent, cuts, smallest, high):
    level = 1.0
    for position, shards_of in cuts:
        draws = jax.random.uniform(jax.random.fold_in(jax.random.fold_in(own_key, 6), position), (shards_of,), jnp.float32, smallest / len(cuts), high / len(cuts))
        level = level * jnp.repeat(jnp.exp(draws), extent[position] // shards_of).reshape((-1,) + (1,) * (len(extent) - 1 - position))
    return level


def gaussian(key, dims, width, reach, cuts=(), kind=jnp.bfloat16):
    result = jax.random.normal(key, dims, jnp.float32) * width
    if len(cuts) > 0:
        result = levels(key, dims, cuts, -0.22, 0.18) * result
    return jnp.clip(result, min=-reach, max=reach).astype(kind)


def setup_inputs(seed: int = 0, part: int = 0) -> dict:
    keys = jax.random.split(jax.random.key(seed), 10)
    own_keys = jax.random.split(jax.random.fold_in(keys[9], part), 10)
    cell_index = plant(jax.random.randint(own_keys[0], (BATCH,), 0, TAB_DEV), jax.random.fold_in(own_keys[0], 1), 0, TAB_DEV - 1).astype(jnp.int32)
    coords_table = jnp.clip(1.0 * jax.random.uniform(own_keys[1], (2, TABLE), jnp.float32) ** levels(own_keys[1], (2, TABLE), ((1, 4),), -0.2, 0.2), 0.0, 1.0)
    expr_table = gaussian(own_keys[2], (TABLE, G), 1.0, 6.0, ((0, 4), (1, 4)))
    inducing = jnp.clip(1.0 * jax.random.uniform(own_keys[3], (2, Q, M), jnp.float32) ** levels(own_keys[3], (2, Q, M), ((1, 2), (2, 2)), -0.2, 0.2), 0.0, 1.0)
    ind_weights = gaussian(own_keys[4], (Q, M), 0.1, 0.6, ((0, 2), (1, 2)), jnp.float32)
    lengthscale = jnp.clip(jnp.exp(math.log(0.1) - 1.609438 * jax.random.uniform(own_keys[5], (Q,), jnp.float32) ** levels(own_keys[5], (Q,), ((0, 2),), -0.2, 0.2)), 0.02, 0.1)
    variance = jnp.clip(jnp.exp(math.log(2.0) - 1.3862944 * jax.random.uniform(own_keys[6], (Q,), jnp.float32) ** levels(own_keys[6], (Q,), ((0, 2),), -0.2, 0.2)), 0.5, 2.0)
    mixing = gaussian(own_keys[7], (Q, G), Q ** -0.5, 0.75, ((1, 4),))
    noise_prec = jnp.clip(jnp.exp(math.log(4.0) - 2.0794415 * jax.random.uniform(own_keys[8], (G,), jnp.float32) ** levels(own_keys[8], (G,), ((0, 4),), -0.2, 0.2)), 0.5, 4.0)
    return dict(cell_index=cell_index, coords_table=coords_table, expr_table=expr_table, inducing=inducing, ind_weights=ind_weights, lengthscale=lengthscale, variance=variance, mixing=mixing, noise_prec=noise_prec)


def kernel_tile(cell_xy, points, length, height):
    delta_x = cell_xy[0][:, None] - points[0][None, :]
    delta_y = cell_xy[1][:, None] - points[1][None, :]
    return height * jnp.exp(-(delta_x * delta_x + delta_y * delta_y) * (0.5 / (length * length)))

def reference(cell_index, coords_table, expr_table, inducing, ind_weights, lengthscale, variance, mixing, noise_prec):
    cell_count = cell_index.shape[0]
    block_start = jnp.arange(cell_count, dtype=jnp.int32) // BAT_DEV * TAB_DEV
    table_rows = block_start + cell_index.astype(jnp.int32)
    cell_xy = jnp.take(coords_table, table_rows, axis=1)
    observed = jnp.take(expr_table, table_rows, axis=0)
    moved = jnp.moveaxis(inducing, 1, 0)

    def forward(packed):
        points, weights, length, height = packed
        return jnp.dot(kernel_tile(cell_xy, points, length, height), weights, precision=lax.Precision.HIGHEST)
    latent = lax.map(forward, (moved, ind_weights, lengthscale, variance)).astype(jnp.bfloat16)
    predicted = lax.dot_general(latent, mixing, (((0,), (0,)), ((), ())), preferred_element_type=jnp.float32)
    weighted = (noise_prec[None, :] * (observed.astype(jnp.float32) - predicted)).astype(jnp.bfloat16)
    grad_scale = -1.0 / math.sqrt(cell_count)
    grad_mixing = grad_scale * jnp.dot(latent, weighted, preferred_element_type=jnp.float32)
    latent_grad = grad_scale * lax.dot_general(mixing, weighted, (((1,), (1,)), ((), ())), preferred_element_type=jnp.float32)

    def backward(packed):
        points, gradient, length, height = packed
        return jnp.dot(gradient, kernel_tile(cell_xy, points, length, height), precision=lax.Precision.HIGHEST)
    grad_inducing = lax.map(backward, (moved, latent_grad, lengthscale, variance))
    return (grad_mixing, grad_inducing)
```

```python
import functools
import math
from typing import NamedTuple

import jax
import jax.numpy as jnp
from jax import lax
from jax.experimental import pallas as pl
from jax.experimental.pallas import tpu as pltpu
from jax.sharding import PartitionSpec as P

F32 = jnp.float32
BF16 = jnp.bfloat16
DEPTH = 24
SPARE = 21
CENTER = 0.5
LOG2E = math.log2(math.e)
LEFT = (0, 0, 1, 1, 0, 2)
RIGHT = (0, 1, 0, 1, 2, 0)


class Plan(NamedTuple):
    gene: int
    lat: int
    sub: int
    rows: int
    table: int
    lats: int
    count: int
    genes: int
    share: int
    split: int
    sliced: bool
    scale: float

    @property
    def blocks(self):
        return self.lat * self.sub

    @property
    def points(self):
        return self.count // self.split

    @property
    def owners(self):
        return self.gene // self.split

    @property
    def total(self):
        return self.lat * self.lats

    @property
    def tile(self):
        return min(256, self.points)

    @property
    def wide(self):
        return min(512, self.genes)


def pieces(value):
    high = value.astype(BF16).astype(F32)
    rest = value - high
    middle = rest.astype(BF16).astype(F32)
    low = (rest - middle).astype(BF16).astype(F32)
    return high, middle, low


def point_features(plan, scale, points_ref, weight_ref, table_ref):
    step = min(512, plan.points)

    def part(i, carry):
        cols = pl.ds(pl.multiple_of(i * step, 128), step)
        x = points_ref[0, :, cols] - CENTER
        y = points_ref[1, :, cols] - CENTER
        px = pieces(x * (2.0 * scale))
        py = pieces(y * (2.0 * scale))
        ps = pieces(jnp.broadcast_to(-scale, x.shape))
        pn = pieces((x * x + y * y) * -scale)
        rows = [px[k] for k in RIGHT] + [py[k] for k in RIGHT] + [ps[k] for k in RIGHT]
        rows += list(pn) + [weight_ref[:, cols]] + [jnp.zeros_like(x)] * (DEPTH - SPARE - 1)
        for place, row in enumerate(rows):
            for lane in range(plan.share):
                table_ref[lane, place : place + 1, cols] = row[lane : lane + 1, :]
        return carry

    lax.fori_loop(0, plan.points // step, part, 0)


def cell_features(plan, xy_ref, side_ref, feat_ref):
    side_ref[...] = jnp.zeros_like(side_ref)
    side_ref[18:21, :] = jnp.ones((3, plan.rows), F32)
    for block in range(plan.blocks):
        x = xy_ref[block, 0:1, :] - CENTER
        y = xy_ref[block, 1:2, :] - CENTER
        px, py, pn = pieces(x), pieces(y), pieces(x * x + y * y)
        rows = [px[k] for k in LEFT] + [py[k] for k in LEFT] + [pn[k] for k in LEFT]
        for place, row in enumerate(rows):
            side_ref[place : place + 1, :] = row
        feat_ref[block * plan.rows : (block + 1) * plan.rows, :] = side_ref[...].T[:, :DEPTH].astype(BF16)


def body(
    plan,
    index_ref,
    coords_ref,
    length_ref,
    height_ref,
    expr_hbm,
    points_hbm,
    weight_hbm,
    mixing_hbm,
    noise_hbm,
    mix_out,
    ind_out,
    expr_ref,
    points_ref,
    weight_ref,
    mixing_ref,
    noise_ref,
    pick_ref,
    xy_ref,
    side_ref,
    feat_ref,
    table_ref,
    wide_ref,
    part_ref,
    near_ref,
    final_ref,
    latent_recv,
    latent_ref,
    side_lat_ref,
    seen_ref,
    cell_ref,
    chunk_ref,
    rs_ref,
    own_ref,
    lg_ref,
    lgpad_ref,
    mix_ref,
    mix_near,
    mix_far,
    mix_two,
    sum_ref,
    all_ref,
    load_sem,
    xy_sem,
    near_sem,
    latent_sem,
    rs_sem,
    lg_sem,
    mix_sem,
    all_sem,
):
    genes, lats, subs = plan.gene, plan.lat, plan.sub
    rows, share = plan.rows, plan.share
    g, l, s = lax.axis_index("gene"), lax.axis_index("lat"), lax.axis_index("sub")
    owner, slab = g // plan.split, lax.rem(g, plan.split)
    me = l * subs + s

    def at(dg=0, dl=0, ds=0):
        place = {}
        if genes > 1:
            place["gene"] = lax.rem(g + dg, genes)
        if lats > 1:
            place["lat"] = lax.rem(l + dl, lats)
        if subs > 1:
            place["sub"] = lax.rem(s + ds, subs)
        return place

    def send(src, dst, sems, k, device):
        copy = pltpu.make_async_remote_copy(
            src_ref=src,
            dst_ref=dst,
            send_sem=sems.at[(0, *k)],
            recv_sem=sems.at[(1, *k)],
            device_id=device,
            device_id_type=pl.DeviceIdType.MESH,
        )
        return copy

    if plan.sliced:
        points_src, weight_src = points_hbm, weight_hbm
    else:
        mine = pl.ds(pl.multiple_of(owner * share, 8), share)
        cut = pl.ds(pl.multiple_of(slab * plan.points, 128), plan.points)
        points_src, weight_src = points_hbm.at[:, mine, cut], weight_hbm.at[mine, cut]
    loads = [
        pltpu.make_async_copy(points_src, points_ref, load_sem.at[0]),
        pltpu.make_async_copy(weight_src, weight_ref, load_sem.at[1]),
        pltpu.make_async_copy(expr_hbm, expr_ref, load_sem.at[2]),
        pltpu.make_async_copy(mixing_hbm, mixing_ref, load_sem.at[3]),
        pltpu.make_async_copy(noise_hbm, noise_ref, load_sem.at[4]),
    ]
    for load in loads:
        load.start()

    far = [(dg, dl, 0) for dg in range(genes) for dl in range(lats) if dg or dl]
    flat = [(0, dl, ds) for dl in range(lats) for ds in range(subs) if dl or ds]
    peers = sorted(set(far) | set(flat))
    barrier = pltpu.get_barrier_semaphore()
    for peer in peers:
        pl.semaphore_signal(barrier, inc=1, device_id=at(*peer), device_id_type=pl.DeviceIdType.MESH)

    pick = lax.broadcasted_iota(jnp.int32, (plan.table, rows), 0) == index_ref[...]
    pick_ref[...] = pick.astype(F32).astype(BF16)
    local = jnp.zeros((2, rows), F32)
    for piece in pieces(coords_ref[...]):
        local = local + jnp.dot(piece.astype(BF16), pick_ref[...], preferred_element_type=F32)
    xy_ref[me] = local
    pl.semaphore_wait(barrier, len(peers))
    copies = []
    for k, peer in enumerate(flat):
        copies.append(send(xy_ref.at[me], xy_ref.at[me], xy_sem, (k,), at(*peer)))
        copies[-1].start()

    lane = lax.broadcasted_iota(jnp.int32, (share, plan.lats), 1)
    chosen = lane == lax.broadcasted_iota(jnp.int32, (share, plan.lats), 0) + owner * share
    length = jnp.sum(jnp.where(chosen, length_ref[...], 0.0), axis=1, keepdims=True)
    height = jnp.sum(jnp.where(chosen, height_ref[...], 0.0), axis=1, keepdims=True)
    loads[0].wait()
    loads[1].wait()
    point_features(plan, (0.5 * LOG2E) / (length * length), points_ref, weight_ref, table_ref)
    for copy in copies:
        copy.wait()
    cell_features(plan, xy_ref, side_ref, feat_ref)

    def forward(i, carry):
        j, block = i // plan.blocks, lax.rem(i, plan.blocks)
        feat = feat_ref[pl.ds(pl.multiple_of(block * rows, rows), rows), :]
        total = jnp.zeros((rows, 128), F32)
        for start in range(0, plan.points, plan.tile):
            part = table_ref[j, :, start : start + plan.tile].astype(BF16)
            value = jnp.exp2(jnp.dot(feat, part, preferred_element_type=F32))
            for first in range(0, plan.tile, 128):
                w = table_ref[j, SPARE : SPARE + 1, start + first : start + first + 128]
                total = total + value[:, first : first + 128] * w
        wide_ref[i] = total
        return carry

    lax.fori_loop(0, share * plan.blocks, forward, 0)
    for block in range(plan.blocks):
        for j in range(share):
            row = jnp.sum(wide_ref[j * plan.blocks + block].T, axis=0, keepdims=True)
            part_ref[block % subs, block // subs, j : j + 1, :] = row * height[j : j + 1, :]

    copies = []
    for ds in range(1, subs):
        copies.append(send(part_ref.at[lax.rem(s + ds, subs)], near_ref.at[ds - 1], near_sem, (ds - 1,), at(ds=ds)))
        copies[-1].start()
    value = part_ref[s]
    for ds in range(1, subs):
        copies[ds - 1].wait()
        value = value + near_ref[ds - 1]
    final_ref[...] = value.astype(final_ref.dtype)
    copies = []
    for k, peer in enumerate(far):
        target = at(*peer)
        source = final_ref.at[target["lat"] if lats > 1 else 0]
        copies.append(send(source, latent_recv.at[g, l], latent_sem, (k,), target))
        copies[-1].start()
    latent_recv[g, l] = final_ref[l]
    loads[2].wait()
    loads[3].wait()
    loads[4].wait()
    gene_tiles = plan.genes // plan.wide

    def gene_tile(i):
        return pl.ds(pl.multiple_of(i * plan.wide, 128), plan.wide)

    def observe(i, carry):
        cols = gene_tile(i)
        seen = lax.dot_general(
            pick_ref[...], expr_ref[:, cols], (((0,), (0,)), ((), ())), preferred_element_type=F32
        )
        seen_ref[:, cols] = seen.astype(BF16)
        return carry

    lax.fori_loop(0, gene_tiles, observe, 0)
    for copy in copies:
        copy.wait()
    for lat in range(lats):
        for own in range(plan.owners):
            first = own * plan.split
            value = latent_recv[first, lat].astype(F32)
            for other in range(1, plan.split):
                value = value + latent_recv[first + other, lat].astype(F32)
            base = lat * plan.lats + own * share
            side_lat_ref[base : base + share, :] = value
    latent_ref[...] = side_lat_ref[...].astype(BF16)
    turned = side_lat_ref[...].T.astype(BF16)
    cell_ref[...] = jnp.zeros_like(cell_ref)

    def middle(i, carry):
        cols = gene_tile(i)
        mixing = mixing_ref[:, cols]
        predicted = jnp.dot(turned, mixing, preferred_element_type=F32)
        weighted = (noise_ref[:, cols] * (seen_ref[:, cols].astype(F32) - predicted)).astype(BF16)
        seen_ref[:, cols] = weighted
        cell_ref[...] += lax.dot_general(
            mixing, weighted, (((1,), (1,)), ((), ())), preferred_element_type=F32
        )
        return carry

    lax.fori_loop(0, gene_tiles, middle, 0)
    for own in range(plan.owners):
        for lat in range(lats):
            base = lat * plan.lats + own * share
            chunk_ref[own, lat] = plan.scale * cell_ref[base : base + share, :]

    copies = []
    for dg in range(1, genes):
        target = at(dg=dg)
        copies.append(
            send(chunk_ref.at[target["gene"] // plan.split], rs_ref.at[dg - 1], rs_sem, (dg - 1,), target)
        )
        copies[-1].start()

    def mix(i, carry):
        cols = gene_tile(i)
        value = plan.scale * jnp.dot(latent_ref[...], seen_ref[:, cols], preferred_element_type=F32)
        depth = mix_ref.shape[2]
        for sub in range(subs):
            for lat in range(lats):
                base = (sub * lats + lat) * depth
                mix_ref[sub, lat, :, cols] = value[base : base + depth, :]
        return carry

    lax.fori_loop(0, gene_tiles, mix, 0)
    value = chunk_ref[owner]
    for dg in range(1, genes):
        copies[dg - 1].wait()
        value = value + rs_ref[dg - 1]
    own_ref[...] = value
    copies = []
    for k, peer in enumerate(flat):
        target = at(*peer)
        source = own_ref.at[target["lat"] if lats > 1 else 0]
        copies.append(send(source, lg_ref.at[me], lg_sem, (k,), target))
        copies[-1].start()
    lg_ref[me] = own_ref[l]

    near = []
    for ds in range(1, subs):
        near.append(
            send(mix_ref.at[lax.rem(s + ds, subs)], mix_near.at[ds - 1], mix_sem, (0, ds - 1), at(ds=ds))
        )
        near[-1].start()
    scatter = [
        send(mix_two.at[lax.rem(l + dl, lats)], mix_far.at[dl - 1], mix_sem, (1, dl - 1), at(dl=dl))
        for dl in range(1, lats)
    ]
    gather = [send(mix_out.at[s, l], mix_out.at[s, l], mix_sem, (2, dl - 1), at(dl=dl)) for dl in range(1, lats)]
    back = [send(mix_out.at[s], mix_out.at[s], mix_sem, (3, ds - 1), at(ds=ds)) for ds in range(1, subs)]

    def stage_one():
        for ds in range(1, subs):
            near[ds - 1].wait()
        value = mix_ref[s]
        for ds in range(1, subs):
            value = value + mix_near[ds - 1]
        mix_two[...] = value
        for copy in scatter:
            copy.start()

    def stage_two():
        for copy in scatter:
            copy.wait()
        value = mix_two[l]
        for dl in range(1, lats):
            value = value + mix_far[dl - 1]
        mix_out[s, l] = value
        for copy in gather:
            copy.start()

    def stage_three():
        for copy in gather:
            copy.wait()
        for copy in back:
            copy.start()

    for copy in copies:
        copy.wait()
    if share < 8:
        lgpad_ref[...] = jnp.zeros_like(lgpad_ref)
    for block in range(plan.blocks):
        lgpad_ref[:share, :] = lg_ref[block] * height
        columns = lgpad_ref[...].T
        for j in range(share):
            wide_ref[j * plan.blocks + block] = jnp.broadcast_to(columns[:, j : j + 1], (rows, 128))

    stages = {0: stage_one, (3 * share) // 8: stage_two, (6 * share) // 8: stage_three}
    loose = [stage_one, stage_two, stage_three] if len(stages) < 3 else []

    def gather_copy(j, dg):
        return send(all_ref.at[g, j], all_ref.at[g, j], all_sem, (j, dg - 1), at(dg=dg))

    def backward(j, carry):
        if not loose:
            for when, stage in stages.items():
                pl.when(j == when)(stage)
        sum_ref[...] = jnp.zeros_like(sum_ref)

        def products(block, inner):
            feat = feat_ref[pl.ds(pl.multiple_of(block * rows, rows), rows), :]
            at_row = j * plan.blocks + block
            for start in range(0, plan.points, plan.tile):
                part = table_ref[j, :, start : start + plan.tile].astype(BF16)
                value = jnp.exp2(jnp.dot(feat, part, preferred_element_type=F32))
                for first in range(0, plan.tile, 128):
                    term = value[:, first : first + 128] * wide_ref[at_row]
                    sum_ref[:, start + first : start + first + 128] += jnp.sum(
                        term.reshape(rows // 8, 8, 128), axis=0
                    )
            return inner

        lax.fori_loop(0, plan.blocks, products, 0)
        for r in range(plan.points // 128):
            all_ref[g, j, r : r + 1, :] = jnp.sum(sum_ref[:, r * 128 : (r + 1) * 128], axis=0, keepdims=True)
        for dg in range(1, genes):
            gather_copy(j, dg).start()
        return carry

    lax.fori_loop(0, share, backward, 0)
    for stage in loose:
        stage()

    def finish(j, carry):
        for dg in range(1, genes):
            gather_copy(j, dg).wait()
        return carry

    lax.fori_loop(0, share, finish, 0)
    for gene in range(genes):
        base, cut = gene // plan.split * share, gene % plan.split * plan.points
        for r in range(plan.points // 128):
            first = cut + r * 128
            ind_out[base : base + share, first : first + 128] = all_ref[gene, :, r, :]
    for copy in back:
        copy.wait()


def fused(plan, *args):
    genes, lats, subs = plan.gene, plan.lat, plan.sub
    rows, share, blocks = plan.rows, plan.share, plan.blocks
    depth = plan.total // (lats * subs)
    sent = BF16 if plan.split == 1 else F32
    dma = pltpu.SemaphoreType.DMA
    far = genes * lats - 1
    flat = blocks - 1
    vmem = pl.BlockSpec(memory_space=pltpu.VMEM)
    anywhere = pl.BlockSpec(memory_space=pl.ANY)
    scratch = [
        pltpu.VMEM((plan.table, plan.genes), BF16),
        pltpu.VMEM((2, share, plan.points), F32),
        pltpu.VMEM((share, plan.points), F32),
        pltpu.VMEM((plan.total, plan.genes), BF16),
        pltpu.VMEM((1, plan.genes), F32),
        pltpu.VMEM((plan.table, rows), BF16),
        pltpu.VMEM((blocks, 2, rows), F32),
        pltpu.VMEM((128, rows), F32),
        pltpu.VMEM((blocks * rows, DEPTH), BF16),
        pltpu.VMEM((share, DEPTH, plan.points), F32),
        pltpu.VMEM((share * blocks, rows, 128), F32),
        pltpu.VMEM((subs, lats, share, rows), F32),
        pltpu.VMEM((max(1, subs - 1), lats, share, rows), F32),
        pltpu.VMEM((lats, share, rows), sent),
        pltpu.VMEM((genes, lats, share, rows), sent),
        pltpu.VMEM((plan.total, rows), BF16),
        pltpu.VMEM((plan.total, rows), F32),
        pltpu.VMEM((rows, plan.genes), BF16),
        pltpu.VMEM((plan.total, rows), F32),
        pltpu.VMEM((plan.owners, lats, share, rows), F32),
        pltpu.VMEM((max(1, genes - 1), lats, share, rows), F32),
        pltpu.VMEM((lats, share, rows), F32),
        pltpu.VMEM((blocks, share, rows), F32),
        pltpu.VMEM((max(8, share), rows), F32),
        pltpu.VMEM((subs, lats, depth, plan.genes), F32),
        pltpu.VMEM((max(1, subs - 1), lats, depth, plan.genes), F32),
        pltpu.VMEM((max(1, lats - 1), depth, plan.genes), F32),
        pltpu.VMEM((lats, depth, plan.genes), F32),
        pltpu.VMEM((8, plan.points), F32),
        pltpu.VMEM((genes, share, plan.points // 128, 128), F32),
        dma((5,)),
        dma((2, max(1, flat))),
        dma((2, max(1, subs - 1))),
        dma((2, max(1, far))),
        dma((2, max(1, genes - 1))),
        dma((2, max(1, flat))),
        dma((2, 4, max(1, subs - 1, lats - 1))),
        dma((2, share, max(1, genes - 1))),
    ]
    return pl.pallas_call(
        functools.partial(body, plan),
        in_specs=[vmem] * 4 + [anywhere] * 5,
        out_specs=[vmem, vmem],
        out_shape=[
            jax.ShapeDtypeStruct((subs, lats, depth, plan.genes), F32),
            jax.ShapeDtypeStruct((plan.lats, plan.count), F32),
        ],
        scratch_shapes=scratch,
        compiler_params=pltpu.CompilerParams(
            collective_id=0, has_side_effects=True, vmem_limit_bytes=60 * 2**20
        ),
    )(*args)


def on_device(
    cell_index,
    coords_table,
    expr_table,
    inducing,
    ind_weights,
    lengthscale,
    variance,
    mixing,
    noise_prec,
):
    genes, lats, subs = (lax.axis_size(axis) for axis in ("gene", "lat", "sub"))
    latents, count = ind_weights.shape
    owners = math.gcd(genes, latents)
    split = genes // owners
    share = latents // owners
    plan = Plan(
        gene=genes,
        lat=lats,
        sub=subs,
        rows=cell_index.shape[0],
        table=coords_table.shape[1],
        lats=latents,
        count=count,
        genes=expr_table.shape[1],
        share=share,
        split=split,
        sliced=share % 8 != 0,
        scale=-1.0 / math.sqrt(cell_index.shape[0] * lats * subs),
    )
    if plan.sliced:
        place = lax.axis_index("gene")
        first, cut = place // split * share, lax.rem(place, split) * plan.points
        inducing = lax.dynamic_slice(inducing, (0, first, cut), (2, share, plan.points))
        ind_weights = lax.dynamic_slice(ind_weights, (first, cut), (share, plan.points))
    grad_mixing, grad_inducing = fused(
        plan,
        cell_index[None, :],
        coords_table,
        lengthscale[None, :],
        variance[None, :],
        expr_table,
        inducing,
        ind_weights,
        mixing,
        noise_prec[None, :],
    )
    return grad_mixing.reshape(mixing.shape), grad_inducing


def solution(mesh):
    in_specs = (
        P(("group", "lat", "sub")),
        P("group", ("lat", "sub")),
        P(("group", "lat", "sub"), "gene"),
        P("group", "lat", "sub"),
        P(("group", "lat"), "sub"),
        P(("group", "lat")),
        P(("group", "lat")),
        P("group", "gene"),
        P(("group", "gene")),
    )
    out_specs = (P("group", "gene"), P(("group", "lat"), "sub"))
    return jax.shard_map(
        on_device, mesh=mesh, in_specs=in_specs, out_specs=out_specs, check_vma=False
    )
```

```python
import functools
import math
from typing import NamedTuple

import jax
import jax.numpy as jnp
from jax import lax
from jax.experimental import pallas as pl
from jax.experimental.pallas import tpu as pltpu
from jax.sharding import PartitionSpec as P

F32 = jnp.float32
BF16 = jnp.bfloat16
DEPTH = 24
SPARE = 21
CENTER = 0.5
LOG2E = math.log2(math.e)
LEFT = (0, 0, 1, 1, 0, 2)
RIGHT = (0, 1, 0, 1, 2, 0)


class Plan(NamedTuple):
    gene: int
    lat: int
    sub: int
    rows: int
    table: int
    lats: int
    count: int
    genes: int
    share: int
    split: int
    sliced: bool
    scale: float

    @property
    def blocks(self):
        return self.lat * self.sub

    @property
    def points(self):
        return self.count // self.split

    @property
    def owners(self):
        return self.gene // self.split

    @property
    def total(self):
        return self.lat * self.lats

    @property
    def half(self):
        return self.rows // 2

    @property
    def turned(self):
        return -(-3 * self.share // 8) * 8

    @property
    def tile(self):
        return min(256, self.points)

    @property
    def wide(self):
        return min(512, self.genes)


def pieces(value):
    high = value.astype(BF16).astype(F32)
    rest = value - high
    middle = rest.astype(BF16).astype(F32)
    low = (rest - middle).astype(BF16).astype(F32)
    return high, middle, low


def point_features(plan, scale, points_ref, weight_ref, table_ref):
    step = min(512, plan.points)

    def part(i, carry):
        cols = pl.ds(pl.multiple_of(i * step, 128), step)
        x = points_ref[0, :, cols] - CENTER
        y = points_ref[1, :, cols] - CENTER
        px = pieces(x * (2.0 * scale))
        py = pieces(y * (2.0 * scale))
        ps = pieces(jnp.broadcast_to(-scale, x.shape))
        pn = pieces((x * x + y * y) * -scale)
        rows = [px[k] for k in RIGHT] + [py[k] for k in RIGHT] + [ps[k] for k in RIGHT]
        rows += list(pn) + [weight_ref[:, cols]] + [jnp.zeros_like(x)] * (DEPTH - SPARE - 1)
        for place, row in enumerate(rows):
            for lane in range(plan.share):
                table_ref[lane, place : place + 1, cols] = row[lane : lane + 1, :]
        return carry

    lax.fori_loop(0, plan.points // step, part, 0)


def cell_features(plan, block, xy_ref, side_ref, feat_ref):
    x = xy_ref[block, 0:1, :] - CENTER
    y = xy_ref[block, 1:2, :] - CENTER
    px, py, pn = pieces(x), pieces(y), pieces(x * x + y * y)
    rows = [px[k] for k in LEFT] + [py[k] for k in LEFT] + [pn[k] for k in LEFT]
    for place, row in enumerate(rows):
        side_ref[place : place + 1, :] = row
    place = pl.ds(pl.multiple_of(block * plan.rows, plan.rows), plan.rows)
    feat_ref[place, :] = side_ref[...].T[:, :DEPTH].astype(BF16)


def body(
    plan,
    index_ref,
    coords_ref,
    length_ref,
    height_ref,
    expr_hbm,
    points_hbm,
    weight_hbm,
    mixing_hbm,
    noise_hbm,
    mix_out,
    ind_out,
    expr_ref,
    points_ref,
    weight_ref,
    mixing_ref,
    noise_ref,
    pick_ref,
    xy_ref,
    side_ref,
    feat_ref,
    table_ref,
    total_ref,
    part_ref,
    near_ref,
    final_ref,
    latent_recv,
    latent_ref,
    side_lat_ref,
    seen_ref,
    cell_ref,
    chunk_ref,
    rs_ref,
    own_ref,
    lg_ref,
    lgside_ref,
    lgt_ref,
    wide_ref,
    mix_ref,
    mix_near,
    mix_all,
    sum_ref,
    all_ref,
    load_sem,
    xy_sem,
    near_sem,
    latent_sem,
    rs_sem,
    lg_sem,
    mix_sem,
    all_sem,
):
    genes, lats, subs, blocks = plan.gene, plan.lat, plan.sub, plan.blocks
    rows, half, share = plan.rows, plan.half, plan.share
    g, l, s = lax.axis_index("gene"), lax.axis_index("lat"), lax.axis_index("sub")
    owner, slab = g // plan.split, lax.rem(g, plan.split)
    me = l * subs + s

    def at(dg=0, dl=0, ds=0):
        return {"gene": lax.rem(g + dg, genes), "lat": lax.rem(l + dl, lats), "sub": lax.rem(s + ds, subs)}

    def send(src, dst, sems, k, device):
        return pltpu.make_async_remote_copy(
            src_ref=src,
            dst_ref=dst,
            send_sem=sems.at[(0, *k)],
            recv_sem=sems.at[(1, *k)],
            device_id=device,
            device_id_type=pl.DeviceIdType.MESH,
        )

    if plan.sliced:
        points_src, weight_src = points_hbm, weight_hbm
    else:
        mine = pl.ds(pl.multiple_of(owner * share, 8), share)
        cut = pl.ds(pl.multiple_of(slab * plan.points, 128), plan.points)
        points_src, weight_src = points_hbm.at[:, mine, cut], weight_hbm.at[mine, cut]
    loads = [
        pltpu.make_async_copy(points_src, points_ref, load_sem.at[0]),
        pltpu.make_async_copy(weight_src, weight_ref, load_sem.at[1]),
        pltpu.make_async_copy(expr_hbm, expr_ref, load_sem.at[2]),
        pltpu.make_async_copy(mixing_hbm, mixing_ref, load_sem.at[3]),
        pltpu.make_async_copy(noise_hbm, noise_ref, load_sem.at[4]),
    ]
    for load in loads:
        load.start()

    far = [(dg, dl, 0) for dg in range(genes) for dl in range(lats) if dg or dl]
    flat = [(0, dl, ds) for dl in range(lats) for ds in range(subs) if dl or ds]
    peers = sorted(set(far) | set(flat))
    barrier = pltpu.get_barrier_semaphore()
    for peer in peers:
        pl.semaphore_signal(barrier, inc=1, device_id=at(*peer), device_id_type=pl.DeviceIdType.MESH)

    pick = lax.broadcasted_iota(jnp.int32, (plan.table, rows), 0) == index_ref[...]
    pick_ref[...] = pick.astype(F32).astype(BF16)
    local = jnp.zeros((2, rows), F32)
    for piece in pieces(coords_ref[...]):
        local = local + jnp.dot(piece.astype(BF16), pick_ref[...], preferred_element_type=F32)
    xy_ref[me] = local
    side_ref[...] = jnp.zeros_like(side_ref)
    side_ref[18:21, :] = jnp.ones((3, rows), F32)
    cell_features(plan, me, xy_ref, side_ref, feat_ref)

    lane = lax.broadcasted_iota(jnp.int32, (share, plan.lats), 1)
    chosen = lane == lax.broadcasted_iota(jnp.int32, (share, plan.lats), 0) + owner * share
    length = jnp.sum(jnp.where(chosen, length_ref[...], 0.0), axis=1, keepdims=True)
    height = jnp.sum(jnp.where(chosen, height_ref[...], 0.0), axis=1, keepdims=True)
    loads[0].wait()
    loads[1].wait()
    point_features(plan, (0.5 * LOG2E) / (length * length), points_ref, weight_ref, table_ref)

    def ring(k):
        return lax.rem(me + k, blocks)

    one = jnp.ones((8, 128), BF16)

    def flush(j, units):
        for u, (block, part) in enumerate(units):
            row = jnp.zeros((8, half), F32)
            for piece in pieces(total_ref[u]):
                row = row + lax.dot_general(
                    one, piece.astype(BF16), (((1,), (1,)), ((), ())), preferred_element_type=F32
                )
            part_ref[part, lax.rem(block, subs), block // subs, pl.ds(j, 1), :] = row[0:1, :]

    def forward(units, stages):
        def step(j, carry):
            for when, stage in stages:
                pl.when(j == when)(stage)
            flush(jnp.maximum(j - 1, 0), units)
            for u, (block, part) in enumerate(units):
                place = pl.multiple_of(block * rows + part * half, half)
                feat = feat_ref[pl.ds(place, half), :]
                total = jnp.zeros((half, 128), F32)
                for start in range(0, plan.points, plan.tile):
                    cols = slice(start, start + plan.tile)
                    value = jnp.exp2(
                        jnp.dot(feat, table_ref[j, :, cols].astype(BF16), preferred_element_type=F32)
                    )
                    for first in range(0, plan.tile, 128):
                        w = table_ref[j, SPARE : SPARE + 1, start + first : start + first + 128]
                        total = total + value[:, first : first + 128] * w
                total_ref[u] = total
            return carry

        total_ref[...] = jnp.zeros_like(total_ref)
        lax.fori_loop(0, share, step, 0)
        flush(share - 1, units)

    forward([(me, 0), (me, 1)], [])

    pl.semaphore_wait(barrier, len(peers))
    copies = []
    for k, peer in enumerate(flat):
        copies.append(send(xy_ref.at[me], xy_ref.at[me], xy_sem, (k,), at(*peer)))
        copies[-1].start()
    for load in loads[2:]:
        load.wait()
    gene_tiles = plan.genes // plan.wide

    def gene_tile(i):
        return pl.ds(pl.multiple_of(i * plan.wide, 128), plan.wide)

    def observe(i, carry):
        cols = gene_tile(i)
        seen = lax.dot_general(
            pick_ref[...], expr_ref[:, cols], (((0,), (0,)), ((), ())), preferred_element_type=F32
        )
        seen_ref[:, cols] = seen.astype(BF16)
        return carry

    lax.fori_loop(0, gene_tiles, observe, 0)
    for copy in copies:
        copy.wait()
    for k in range(1, blocks):
        cell_features(plan, ring(k), xy_ref, side_ref, feat_ref)

    def near_copies(part):
        return [
            send(part_ref.at[part, lax.rem(s + ds, subs)], near_ref.at[part, ds - 1], near_sem, (part, ds - 1), at(ds=ds))
            for ds in range(1, subs)
        ]

    def latent_copies(part):
        out = []
        for k, peer in enumerate(far):
            target = at(*peer)
            out.append(
                send(final_ref.at[part, target["lat"]], latent_recv.at[part, g, l], latent_sem, (part, k), target)
            )
        return out

    def rs_copies(part):
        out = []
        for dg in range(1, genes):
            target = at(dg=dg)
            source = chunk_ref.at[part, target["gene"] // plan.split]
            out.append(send(source, rs_ref.at[part, dg - 1], rs_sem, (part, dg - 1), target))
        return out

    def lg_copies(part):
        out = []
        for k, peer in enumerate(flat):
            target = at(*peer)
            out.append(send(own_ref.at[part, target["lat"]], lg_ref.at[part, me], lg_sem, (part, k), target))
        return out

    def start(copies):
        for copy in copies:
            copy.start()

    def wait(copies):
        for copy in copies:
            copy.wait()

    def sum_near(part):
        wait(near_copies(part))
        value = part_ref[part, s]
        for ds in range(1, subs):
            value = value + near_ref[part, ds - 1]
        value = value * height[None]
        final_ref[part] = value.astype(final_ref.dtype)
        start(latent_copies(part))
        latent_recv[part, g, l] = final_ref[part, l]

    def middle(part):
        wait(latent_copies(part))
        for lat in range(lats):
            for own in range(plan.owners):
                first = own * plan.split
                value = latent_recv[part, first, lat].astype(F32)
                for other in range(1, plan.split):
                    value = value + latent_recv[part, first + other, lat].astype(F32)
                base = lat * plan.lats + own * share
                side_lat_ref[base : base + share, :] = value
        cells = slice(part * half, (part + 1) * half)
        latent_ref[:, cells] = side_lat_ref[...].astype(BF16)
        turned = side_lat_ref[...].T.astype(BF16)
        cell_ref[...] = jnp.zeros_like(cell_ref)

        def tile(i, carry):
            cols = gene_tile(i)
            mixing = mixing_ref[:, cols]
            predicted = jnp.dot(turned, mixing, preferred_element_type=F32)
            weighted = (noise_ref[:, cols] * (seen_ref[cells, cols].astype(F32) - predicted)).astype(BF16)
            seen_ref[cells, cols] = weighted
            cell_ref[...] += lax.dot_general(
                mixing, weighted, (((1,), (1,)), ((), ())), preferred_element_type=F32
            )
            return carry

        lax.fori_loop(0, gene_tiles, tile, 0)
        for own in range(plan.owners):
            for lat in range(lats):
                base = lat * plan.lats + own * share
                chunk_ref[part, own, lat] = plan.scale * cell_ref[base : base + share, :]
        start(rs_copies(part))

    def sum_gene(part):
        wait(rs_copies(part))
        value = chunk_ref[part, owner]
        for dg in range(1, genes):
            value = value + rs_ref[part, dg - 1]
        own_ref[part] = value
        start(lg_copies(part))
        lg_ref[part, me] = own_ref[part, l]

    def turn(part):
        wait(lg_copies(part))
        for block in range(blocks):
            for p, piece in enumerate(pieces(lg_ref[part, block] * height)):
                lgside_ref[p * share : (p + 1) * share, :] = piece
            lgt_ref[block * half : (block + 1) * half, :] = (
                lgside_ref[...].T[:, : plan.turned].astype(BF16)
            )

    def mix_near_copies():
        return [
            send(mix_ref.at[lax.rem(s + ds, subs)], mix_near.at[ds - 1], mix_sem, (0, ds - 1, 0), at(ds=ds))
            for ds in range(1, subs)
        ]

    def mix_lat_copies(p):
        return [send(mix_all.at[l, p], mix_all.at[l, p], mix_sem, (1, dl - 1, p), at(dl=dl)) for dl in range(1, lats)]

    def mix_back_copies(p):
        return [send(mix_out.at[s, p], mix_out.at[s, p], mix_sem, (2, ds - 1, p), at(ds=ds)) for ds in range(1, subs)]

    def mix_part():
        def tile(i, carry):
            cols = gene_tile(i)
            value = plan.scale * jnp.dot(latent_ref[...], seen_ref[:, cols], preferred_element_type=F32)
            depth = mix_ref.shape[2]
            for sub in range(subs):
                for p in range(lats):
                    base = (sub * lats + p) * depth
                    mix_ref[sub, p, :, cols] = value[base : base + depth, :]
            return carry

        lax.fori_loop(0, gene_tiles, tile, 0)
        start(mix_near_copies())

    def mix_sub():
        wait(mix_near_copies())
        for p in range(lats):
            value = mix_ref[s, p]
            for ds in range(1, subs):
                value = value + mix_near[ds - 1, p]
            mix_all[l, p] = value
            start(mix_lat_copies(p))

    def mix_lat(p):
        wait(mix_lat_copies(p))
        value = mix_all[0, p]
        for lat in range(1, lats):
            value = value + mix_all[lat, p]
        mix_out[s, p] = value
        start(mix_back_copies(p))

    def gather_copies(j):
        return [
            send(all_ref.at[g, j], all_ref.at[g, j], all_sem, (j, dg - 1), at(dg=dg)) for dg in range(1, genes)
        ]

    def backward(part, stages):
        def step(j, carry):
            for when, stage in stages:
                pl.when(j == when)(stage)
            row = lax.broadcasted_iota(jnp.int32, (plan.turned, 128), 0)
            select = (lax.rem(row, share) == j).astype(F32).astype(BF16)
            for block in range(blocks):
                turned = lgt_ref[block * half : (block + 1) * half, :]
                wide_ref[block] = jnp.dot(turned, select, preferred_element_type=F32)
            for start_ in range(0, plan.points, plan.tile):
                cols = slice(start_, start_ + plan.tile)
                points = table_ref[j, :, cols].astype(BF16)
                sums = [None] * (plan.tile // 128)
                for block in range(blocks):
                    feat = feat_ref[block * rows + part * half : block * rows + (part + 1) * half, :]
                    value = jnp.exp2(jnp.dot(feat, points, preferred_element_type=F32))
                    for f in range(plan.tile // 128):
                        term = value[:, f * 128 : (f + 1) * 128] * wide_ref[block]
                        term = jnp.sum(term.reshape(half // 8, 8, 128), axis=0)
                        sums[f] = term if sums[f] is None else sums[f] + term
                for f in range(plan.tile // 128):
                    here = slice(start_ + f * 128, start_ + (f + 1) * 128)
                    if part == 0:
                        sum_ref[j, :, here] = sums[f]
                    else:
                        r = start_ // 128 + f
                        all_ref[g, j, r : r + 1, :] = jnp.sum(sum_ref[j, :, here] + sums[f], axis=0, keepdims=True)
            if part == 1:
                start(gather_copies(j))
            return carry

        lax.fori_loop(0, share, step, 0)

    def when(k):
        return k * share // 8

    forward([(ring(k), 0) for k in range(1, blocks)], [])
    start(near_copies(0))
    forward(
        [(ring(k), 1) for k in range(1, blocks)],
        [
            (when(1), lambda: sum_near(0)),
            (when(4), lambda: middle(0)),
            (when(7), lambda: sum_gene(0)),
        ],
    )
    start(near_copies(1))
    lgside_ref[...] = jnp.zeros_like(lgside_ref)
    turn(0)
    backward(
        0,
        [
            (when(1), lambda: sum_near(1)),
            (when(3), lambda: middle(1)),
            (when(3), mix_part),
            (when(6), lambda: sum_gene(1)),
            (when(6), mix_sub),
        ],
    )
    turn(1)
    early = max(1, lats // 2)

    def first_parts():
        for p in range(early):
            mix_lat(p)

    backward(1, [(when(3), first_parts)])
    for p in range(early, lats):
        mix_lat(p)

    def finish(j, carry):
        wait(gather_copies(j))
        return carry

    lax.fori_loop(0, share, finish, 0)
    for gene in range(genes):
        base, cut = gene // plan.split * share, gene % plan.split * plan.points
        for r in range(plan.points // 128):
            first = cut + r * 128
            ind_out[base : base + share, first : first + 128] = all_ref[gene, :, r, :]
    for p in range(lats):
        wait(mix_back_copies(p))


def fused(plan, *args):
    genes, lats, subs = plan.gene, plan.lat, plan.sub
    rows, half, share, blocks = plan.rows, plan.half, plan.share, plan.blocks
    depth = plan.total // (lats * subs)
    sent = BF16 if plan.split == 1 else F32
    dma = pltpu.SemaphoreType.DMA
    far = genes * lats - 1
    flat = blocks - 1
    vmem = pl.BlockSpec(memory_space=pltpu.VMEM)
    anywhere = pl.BlockSpec(memory_space=pl.ANY)
    scratch = [
        pltpu.VMEM((plan.table, plan.genes), BF16),
        pltpu.VMEM((2, share, plan.points), F32),
        pltpu.VMEM((share, plan.points), F32),
        pltpu.VMEM((plan.total, plan.genes), BF16),
        pltpu.VMEM((1, plan.genes), F32),
        pltpu.VMEM((plan.table, rows), BF16),
        pltpu.VMEM((blocks, 2, rows), F32),
        pltpu.VMEM((128, rows), F32),
        pltpu.VMEM((blocks * rows, DEPTH), BF16),
        pltpu.VMEM((share, DEPTH, plan.points), F32),
        pltpu.VMEM((max(2, blocks - 1), half, 128), F32),
        pltpu.VMEM((2, subs, lats, share, half), F32),
        pltpu.VMEM((2, max(1, subs - 1), lats, share, half), F32),
        pltpu.VMEM((2, lats, share, half), sent),
        pltpu.VMEM((2, genes, lats, share, half), sent),
        pltpu.VMEM((plan.total, rows), BF16),
        pltpu.VMEM((plan.total, half), F32),
        pltpu.VMEM((rows, plan.genes), BF16),
        pltpu.VMEM((plan.total, half), F32),
        pltpu.VMEM((2, plan.owners, lats, share, half), F32),
        pltpu.VMEM((2, max(1, genes - 1), lats, share, half), F32),
        pltpu.VMEM((2, lats, share, half), F32),
        pltpu.VMEM((2, blocks, share, half), F32),
        pltpu.VMEM((128, half), F32),
        pltpu.VMEM((blocks * half, plan.turned), BF16),
        pltpu.VMEM((blocks, half, 128), F32),
        pltpu.VMEM((subs, lats, depth, plan.genes), F32),
        pltpu.VMEM((max(1, subs - 1), lats, depth, plan.genes), F32),
        pltpu.VMEM((lats, lats, depth, plan.genes), F32),
        pltpu.VMEM((share, 8, plan.points), F32),
        pltpu.VMEM((genes, share, plan.points // 128, 128), F32),
        dma((5,)),
        dma((2, max(1, flat))),
        dma((2, 2, max(1, subs - 1))),
        dma((2, 2, max(1, far))),
        dma((2, 2, max(1, genes - 1))),
        dma((2, 2, max(1, flat))),
        dma((2, 3, max(1, subs - 1, lats - 1), lats)),
        dma((2, share, max(1, genes - 1))),
    ]
    return pl.pallas_call(
        functools.partial(body, plan),
        in_specs=[vmem] * 4 + [anywhere] * 5,
        out_specs=[vmem, vmem],
        out_shape=[
            jax.ShapeDtypeStruct((subs, lats, depth, plan.genes), F32),
            jax.ShapeDtypeStruct((plan.lats, plan.count), F32),
        ],
        scratch_shapes=scratch,
        compiler_params=pltpu.CompilerParams(
            collective_id=0, has_side_effects=True, vmem_limit_bytes=60 * 2**20
        ),
    )(*args)


def on_device(
    cell_index,
    coords_table,
    expr_table,
    inducing,
    ind_weights,
    lengthscale,
    variance,
    mixing,
    noise_prec,
):
    genes, lats, subs = (lax.axis_size(axis) for axis in ("gene", "lat", "sub"))
    latents, count = ind_weights.shape
    owners = math.gcd(genes, latents)
    split = genes // owners
    share = latents // owners
    plan = Plan(
        gene=genes,
        lat=lats,
        sub=subs,
        rows=cell_index.shape[0],
        table=coords_table.shape[1],
        lats=latents,
        count=count,
        genes=expr_table.shape[1],
        share=share,
        split=split,
        sliced=share % 8 != 0,
        scale=-1.0 / math.sqrt(cell_index.shape[0] * lats * subs),
    )
    if plan.sliced:
        place = lax.axis_index("gene")
        first, cut = place // split * share, lax.rem(place, split) * plan.points
        inducing = lax.dynamic_slice(inducing, (0, first, cut), (2, share, plan.points))
        ind_weights = lax.dynamic_slice(ind_weights, (first, cut), (share, plan.points))
    grad_mixing, grad_inducing = fused(
        plan,
        cell_index[None, :],
        coords_table,
        lengthscale[None, :],
        variance[None, :],
        expr_table,
        inducing,
        ind_weights,
        mixing,
        noise_prec[None, :],
    )
    return grad_mixing.reshape(mixing.shape), grad_inducing


def solution(mesh):
    in_specs = (
        P(("group", "lat", "sub")),
        P("group", ("lat", "sub")),
        P(("group", "lat", "sub"), "gene"),
        P("group", "lat", "sub"),
        P(("group", "lat"), "sub"),
        P(("group", "lat")),
        P(("group", "lat")),
        P("group", "gene"),
        P(("group", "gene")),
    )
    out_specs = (P("group", "gene"), P(("group", "lat"), "sub"))
    return jax.shard_map(
        on_device, mesh=mesh, in_specs=in_specs, out_specs=out_specs, check_vma=False
    )
```

```python
import functools
import math
from typing import NamedTuple

import jax
import jax.numpy as jnp
from jax import lax
from jax.experimental import pallas as pl
from jax.experimental.pallas import tpu as pltpu
from jax.sharding import PartitionSpec as P

F32 = jnp.float32
BF16 = jnp.bfloat16
DEPTH = 24
SPARE = 21
CENTER = 0.5
LOG2E = math.log2(math.e)
LEFT = (0, 0, 1, 1, 0, 2)
RIGHT = (0, 1, 0, 1, 2, 0)


class Plan(NamedTuple):
    gene: int
    lat: int
    sub: int
    rows: int
    table: int
    lats: int
    count: int
    genes: int
    share: int
    split: int
    sliced: bool
    scale: float

    @property
    def blocks(self):
        return self.lat * self.sub

    @property
    def points(self):
        return self.count // self.split

    @property
    def owners(self):
        return self.gene // self.split

    @property
    def total(self):
        return self.lat * self.lats

    @property
    def half(self):
        return self.rows // 2

    @property
    def turned(self):
        return -(-3 * self.share // 8) * 8

    @property
    def tile(self):
        return min(256, self.points)

    @property
    def wide(self):
        return min(512, self.genes)


def pieces(value):
    high = value.astype(BF16).astype(F32)
    rest = value - high
    middle = rest.astype(BF16).astype(F32)
    low = (rest - middle).astype(BF16).astype(F32)
    return high, middle, low


def point_features(plan, scale, points_ref, weight_ref, table_ref):
    step = min(512, plan.points)

    def part(i, carry):
        cols = pl.ds(pl.multiple_of(i * step, 128), step)
        x = points_ref[0, :, cols] - CENTER
        y = points_ref[1, :, cols] - CENTER
        px = pieces(x * (2.0 * scale))
        py = pieces(y * (2.0 * scale))
        ps = pieces(jnp.broadcast_to(-scale, x.shape))
        pn = pieces((x * x + y * y) * -scale)
        rows = [px[k] for k in RIGHT] + [py[k] for k in RIGHT] + [ps[k] for k in RIGHT]
        rows += list(pn) + [weight_ref[:, cols]] + [jnp.zeros_like(x)] * (DEPTH - SPARE - 1)
        for place, row in enumerate(rows):
            for lane in range(plan.share):
                table_ref[lane, place : place + 1, cols] = row[lane : lane + 1, :]
        return carry

    lax.fori_loop(0, plan.points // step, part, 0)


def cell_features(plan, block, xy_ref, side_ref, feat_ref):
    x = xy_ref[block, 0:1, :] - CENTER
    y = xy_ref[block, 1:2, :] - CENTER
    px, py, pn = pieces(x), pieces(y), pieces(x * x + y * y)
    rows = [px[k] for k in LEFT] + [py[k] for k in LEFT] + [pn[k] for k in LEFT]
    for place, row in enumerate(rows):
        side_ref[place : place + 1, :] = row
    place = pl.ds(pl.multiple_of(block * plan.rows, plan.rows), plan.rows)
    feat_ref[place, :] = side_ref[...].T[:, :DEPTH].astype(BF16)


def body(
    plan,
    index_ref,
    coords_ref,
    length_ref,
    height_ref,
    expr_hbm,
    points_hbm,
    weight_hbm,
    mixing_hbm,
    noise_hbm,
    mix_out,
    all_out,
    expr_ref,
    points_ref,
    weight_ref,
    mixing_ref,
    noise_ref,
    pick_ref,
    xy_ref,
    side_ref,
    feat_ref,
    table_ref,
    total_ref,
    part_ref,
    near_ref,
    final_ref,
    latent_recv,
    latent_ref,
    side_lat_ref,
    seen_ref,
    cell_ref,
    chunk_ref,
    rs_ref,
    own_ref,
    lg_ref,
    lgside_ref,
    lgt_ref,
    wide_ref,
    mix_ref,
    mix_near,
    mix_all,
    mix_sum,
    sum_ref,
    all_ref,
    load_sem,
    xy_sem,
    near_sem,
    latent_sem,
    rs_sem,
    lg_sem,
    mix_sem,
    all_sem,
    keep_sem,
):
    genes, lats, subs, blocks = plan.gene, plan.lat, plan.sub, plan.blocks
    rows, half, share = plan.rows, plan.half, plan.share
    g, l, s = lax.axis_index("gene"), lax.axis_index("lat"), lax.axis_index("sub")
    owner, slab = g // plan.split, lax.rem(g, plan.split)
    me = l * subs + s

    def at(dg=0, dl=0, ds=0):
        return {"gene": lax.rem(g + dg, genes), "lat": lax.rem(l + dl, lats), "sub": lax.rem(s + ds, subs)}

    def send(src, dst, sems, k, device):
        return pltpu.make_async_remote_copy(
            src_ref=src,
            dst_ref=dst,
            send_sem=sems.at[(0, *k)],
            recv_sem=sems.at[(1, *k)],
            device_id=device,
            device_id_type=pl.DeviceIdType.MESH,
        )

    if plan.sliced:
        points_src, weight_src = points_hbm, weight_hbm
    else:
        mine = pl.ds(pl.multiple_of(owner * share, 8), share)
        cut = pl.ds(pl.multiple_of(slab * plan.points, 128), plan.points)
        points_src, weight_src = points_hbm.at[:, mine, cut], weight_hbm.at[mine, cut]
    loads = [
        pltpu.make_async_copy(points_src, points_ref, load_sem.at[0]),
        pltpu.make_async_copy(weight_src, weight_ref, load_sem.at[1]),
        pltpu.make_async_copy(expr_hbm, expr_ref, load_sem.at[2]),
        pltpu.make_async_copy(mixing_hbm, mixing_ref, load_sem.at[3]),
        pltpu.make_async_copy(noise_hbm, noise_ref, load_sem.at[4]),
    ]
    for load in loads[:2]:
        load.start()

    far = [(dg, dl, 0) for dg in range(genes) for dl in range(lats) if dg or dl]
    flat = [(0, dl, ds) for dl in range(lats) for ds in range(subs) if dl or ds]
    peers = sorted(set(far) | set(flat))
    barrier = pltpu.get_barrier_semaphore()
    for peer in peers:
        pl.semaphore_signal(barrier, inc=1, device_id=at(*peer), device_id_type=pl.DeviceIdType.MESH)

    pick = lax.broadcasted_iota(jnp.int32, (plan.table, rows), 0) == index_ref[...]
    pick_ref[...] = pick.astype(F32).astype(BF16)
    local = jnp.zeros((2, rows), F32)
    for piece in pieces(coords_ref[...]):
        local = local + jnp.dot(piece.astype(BF16), pick_ref[...], preferred_element_type=F32)
    xy_ref[me] = local
    side_ref[...] = jnp.zeros_like(side_ref)
    side_ref[18:21, :] = jnp.ones((3, rows), F32)
    cell_features(plan, me, xy_ref, side_ref, feat_ref)

    lane = lax.broadcasted_iota(jnp.int32, (share, plan.lats), 1)
    chosen = lane == lax.broadcasted_iota(jnp.int32, (share, plan.lats), 0) + owner * share
    length = jnp.sum(jnp.where(chosen, length_ref[...], 0.0), axis=1, keepdims=True)
    height = jnp.sum(jnp.where(chosen, height_ref[...], 0.0), axis=1, keepdims=True)
    loads[0].wait()
    loads[1].wait()
    for load in loads[2:]:
        load.start()
    point_features(plan, (0.5 * LOG2E) / (length * length), points_ref, weight_ref, table_ref)

    def ring(k):
        return lax.rem(me + k, blocks)

    def flush(part):
        for k in range(blocks):
            for j in range(share):
                row = jnp.sum(total_ref[j, 2 * k + part].T, axis=0, keepdims=True)
                part_ref[part, lax.rem(ring(k), subs), ring(k) // subs, j : j + 1, :] = row
        start(near_copies(part))

    def forward(units, stages):
        def step(j, carry):
            for when, stage in stages:
                pl.when(j == when)(stage)
            for k, part in units:
                place = pl.multiple_of(ring(k) * rows + part * half, half)
                feat = feat_ref[pl.ds(place, half), :]
                total = jnp.zeros((half, 128), F32)
                for start in range(0, plan.points, plan.tile):
                    cols = slice(start, start + plan.tile)
                    value = jnp.exp2(
                        jnp.dot(feat, table_ref[j, :, cols].astype(BF16), preferred_element_type=F32)
                    )
                    for first in range(0, plan.tile, 128):
                        w = table_ref[j, SPARE : SPARE + 1, start + first : start + first + 128]
                        total = total + value[:, first : first + 128] * w
                total_ref[j, 2 * k + part] = total
            return carry

        lax.fori_loop(0, share, step, 0)

    forward([(0, 0), (0, 1)], [])

    pl.semaphore_wait(barrier, len(peers))
    copies = []
    for k, peer in enumerate(flat):
        copies.append(send(xy_ref.at[me], xy_ref.at[me], xy_sem, (k,), at(*peer)))
        copies[-1].start()
    for load in loads[2:]:
        load.wait()
    gene_tiles = [slice(first, first + plan.wide) for first in range(0, plan.genes, plan.wide)]
    for cols in gene_tiles:
        seen = lax.dot_general(
            pick_ref[...], expr_ref[:, cols], (((0,), (0,)), ((), ())), preferred_element_type=F32
        )
        seen_ref[:, cols] = seen.astype(BF16)
    for copy in copies:
        copy.wait()
    for k in range(1, blocks):
        cell_features(plan, ring(k), xy_ref, side_ref, feat_ref)

    def near_copies(part):
        return [
            send(part_ref.at[part, lax.rem(s + ds, subs)], near_ref.at[part, ds - 1], near_sem, (part, ds - 1), at(ds=ds))
            for ds in range(1, subs)
        ]

    def latent_copies(part):
        out = []
        for k, peer in enumerate(far):
            target = at(*peer)
            out.append(
                send(final_ref.at[part, target["lat"]], latent_recv.at[part, g, l], latent_sem, (part, k), target)
            )
        return out

    def rs_copies(part):
        out = []
        for dg in range(1, genes):
            target = at(dg=dg)
            source = chunk_ref.at[part, target["gene"] // plan.split]
            out.append(send(source, rs_ref.at[part, dg - 1], rs_sem, (part, dg - 1), target))
        return out

    def lg_copies(part):
        out = []
        for k, peer in enumerate(flat):
            target = at(*peer)
            out.append(send(own_ref.at[part, target["lat"]], lg_ref.at[part, me], lg_sem, (part, k), target))
        return out

    def start(copies):
        for copy in copies:
            copy.start()

    def wait(copies):
        for copy in copies:
            copy.wait()

    def sum_near(part):
        wait(near_copies(part))
        value = part_ref[part, s]
        for ds in range(1, subs):
            value = value + near_ref[part, ds - 1]
        value = value * height[None]
        final_ref[part] = value.astype(final_ref.dtype)
        start(latent_copies(part))
        latent_recv[part, g, l] = final_ref[part, l]

    def middle(part):
        wait(latent_copies(part))
        for lat in range(lats):
            for own in range(plan.owners):
                first = own * plan.split
                value = latent_recv[part, first, lat].astype(F32)
                for other in range(1, plan.split):
                    value = value + latent_recv[part, first + other, lat].astype(F32)
                base = lat * plan.lats + own * share
                side_lat_ref[base : base + share, :] = value
        cells = slice(part * half, (part + 1) * half)
        latent_ref[:, cells] = side_lat_ref[...].astype(BF16)
        turned = side_lat_ref[...].T.astype(BF16)
        cell = jnp.zeros((plan.total, half), F32)
        for cols in gene_tiles:
            mixing = mixing_ref[:, cols]
            predicted = jnp.dot(turned, mixing, preferred_element_type=F32)
            weighted = (noise_ref[:, cols] * (seen_ref[cells, cols].astype(F32) - predicted)).astype(BF16)
            seen_ref[cells, cols] = weighted
            cell = cell + lax.dot_general(
                mixing, weighted, (((1,), (1,)), ((), ())), preferred_element_type=F32
            )
        cell_ref[...] = cell
        for own in range(plan.owners):
            for lat in range(lats):
                base = lat * plan.lats + own * share
                chunk_ref[part, own, lat] = plan.scale * cell_ref[base : base + share, :]
        start(rs_copies(part))

    def sum_gene(part):
        wait(rs_copies(part))
        value = chunk_ref[part, owner]
        for dg in range(1, genes):
            value = value + rs_ref[part, dg - 1]
        own_ref[part] = value
        start(lg_copies(part))
        lg_ref[part, me] = own_ref[part, l]

    def turn(part):
        wait(lg_copies(part))
        for block in range(blocks):
            for p, piece in enumerate(pieces(lg_ref[part, block] * height)):
                lgside_ref[p * share : (p + 1) * share, :] = piece
            lgt_ref[block * half : (block + 1) * half, :] = (
                lgside_ref[...].T[:, : plan.turned].astype(BF16)
            )

    def mix_near_copies():
        return [
            send(mix_ref.at[lax.rem(s + ds, subs)], mix_near.at[ds - 1], mix_sem, (0, ds - 1, 0), at(ds=ds))
            for ds in range(1, subs)
        ]

    def mix_lat_copies(p):
        return [send(mix_all.at[l, p], mix_all.at[l, p], mix_sem, (1, dl - 1, p), at(dl=dl)) for dl in range(1, lats)]

    def mix_back_copies(p):
        return [send(mix_sum.at[p], mix_out.at[s, p], mix_sem, (2, ds - 1, p), at(ds=ds)) for ds in range(1, subs)]

    def mix_keep(p):
        return pltpu.make_async_copy(mix_sum.at[p], mix_out.at[s, p], keep_sem.at[p])

    def mix_part():
        depth = mix_ref.shape[2]
        for cols in gene_tiles:
            value = plan.scale * jnp.dot(latent_ref[...], seen_ref[:, cols], preferred_element_type=F32)
            for sub in range(subs):
                for p in range(lats):
                    base = (sub * lats + p) * depth
                    mix_ref[sub, p, :, cols] = value[base : base + depth, :]
        start(mix_near_copies())

    def mix_sub():
        wait(mix_near_copies())
        for p in range(lats):
            value = mix_ref[s, p]
            for ds in range(1, subs):
                value = value + mix_near[ds - 1, p]
            mix_all[l, p] = value
            start(mix_lat_copies(p))

    def mix_lat(p):
        wait(mix_lat_copies(p))
        value = mix_all[0, p]
        for lat in range(1, lats):
            value = value + mix_all[lat, p]
        mix_sum[p] = value
        start(mix_back_copies(p))
        mix_keep(p).start()

    def gather_copies(j, h):
        return [
            send(all_ref.at[j, h], all_out.at[g, j, h], all_sem, (j, h, dg - 1), at(dg=dg))
            for dg in range(1, genes)
        ] + [pltpu.make_async_copy(all_ref.at[j, h], all_out.at[g, j, h], keep_sem.at[lats + 2 * j + h])]

    def backward(part, stages):
        def step(j, carry):
            for when, stage in stages:
                pl.when(j == when)(stage)
            row = lax.broadcasted_iota(jnp.int32, (plan.turned, 128), 0)
            select = (lax.rem(row, share) == j).astype(F32).astype(BF16)
            for block in range(blocks):
                turned = lgt_ref[block * half : (block + 1) * half, :]
                wide_ref[block] = jnp.dot(turned, select, preferred_element_type=F32)
            for start_ in range(0, plan.points, plan.tile):
                cols = slice(start_, start_ + plan.tile)
                points = table_ref[j, :, cols].astype(BF16)
                sums = [None] * (plan.tile // 128)
                for block in range(blocks):
                    feat = feat_ref[block * rows + part * half : block * rows + (part + 1) * half, :]
                    value = jnp.exp2(jnp.dot(feat, points, preferred_element_type=F32))
                    for f in range(plan.tile // 128):
                        term = value[:, f * 128 : (f + 1) * 128] * wide_ref[block]
                        term = jnp.sum(term.reshape(half // 8, 8, 128), axis=0)
                        sums[f] = term if sums[f] is None else sums[f] + term
                for f in range(plan.tile // 128):
                    here = slice(start_ + f * 128, start_ + (f + 1) * 128)
                    if part == 0:
                        sum_ref[j, :, here] = sums[f]
                    else:
                        h, r = divmod(start_ // 128 + f, plan.points // 256)
                        all_ref[j, h, r : r + 1, :] = jnp.sum(sum_ref[j, :, here] + sums[f], axis=0, keepdims=True)
                if part == 1 and start_ + plan.tile == plan.points // 2:
                    start(gather_copies(j, 0))
            if part == 1:
                if plan.tile > plan.points // 2:
                    start(gather_copies(j, 0))
                start(gather_copies(j, 1))
            return carry

        lax.fori_loop(0, share, step, 0)

    def when(k):
        return k * share // 8

    forward([(k, 0) for k in range(1, blocks)], [])
    flush(0)
    forward(
        [(k, 1) for k in range(1, blocks)],
        [
            (when(1), lambda: sum_near(0)),
            (when(5), lambda: middle(0)),
            (when(7), lambda: sum_gene(0)),
        ],
    )
    flush(1)
    lgside_ref[...] = jnp.zeros_like(lgside_ref)
    turn(0)
    backward(
        0,
        [
            (when(1), lambda: sum_near(1)),
            (when(3), lambda: middle(1)),
            (when(3), mix_part),
            (when(6), lambda: sum_gene(1)),
            (when(6), mix_sub),
        ],
    )
    turn(1)
    early = max(1, lats // 2)

    def first_parts():
        for p in range(early):
            mix_lat(p)

    backward(1, [(when(5), first_parts)])
    for p in range(early, lats):
        mix_lat(p)

    def finish(j, carry):
        wait(gather_copies(j, 0))
        wait(gather_copies(j, 1))
        return carry

    lax.fori_loop(0, share, finish, 0)
    for p in range(lats):
        wait(mix_back_copies(p))
        mix_keep(p).wait()


def lay_body(plan, mix_hbm, all_hbm, mix_out, ind_out, mix_ref, all_ref, ind_ref, in_sem, out_sem):
    subs, lats, depth, _ = mix_hbm.shape
    parts = [(sub, p) for sub in range(subs) for p in range(lats)]
    mixes = [
        pltpu.make_async_copy(mix_hbm.at[sub, p], mix_ref.at[i], in_sem.at[i]) for i, (sub, p) in enumerate(parts)
    ]
    outs = [
        pltpu.make_async_copy(mix_ref.at[i], mix_out.at[pl.ds(i * depth, depth)], out_sem.at[i])
        for i in range(len(parts))
    ]
    whole = pltpu.make_async_copy(all_hbm, all_ref, in_sem.at[len(parts)])
    whole.start()
    for copy in mixes:
        copy.start()
    whole.wait()
    last = []
    half = plan.points // 256
    for owner in range(plan.owners):
        base = owner * plan.share
        for slab in range(plan.split):
            for r in range(plan.points // 128):
                first = slab * plan.points + r * 128
                h, row = divmod(r, half)
                piece = all_ref[owner * plan.split + slab, :, h, row, :]
                ind_ref[base : base + plan.share, first : first + 128] = piece
        if plan.share % 8 == 0:
            rows = pl.ds(base, plan.share)
            last.append(pltpu.make_async_copy(ind_ref.at[rows], ind_out.at[rows], out_sem.at[len(parts) + owner]))
            last[-1].start()
    if plan.share % 8:
        last.append(pltpu.make_async_copy(ind_ref, ind_out, out_sem.at[len(parts)]))
        last[-1].start()
    for copy, out in zip(mixes, outs):
        copy.wait()
        out.start()
    for copy in outs + last:
        copy.wait()


def lay(plan, mix, all_):
    subs, lats, depth, genes = mix.shape
    parts = subs * lats
    anywhere = pl.BlockSpec(memory_space=pl.ANY)
    return pl.pallas_call(
        functools.partial(lay_body, plan),
        in_specs=[anywhere] * 2,
        out_specs=[anywhere] * 2,
        out_shape=[
            jax.ShapeDtypeStruct((plan.total, genes), F32),
            jax.ShapeDtypeStruct((plan.lats, plan.count), F32),
        ],
        scratch_shapes=[
            pltpu.VMEM((parts, depth, genes), F32),
            pltpu.VMEM(all_.shape, F32),
            pltpu.VMEM((plan.lats, plan.count), F32),
            pltpu.SemaphoreType.DMA((parts + 1,)),
            pltpu.SemaphoreType.DMA((parts + plan.owners,)),
        ],
        compiler_params=pltpu.CompilerParams(vmem_limit_bytes=16 * 2**20),
    )(mix, all_)


def fused(plan, *args):
    genes, lats, subs = plan.gene, plan.lat, plan.sub
    rows, half, share, blocks = plan.rows, plan.half, plan.share, plan.blocks
    depth = plan.total // (lats * subs)
    sent = BF16 if plan.split == 1 else F32
    dma = pltpu.SemaphoreType.DMA
    far = genes * lats - 1
    flat = blocks - 1
    vmem = pl.BlockSpec(memory_space=pltpu.VMEM)
    anywhere = pl.BlockSpec(memory_space=pl.ANY)
    scratch = [
        pltpu.VMEM((plan.table, plan.genes), BF16),
        pltpu.VMEM((2, share, plan.points), F32),
        pltpu.VMEM((share, plan.points), F32),
        pltpu.VMEM((plan.total, plan.genes), BF16),
        pltpu.VMEM((1, plan.genes), F32),
        pltpu.VMEM((plan.table, rows), BF16),
        pltpu.VMEM((blocks, 2, rows), F32),
        pltpu.VMEM((128, rows), F32),
        pltpu.VMEM((blocks * rows, DEPTH), BF16),
        pltpu.VMEM((share, DEPTH, plan.points), F32),
        pltpu.VMEM((share, 2 * blocks, half, 128), F32),
        pltpu.VMEM((2, subs, lats, share, half), F32),
        pltpu.VMEM((2, max(1, subs - 1), lats, share, half), F32),
        pltpu.VMEM((2, lats, share, half), sent),
        pltpu.VMEM((2, genes, lats, share, half), sent),
        pltpu.VMEM((plan.total, rows), BF16),
        pltpu.VMEM((plan.total, half), F32),
        pltpu.VMEM((rows, plan.genes), BF16),
        pltpu.VMEM((plan.total, half), F32),
        pltpu.VMEM((2, plan.owners, lats, share, half), F32),
        pltpu.VMEM((2, max(1, genes - 1), lats, share, half), F32),
        pltpu.VMEM((2, lats, share, half), F32),
        pltpu.VMEM((2, blocks, share, half), F32),
        pltpu.VMEM((128, half), F32),
        pltpu.VMEM((blocks * half, plan.turned), BF16),
        pltpu.VMEM((blocks, half, 128), F32),
        pltpu.VMEM((subs, lats, depth, plan.genes), F32),
        pltpu.VMEM((max(1, subs - 1), lats, depth, plan.genes), F32),
        pltpu.VMEM((lats, lats, depth, plan.genes), F32),
        pltpu.VMEM((lats, depth, plan.genes), F32),
        pltpu.VMEM((share, 8, plan.points), F32),
        pltpu.VMEM((share, 2, plan.points // 256, 128), F32),
        dma((5,)),
        dma((2, max(1, flat))),
        dma((2, 2, max(1, subs - 1))),
        dma((2, 2, max(1, far))),
        dma((2, 2, max(1, genes - 1))),
        dma((2, 2, max(1, flat))),
        dma((2, 3, max(1, subs - 1, lats - 1), lats)),
        dma((2, share, 2, max(1, genes - 1))),
        dma((lats + 2 * share,)),
    ]
    return pl.pallas_call(
        functools.partial(body, plan),
        in_specs=[vmem] * 4 + [anywhere] * 5,
        out_specs=[anywhere, anywhere],
        out_shape=[
            jax.ShapeDtypeStruct((subs, lats, depth, plan.genes), F32),
            jax.ShapeDtypeStruct((genes, share, 2, plan.points // 256, 128), F32),
        ],
        scratch_shapes=scratch,
        compiler_params=pltpu.CompilerParams(
            collective_id=0, has_side_effects=True, vmem_limit_bytes=60 * 2**20
        ),
    )(*args)


def on_device(
    cell_index,
    coords_table,
    expr_table,
    inducing,
    ind_weights,
    lengthscale,
    variance,
    mixing,
    noise_prec,
):
    genes, lats, subs = (lax.axis_size(axis) for axis in ("gene", "lat", "sub"))
    latents, count = ind_weights.shape
    owners = math.gcd(genes, latents)
    split = genes // owners
    share = latents // owners
    plan = Plan(
        gene=genes,
        lat=lats,
        sub=subs,
        rows=cell_index.shape[0],
        table=coords_table.shape[1],
        lats=latents,
        count=count,
        genes=expr_table.shape[1],
        share=share,
        split=split,
        sliced=share % 8 != 0,
        scale=-1.0 / math.sqrt(cell_index.shape[0] * lats * subs),
    )
    if plan.sliced:
        place = lax.axis_index("gene")
        first, cut = place // split * share, lax.rem(place, split) * plan.points
        inducing = lax.dynamic_slice(inducing, (0, first, cut), (2, share, plan.points))
        ind_weights = lax.dynamic_slice(ind_weights, (first, cut), (share, plan.points))
    mix, gathered = fused(
        plan,
        cell_index[None, :],
        coords_table,
        lengthscale[None, :],
        variance[None, :],
        expr_table,
        inducing,
        ind_weights,
        mixing,
        noise_prec[None, :],
    )
    return lay(plan, mix, gathered)


def solution(mesh):
    in_specs = (
        P(("group", "lat", "sub")),
        P("group", ("lat", "sub")),
        P(("group", "lat", "sub"), "gene"),
        P("group", "lat", "sub"),
        P(("group", "lat"), "sub"),
        P(("group", "lat")),
        P(("group", "lat")),
        P("group", "gene"),
        P(("group", "gene")),
    )
    out_specs = (P("group", "gene"), P(("group", "lat"), "sub"))
    return jax.shard_map(
        on_device, mesh=mesh, in_specs=in_specs, out_specs=out_specs, check_vma=False
    )
```

```python
import functools
import math
from typing import NamedTuple

import jax
import jax.numpy as jnp
from jax import lax
from jax.experimental import pallas as pl
from jax.experimental.pallas import tpu as pltpu
from jax.sharding import PartitionSpec as P

F32 = jnp.float32
BF16 = jnp.bfloat16
DEPTH = 24
SPARE = 21
CENTER = 0.5
LOG2E = math.log2(math.e)
LEFT = (0, 0, 1, 1, 0, 2)
RIGHT = (0, 1, 0, 1, 2, 0)


class Plan(NamedTuple):
    gene: int
    lat: int
    sub: int
    rows: int
    table: int
    lats: int
    count: int
    genes: int
    share: int
    split: int
    sliced: bool
    scale: float

    @property
    def blocks(self):
        return self.lat * self.sub

    @property
    def points(self):
        return self.count // self.split

    @property
    def owners(self):
        return self.gene // self.split

    @property
    def total(self):
        return self.lat * self.lats

    @property
    def half(self):
        return self.rows // 2

    @property
    def turned(self):
        return -(-3 * self.share // 8) * 8

    @property
    def tile(self):
        return min(256, self.points)

    @property
    def wide(self):
        return min(512, self.genes)


CODES = 32767.0
TINY = 1e-30


def code(value, top):
    return jnp.floor(value * (CODES / top) + 0.5).astype(jnp.int32).astype(jnp.int16)


def decode(codes, top):
    return codes.astype(jnp.int32).astype(F32) * (top * (1.0 / CODES))


def pieces(value):
    high = value.astype(BF16).astype(F32)
    rest = value - high
    middle = rest.astype(BF16).astype(F32)
    low = (rest - middle).astype(BF16).astype(F32)
    return high, middle, low


def point_features(plan, scale, points_ref, weight_ref, table_ref):
    step = min(512, plan.points)

    def part(i, carry):
        cols = pl.ds(pl.multiple_of(i * step, 128), step)
        x = points_ref[0, :, cols] - CENTER
        y = points_ref[1, :, cols] - CENTER
        px = pieces(x * (2.0 * scale))
        py = pieces(y * (2.0 * scale))
        ps = pieces(jnp.broadcast_to(-scale, x.shape))
        pn = pieces((x * x + y * y) * -scale)
        rows = [px[k] for k in RIGHT] + [py[k] for k in RIGHT] + [ps[k] for k in RIGHT]
        rows += list(pn) + [weight_ref[:, cols]] + [jnp.zeros_like(x)] * (DEPTH - SPARE - 1)
        for place, row in enumerate(rows):
            for lane in range(plan.share):
                table_ref[lane, place : place + 1, cols] = row[lane : lane + 1, :]
        return carry

    lax.fori_loop(0, plan.points // step, part, 0)


def cell_features(plan, block, xy_ref, side_ref, feat_ref):
    x = xy_ref[block, 0:1, :] - CENTER
    y = xy_ref[block, 1:2, :] - CENTER
    px, py, pn = pieces(x), pieces(y), pieces(x * x + y * y)
    rows = [px[k] for k in LEFT] + [py[k] for k in LEFT] + [pn[k] for k in LEFT]
    for place, row in enumerate(rows):
        side_ref[place : place + 1, :] = row
    place = pl.ds(pl.multiple_of(block * plan.rows, plan.rows), plan.rows)
    feat_ref[place, :] = side_ref[...].T[:, :DEPTH].astype(BF16)


def body(
    plan,
    index_ref,
    coords_ref,
    length_ref,
    height_ref,
    expr_hbm,
    points_hbm,
    weight_hbm,
    mixing_hbm,
    noise_hbm,
    mix_out,
    all_out,
    top_out,
    expr_ref,
    points_ref,
    weight_ref,
    mixing_ref,
    noise_ref,
    pick_ref,
    xy_ref,
    side_ref,
    feat_ref,
    table_ref,
    total_ref,
    part_ref,
    near_ref,
    final_ref,
    latent_recv,
    latent_ref,
    side_lat_ref,
    seen_ref,
    cell_ref,
    chunk_ref,
    rs_ref,
    own_ref,
    lg_ref,
    lgside_ref,
    lgt_ref,
    wide_ref,
    mix_ref,
    mix_near,
    mix_all,
    mix_sum,
    sum_ref,
    row_ref,
    all_ref,
    top_ref,
    load_sem,
    xy_sem,
    near_sem,
    latent_sem,
    rs_sem,
    lg_sem,
    mix_sem,
    all_sem,
    all_keep,
    keep_sem,
):
    genes, lats, subs, blocks = plan.gene, plan.lat, plan.sub, plan.blocks
    rows, half, share = plan.rows, plan.half, plan.share
    g, l, s = lax.axis_index("gene"), lax.axis_index("lat"), lax.axis_index("sub")
    owner, slab = g // plan.split, lax.rem(g, plan.split)
    me = l * subs + s

    def at(dg=0, dl=0, ds=0):
        return {"gene": lax.rem(g + dg, genes), "lat": lax.rem(l + dl, lats), "sub": lax.rem(s + ds, subs)}

    def send(src, dst, sems, k, device):
        return pltpu.make_async_remote_copy(
            src_ref=src,
            dst_ref=dst,
            send_sem=sems.at[(0, *k)],
            recv_sem=sems.at[(1, *k)],
            device_id=device,
            device_id_type=pl.DeviceIdType.MESH,
        )

    if plan.sliced:
        points_src, weight_src = points_hbm, weight_hbm
    else:
        mine = pl.ds(pl.multiple_of(owner * share, 8), share)
        cut = pl.ds(pl.multiple_of(slab * plan.points, 128), plan.points)
        points_src, weight_src = points_hbm.at[:, mine, cut], weight_hbm.at[mine, cut]
    loads = [
        pltpu.make_async_copy(points_src, points_ref, load_sem.at[0]),
        pltpu.make_async_copy(weight_src, weight_ref, load_sem.at[1]),
        pltpu.make_async_copy(expr_hbm, expr_ref, load_sem.at[2]),
        pltpu.make_async_copy(mixing_hbm, mixing_ref, load_sem.at[3]),
        pltpu.make_async_copy(noise_hbm, noise_ref, load_sem.at[4]),
    ]
    for load in loads[:2]:
        load.start()

    far = [(dg, dl, 0) for dg in range(genes) for dl in range(lats) if dg or dl]
    flat = [(0, dl, ds) for dl in range(lats) for ds in range(subs) if dl or ds]
    peers = sorted(set(far) | set(flat))
    barrier = pltpu.get_barrier_semaphore()
    for peer in peers:
        pl.semaphore_signal(barrier, inc=1, device_id=at(*peer), device_id_type=pl.DeviceIdType.MESH)

    pick = lax.broadcasted_iota(jnp.int32, (plan.table, rows), 0) == index_ref[...]
    pick_ref[...] = pick.astype(F32).astype(BF16)
    local = jnp.zeros((2, rows), F32)
    for piece in pieces(coords_ref[...]):
        local = local + jnp.dot(piece.astype(BF16), pick_ref[...], preferred_element_type=F32)
    xy_ref[me] = local
    side_ref[...] = jnp.zeros_like(side_ref)
    side_ref[18:21, :] = jnp.ones((3, rows), F32)
    cell_features(plan, me, xy_ref, side_ref, feat_ref)

    lane = lax.broadcasted_iota(jnp.int32, (share, plan.lats), 1)
    chosen = lane == lax.broadcasted_iota(jnp.int32, (share, plan.lats), 0) + owner * share
    length = jnp.sum(jnp.where(chosen, length_ref[...], 0.0), axis=1, keepdims=True)
    height = jnp.sum(jnp.where(chosen, height_ref[...], 0.0), axis=1, keepdims=True)
    loads[0].wait()
    loads[1].wait()
    for load in loads[2:]:
        load.start()
    point_features(plan, (0.5 * LOG2E) / (length * length), points_ref, weight_ref, table_ref)

    def ring(k):
        return lax.rem(me + k, blocks)

    def flush(part):
        for k in range(blocks):
            for j in range(share):
                row = jnp.sum(total_ref[j, 2 * k + part].T, axis=0, keepdims=True)
                part_ref[part, lax.rem(ring(k), subs), ring(k) // subs, j : j + 1, :] = row
        start(near_copies(part))

    def forward(units, stages):
        def step(j, carry):
            for when, stage in stages:
                pl.when(j == when)(stage)
            for k, part in units:
                place = pl.multiple_of(ring(k) * rows + part * half, half)
                feat = feat_ref[pl.ds(place, half), :]
                total = jnp.zeros((half, 128), F32)
                for start in range(0, plan.points, plan.tile):
                    cols = slice(start, start + plan.tile)
                    value = jnp.exp2(
                        jnp.dot(feat, table_ref[j, :, cols].astype(BF16), preferred_element_type=F32)
                    )
                    for first in range(0, plan.tile, 128):
                        w = table_ref[j, SPARE : SPARE + 1, start + first : start + first + 128]
                        total = total + value[:, first : first + 128] * w
                total_ref[j, 2 * k + part] = total
            return carry

        lax.fori_loop(0, share, step, 0)

    forward([(0, 0)], [])

    pl.semaphore_wait(barrier, len(peers))
    copies = []
    for k, peer in enumerate(flat):
        copies.append(send(xy_ref.at[me], xy_ref.at[me], xy_sem, (k,), at(*peer)))
        copies[-1].start()
    forward([(0, 1)], [])
    for load in loads[2:]:
        load.wait()
    gene_tiles = [slice(first, first + plan.wide) for first in range(0, plan.genes, plan.wide)]
    for cols in gene_tiles:
        seen = lax.dot_general(
            pick_ref[...], expr_ref[:, cols], (((0,), (0,)), ((), ())), preferred_element_type=F32
        )
        seen_ref[:, cols] = seen.astype(BF16)
    for copy in copies:
        copy.wait()
    for k in range(1, blocks):
        cell_features(plan, ring(k), xy_ref, side_ref, feat_ref)

    def near_copies(part):
        return [
            send(part_ref.at[part, lax.rem(s + ds, subs)], near_ref.at[part, ds - 1], near_sem, (part, ds - 1), at(ds=ds))
            for ds in range(1, subs)
        ]

    def latent_copies(part):
        out = []
        for k, peer in enumerate(far):
            target = at(*peer)
            out.append(
                send(final_ref.at[part, target["lat"]], latent_recv.at[part, g, l], latent_sem, (part, k), target)
            )
        return out

    def rs_copies(part):
        out = []
        for dg in range(1, genes):
            target = at(dg=dg)
            source = chunk_ref.at[part, target["gene"] // plan.split]
            out.append(send(source, rs_ref.at[part, dg - 1], rs_sem, (part, dg - 1), target))
        return out

    def lg_copies(part):
        out = []
        for k, peer in enumerate(flat):
            target = at(*peer)
            out.append(send(own_ref.at[part, target["lat"]], lg_ref.at[part, me], lg_sem, (part, k), target))
        return out

    def start(copies):
        for copy in copies:
            copy.start()

    def wait(copies):
        for copy in copies:
            copy.wait()

    def sum_near(part):
        wait(near_copies(part))
        value = part_ref[part, s]
        for ds in range(1, subs):
            value = value + near_ref[part, ds - 1]
        value = value * height[None]
        final_ref[part] = value.astype(final_ref.dtype)
        start(latent_copies(part))
        latent_recv[part, g, l] = final_ref[part, l]

    def middle(part):
        wait(latent_copies(part))
        for lat in range(lats):
            for own in range(plan.owners):
                first = own * plan.split
                value = latent_recv[part, first, lat].astype(F32)
                for other in range(1, plan.split):
                    value = value + latent_recv[part, first + other, lat].astype(F32)
                base = lat * plan.lats + own * share
                side_lat_ref[base : base + share, :] = value
        cells = slice(part * half, (part + 1) * half)
        latent_ref[:, cells] = side_lat_ref[...].astype(BF16)
        turned = side_lat_ref[...].T.astype(BF16)
        cell = jnp.zeros((plan.total, half), F32)
        for cols in gene_tiles:
            mixing = mixing_ref[:, cols]
            predicted = jnp.dot(turned, mixing, preferred_element_type=F32)
            weighted = (noise_ref[:, cols] * (seen_ref[cells, cols].astype(F32) - predicted)).astype(BF16)
            seen_ref[cells, cols] = weighted
            cell = cell + lax.dot_general(
                mixing, weighted, (((1,), (1,)), ((), ())), preferred_element_type=F32
            )
        cell_ref[...] = cell
        for own in range(plan.owners):
            for lat in range(lats):
                base = lat * plan.lats + own * share
                chunk_ref[part, own, lat] = plan.scale * cell_ref[base : base + share, :]
        start(rs_copies(part))

    def sum_gene(part):
        wait(rs_copies(part))
        value = chunk_ref[part, owner]
        for dg in range(1, genes):
            value = value + rs_ref[part, dg - 1]
        own_ref[part] = value
        start(lg_copies(part))
        lg_ref[part, me] = own_ref[part, l]

    def turn(part):
        wait(lg_copies(part))
        for block in range(blocks):
            for p, piece in enumerate(pieces(lg_ref[part, block] * height)):
                lgside_ref[p * share : (p + 1) * share, :] = piece
            lgt_ref[block * half : (block + 1) * half, :] = (
                lgside_ref[...].T[:, : plan.turned].astype(BF16)
            )

    def mix_near_copies():
        return [
            send(mix_ref.at[lax.rem(s + ds, subs)], mix_near.at[ds - 1], mix_sem, (0, ds - 1, 0), at(ds=ds))
            for ds in range(1, subs)
        ]

    def mix_lat_copies(p):
        return [send(mix_all.at[l, p], mix_all.at[l, p], mix_sem, (1, dl - 1, p), at(dl=dl)) for dl in range(1, lats)]

    def mix_back_copies(p):
        return [send(mix_sum.at[p], mix_out.at[s, p], mix_sem, (2, ds - 1, p), at(ds=ds)) for ds in range(1, subs)]

    def mix_keep(p):
        return pltpu.make_async_copy(mix_sum.at[p], mix_out.at[s, p], keep_sem.at[p])

    def mix_part():
        depth = mix_ref.shape[2]
        for cols in gene_tiles:
            value = plan.scale * jnp.dot(latent_ref[...], seen_ref[:, cols], preferred_element_type=F32)
            for sub in range(subs):
                for p in range(lats):
                    base = (sub * lats + p) * depth
                    mix_ref[sub, p, :, cols] = value[base : base + depth, :]
        start(mix_near_copies())

    def mix_sub():
        wait(mix_near_copies())
        for p in range(lats):
            value = mix_ref[s, p]
            for ds in range(1, subs):
                value = value + mix_near[ds - 1, p]
            mix_all[l, p] = value
            start(mix_lat_copies(p))

    def mix_lat(p):
        wait(mix_lat_copies(p))
        value = mix_all[0, p]
        for lat in range(1, lats):
            value = value + mix_all[lat, p]
        mix_sum[p] = value
        start(mix_back_copies(p))
        mix_keep(p).start()

    def gather_copies(j, h):
        out = []
        for i, (src, dst) in enumerate(((all_ref, all_out), (top_ref, top_out))):
            for dg in range(1, genes):
                out.append(send(src.at[j, h], dst.at[g, j, h], all_sem, (i, j, h, dg - 1), at(dg=dg)))
            out.append(pltpu.make_async_copy(src.at[j, h], dst.at[g, j, h], all_keep.at[i, j, h]))
        return out

    def gather(j, h):
        value = row_ref[h]
        top = jnp.maximum(jnp.max(jnp.abs(value), axis=0, keepdims=True), TINY)
        top_ref[j, h] = top
        all_ref[j, h] = code(value, top)
        start(gather_copies(j, h))

    def backward(part, stages):
        def step(j, carry):
            for when, stage in stages:
                pl.when(j == when)(stage)
            row = lax.broadcasted_iota(jnp.int32, (plan.turned, 128), 0)
            select = (lax.rem(row, share) == j).astype(F32).astype(BF16)
            for block in range(blocks):
                turned = lgt_ref[block * half : (block + 1) * half, :]
                wide_ref[block] = jnp.dot(turned, select, preferred_element_type=F32)
            for start_ in range(0, plan.points, plan.tile):
                cols = slice(start_, start_ + plan.tile)
                points = table_ref[j, :, cols].astype(BF16)
                sums = [None] * (plan.tile // 128)
                for block in range(blocks):
                    feat = feat_ref[block * rows + part * half : block * rows + (part + 1) * half, :]
                    value = jnp.exp2(jnp.dot(feat, points, preferred_element_type=F32))
                    for f in range(plan.tile // 128):
                        term = value[:, f * 128 : (f + 1) * 128] * wide_ref[block]
                        term = jnp.sum(term.reshape(half // 8, 8, 128), axis=0)
                        sums[f] = term if sums[f] is None else sums[f] + term
                for f in range(plan.tile // 128):
                    here = slice(start_ + f * 128, start_ + (f + 1) * 128)
                    if part == 0:
                        sum_ref[j, :, here] = sums[f]
                    else:
                        h, r = divmod(start_ // 128 + f, plan.points // 256)
                        row_ref[h, r : r + 1, :] = jnp.sum(sum_ref[j, :, here] + sums[f], axis=0, keepdims=True)
                if part == 1 and start_ + plan.tile == plan.points // 2:
                    gather(j, 0)
            if part == 1:
                if plan.tile > plan.points // 2:
                    gather(j, 0)
                gather(j, 1)
            return carry

        lax.fori_loop(0, share, step, 0)

    def when(k):
        return k * share // 8

    forward([(k, 0) for k in range(1, blocks)], [])
    flush(0)
    forward(
        [(k, 1) for k in range(1, blocks)],
        [
            (when(1), lambda: sum_near(0)),
            (when(5), lambda: middle(0)),
            (when(7), lambda: sum_gene(0)),
        ],
    )
    flush(1)
    lgside_ref[...] = jnp.zeros_like(lgside_ref)
    turn(0)
    backward(
        0,
        [
            (when(1), lambda: sum_near(1)),
            (when(4), lambda: middle(1)),
            (when(4), mix_part),
            (when(6), lambda: sum_gene(1)),
            (when(6), mix_sub),
        ],
    )
    turn(1)
    early = max(1, lats // 2)

    def first_parts():
        for p in range(early):
            mix_lat(p)

    backward(1, [(when(5), first_parts)])
    for p in range(early, lats):
        mix_lat(p)

    def finish(j, carry):
        wait(gather_copies(j, 0))
        wait(gather_copies(j, 1))
        return carry

    lax.fori_loop(0, share, finish, 0)
    for p in range(lats):
        wait(mix_back_copies(p))
        mix_keep(p).wait()


def lay_body(plan, mix_hbm, all_hbm, top_hbm, mix_out, ind_out, mix_ref, all_ref, top_ref, row_ref, ind_ref, in_sem, out_sem):
    subs, lats, depth, _ = mix_hbm.shape
    parts = [(sub, p) for sub in range(subs) for p in range(lats)]
    mixes = [
        pltpu.make_async_copy(mix_hbm.at[sub, p], mix_ref.at[i], in_sem.at[i]) for i, (sub, p) in enumerate(parts)
    ]
    outs = [
        pltpu.make_async_copy(mix_ref.at[i], mix_out.at[pl.ds(i * depth, depth)], out_sem.at[i])
        for i in range(len(parts))
    ]
    wholes = [
        pltpu.make_async_copy(all_hbm, all_ref, in_sem.at[len(parts)]),
        pltpu.make_async_copy(top_hbm, top_ref, in_sem.at[len(parts) + 1]),
    ]
    for copy in wholes + mixes:
        copy.start()
    for copy in wholes:
        copy.wait()
    last = []
    half = plan.points // 256
    for owner in range(plan.owners):
        base = owner * plan.share
        for slab in range(plan.split):
            gene = owner * plan.split + slab
            for j in range(plan.share):
                for h in range(2):
                    row_ref[gene, j, h * half : (h + 1) * half, :] = decode(all_ref[gene, j, h], top_ref[gene, j, h])
            for r in range(plan.points // 128):
                first = slab * plan.points + r * 128
                ind_ref[base : base + plan.share, first : first + 128] = row_ref[gene, :, r, :]
        if plan.share % 8 == 0:
            rows = pl.ds(base, plan.share)
            last.append(pltpu.make_async_copy(ind_ref.at[rows], ind_out.at[rows], out_sem.at[len(parts) + owner]))
            last[-1].start()
    if plan.share % 8:
        last.append(pltpu.make_async_copy(ind_ref, ind_out, out_sem.at[len(parts)]))
        last[-1].start()
    for copy, out in zip(mixes, outs):
        copy.wait()
        out.start()
    for copy in outs + last:
        copy.wait()


def lay(plan, mix, codes, tops):
    subs, lats, depth, genes = mix.shape
    parts = subs * lats
    anywhere = pl.BlockSpec(memory_space=pl.ANY)
    return pl.pallas_call(
        functools.partial(lay_body, plan),
        in_specs=[anywhere] * 3,
        out_specs=[anywhere] * 2,
        out_shape=[
            jax.ShapeDtypeStruct((plan.total, genes), F32),
            jax.ShapeDtypeStruct((plan.lats, plan.count), F32),
        ],
        scratch_shapes=[
            pltpu.VMEM((parts, depth, genes), F32),
            pltpu.VMEM(codes.shape, jnp.int16),
            pltpu.VMEM(tops.shape, F32),
            pltpu.VMEM((plan.gene, plan.share, plan.points // 128, 128), F32),
            pltpu.VMEM((plan.lats, plan.count), F32),
            pltpu.SemaphoreType.DMA((parts + 2,)),
            pltpu.SemaphoreType.DMA((parts + plan.owners,)),
        ],
        compiler_params=pltpu.CompilerParams(vmem_limit_bytes=60 * 2**20),
    )(mix, codes, tops)


def fused(plan, *args):
    genes, lats, subs = plan.gene, plan.lat, plan.sub
    rows, half, share, blocks = plan.rows, plan.half, plan.share, plan.blocks
    depth = plan.total // (lats * subs)
    sent = BF16 if plan.split == 1 else F32
    dma = pltpu.SemaphoreType.DMA
    far = genes * lats - 1
    flat = blocks - 1
    vmem = pl.BlockSpec(memory_space=pltpu.VMEM)
    anywhere = pl.BlockSpec(memory_space=pl.ANY)
    scratch = [
        pltpu.VMEM((plan.table, plan.genes), BF16),
        pltpu.VMEM((2, share, plan.points), F32),
        pltpu.VMEM((share, plan.points), F32),
        pltpu.VMEM((plan.total, plan.genes), BF16),
        pltpu.VMEM((1, plan.genes), F32),
        pltpu.VMEM((plan.table, rows), BF16),
        pltpu.VMEM((blocks, 2, rows), F32),
        pltpu.VMEM((128, rows), F32),
        pltpu.VMEM((blocks * rows, DEPTH), BF16),
        pltpu.VMEM((share, DEPTH, plan.points), F32),
        pltpu.VMEM((share, 2 * blocks, half, 128), F32),
        pltpu.VMEM((2, subs, lats, share, half), F32),
        pltpu.VMEM((2, max(1, subs - 1), lats, share, half), F32),
        pltpu.VMEM((2, lats, share, half), sent),
        pltpu.VMEM((2, genes, lats, share, half), sent),
        pltpu.VMEM((plan.total, rows), BF16),
        pltpu.VMEM((plan.total, half), F32),
        pltpu.VMEM((rows, plan.genes), BF16),
        pltpu.VMEM((plan.total, half), F32),
        pltpu.VMEM((2, plan.owners, lats, share, half), F32),
        pltpu.VMEM((2, max(1, genes - 1), lats, share, half), F32),
        pltpu.VMEM((2, lats, share, half), F32),
        pltpu.VMEM((2, blocks, share, half), F32),
        pltpu.VMEM((128, half), F32),
        pltpu.VMEM((blocks * half, plan.turned), BF16),
        pltpu.VMEM((blocks, half, 128), F32),
        pltpu.VMEM((subs, lats, depth, plan.genes), F32),
        pltpu.VMEM((max(1, subs - 1), lats, depth, plan.genes), F32),
        pltpu.VMEM((lats, lats, depth, plan.genes), F32),
        pltpu.VMEM((lats, depth, plan.genes), F32),
        pltpu.VMEM((share, 8, plan.points), F32),
        pltpu.VMEM((2, plan.points // 256, 128), F32),
        pltpu.VMEM((share, 2, plan.points // 256, 128), jnp.int16),
        pltpu.VMEM((share, 2, 1, 128), F32),
        dma((5,)),
        dma((2, max(1, flat))),
        dma((2, 2, max(1, subs - 1))),
        dma((2, 2, max(1, far))),
        dma((2, 2, max(1, genes - 1))),
        dma((2, 2, max(1, flat))),
        dma((2, 3, max(1, subs - 1, lats - 1), lats)),
        dma((2, 2, share, 2, max(1, genes - 1))),
        dma((2, share, 2)),
        dma((lats,)),
    ]
    return pl.pallas_call(
        functools.partial(body, plan),
        in_specs=[vmem] * 4 + [anywhere] * 5,
        out_specs=[anywhere] * 3,
        out_shape=[
            jax.ShapeDtypeStruct((subs, lats, depth, plan.genes), F32),
            jax.ShapeDtypeStruct((genes, share, 2, plan.points // 256, 128), jnp.int16),
            jax.ShapeDtypeStruct((genes, share, 2, 1, 128), F32),
        ],
        scratch_shapes=scratch,
        compiler_params=pltpu.CompilerParams(
            collective_id=0, has_side_effects=True, vmem_limit_bytes=60 * 2**20
        ),
    )(*args)


def on_device(
    cell_index,
    coords_table,
    expr_table,
    inducing,
    ind_weights,
    lengthscale,
    variance,
    mixing,
    noise_prec,
):
    genes, lats, subs = (lax.axis_size(axis) for axis in ("gene", "lat", "sub"))
    latents, count = ind_weights.shape
    owners = math.gcd(genes, latents)
    split = genes // owners
    share = latents // owners
    plan = Plan(
        gene=genes,
        lat=lats,
        sub=subs,
        rows=cell_index.shape[0],
        table=coords_table.shape[1],
        lats=latents,
        count=count,
        genes=expr_table.shape[1],
        share=share,
        split=split,
        sliced=share % 8 != 0,
        scale=-1.0 / math.sqrt(cell_index.shape[0] * lats * subs),
    )
    if plan.sliced:
        place = lax.axis_index("gene")
        first, cut = place // split * share, lax.rem(place, split) * plan.points
        inducing = lax.dynamic_slice(inducing, (0, first, cut), (2, share, plan.points))
        ind_weights = lax.dynamic_slice(ind_weights, (first, cut), (share, plan.points))
    mix, codes, tops = fused(
        plan,
        cell_index[None, :],
        coords_table,
        lengthscale[None, :],
        variance[None, :],
        expr_table,
        inducing,
        ind_weights,
        mixing,
        noise_prec[None, :],
    )
    return lay(plan, mix, codes, tops)


def solution(mesh):
    in_specs = (
        P(("group", "lat", "sub")),
        P("group", ("lat", "sub")),
        P(("group", "lat", "sub"), "gene"),
        P("group", "lat", "sub"),
        P(("group", "lat"), "sub"),
        P(("group", "lat")),
        P(("group", "lat")),
        P("group", "gene"),
        P(("group", "gene")),
    )
    out_specs = (P("group", "gene"), P(("group", "lat"), "sub"))
    return jax.shard_map(
        on_device, mesh=mesh, in_specs=in_specs, out_specs=out_specs, check_vma=False
    )
```

```python
import functools
import math
from typing import NamedTuple

import jax
import jax.numpy as jnp
from jax import lax
from jax.experimental import pallas as pl
from jax.experimental.pallas import tpu as pltpu
from jax.sharding import PartitionSpec as P

F32 = jnp.float32
BF16 = jnp.bfloat16
DEPTH = 24
SPARE = 21
CENTER = 0.5
LOG2E = math.log2(math.e)
CACHE = 40 * 2**20
LEFT = (0, 0, 1, 1, 0, 2)
RIGHT = (0, 1, 0, 1, 2, 0)


class Plan(NamedTuple):
    gene: int
    lat: int
    sub: int
    rows: int
    table: int
    lats: int
    count: int
    genes: int
    share: int
    split: int
    sliced: bool
    scale: float

    @property
    def blocks(self):
        return self.lat * self.sub

    @property
    def points(self):
        return self.count // self.split

    @property
    def owners(self):
        return self.gene // self.split

    @property
    def total(self):
        return self.lat * self.lats

    @property
    def half(self):
        return self.rows // 2

    @property
    def turned(self):
        return -(-3 * self.share // 8) * 8

    @property
    def tile(self):
        return min(256, self.points)

    @property
    def cached(self):
        return min(self.points // self.tile, CACHE // (self.share * self.blocks * self.half * self.tile * 4))

    @property
    def wide(self):
        return min(512, self.genes)


BIAS = 128
LEAST = 2.0**-120


def bit_rows(shape):
    row = lax.broadcasted_iota(jnp.int32, shape, 0)
    return row, row < 8


def code(value):
    top = jnp.maximum(jnp.max(jnp.abs(value), axis=0, keepdims=True), LEAST)
    power = jnp.floor(jnp.log(top) * LOG2E + 1e-5) + 1.0
    row, marked = bit_rows(value.shape)
    scaled = value * jnp.exp2(15.0 - power)
    fine = jnp.clip(jnp.floor(scaled + 0.5), -32767.0, 32767.0).astype(jnp.int32)
    coarse = jnp.clip(jnp.floor(scaled * 0.5 + 0.5), -16383.0, 16383.0).astype(jnp.int32) * 2
    place = jnp.where(marked, row, 0)
    bit = jnp.bitwise_and(jnp.right_shift(power.astype(jnp.int32) + BIAS, place), 1)
    return jnp.where(marked, coarse + bit, fine).astype(jnp.int16)


def decode(codes):
    codes = codes.astype(jnp.int32)
    row, marked = bit_rows(codes.shape)
    bit = jnp.where(marked, jnp.bitwise_and(codes, 1), 0)
    weight = jnp.left_shift(bit, jnp.where(marked, row, 0)).astype(F32)
    power = jnp.sum(weight, axis=0, keepdims=True) - float(BIAS)
    return (codes - bit).astype(F32) * jnp.exp2(power - 15.0)


def pieces(value):
    high = value.astype(BF16).astype(F32)
    rest = value - high
    middle = rest.astype(BF16).astype(F32)
    low = (rest - middle).astype(BF16).astype(F32)
    return high, middle, low


def point_features(plan, scale, points_ref, weight_ref, table_ref):
    step = min(512, plan.points)

    def part(i, carry):
        cols = pl.ds(pl.multiple_of(i * step, 128), step)
        x = points_ref[0, :, cols] - CENTER
        y = points_ref[1, :, cols] - CENTER
        px = pieces(x * (2.0 * scale))
        py = pieces(y * (2.0 * scale))
        ps = pieces(jnp.broadcast_to(-scale, x.shape))
        pn = pieces((x * x + y * y) * -scale)
        rows = [px[k] for k in RIGHT] + [py[k] for k in RIGHT] + [ps[k] for k in RIGHT]
        rows += list(pn) + [weight_ref[:, cols]] + [jnp.zeros_like(x)] * (DEPTH - SPARE - 1)
        for place, row in enumerate(rows):
            for lane in range(plan.share):
                table_ref[lane, place : place + 1, cols] = row[lane : lane + 1, :]
        return carry

    lax.fori_loop(0, plan.points // step, part, 0)


def cell_features(plan, block, xy_ref, side_ref, feat_ref):
    x = xy_ref[block, 0:1, :] - CENTER
    y = xy_ref[block, 1:2, :] - CENTER
    px, py, pn = pieces(x), pieces(y), pieces(x * x + y * y)
    rows = [px[k] for k in LEFT] + [py[k] for k in LEFT] + [pn[k] for k in LEFT]
    for place, row in enumerate(rows):
        side_ref[place : place + 1, :] = row
    place = pl.ds(pl.multiple_of(block * plan.rows, plan.rows), plan.rows)
    feat_ref[place, :] = side_ref[...].T[:, :DEPTH].astype(BF16)


def body(
    plan,
    index_ref,
    coords_ref,
    length_ref,
    height_ref,
    expr_hbm,
    points_hbm,
    weight_hbm,
    mixing_hbm,
    noise_hbm,
    mix_out,
    all_out,
    expr_ref,
    points_ref,
    weight_ref,
    mixing_ref,
    noise_ref,
    pick_ref,
    xy_ref,
    side_ref,
    feat_ref,
    table_ref,
    total_ref,
    part_ref,
    near_ref,
    final_ref,
    latent_recv,
    latent_ref,
    side_lat_ref,
    seen_ref,
    cell_ref,
    chunk_ref,
    rs_ref,
    own_ref,
    lg_ref,
    lgside_ref,
    lgt_ref,
    wide_ref,
    mix_ref,
    mix_near,
    mix_all,
    mix_sum,
    sum_ref,
    row_ref,
    all_ref,
    cache_ref,
    load_sem,
    xy_sem,
    near_sem,
    latent_sem,
    rs_sem,
    lg_sem,
    mix_sem,
    all_sem,
    all_keep,
    keep_sem,
):
    genes, lats, subs, blocks = plan.gene, plan.lat, plan.sub, plan.blocks
    rows, half, share = plan.rows, plan.half, plan.share
    g, l, s = lax.axis_index("gene"), lax.axis_index("lat"), lax.axis_index("sub")
    owner, slab = g // plan.split, lax.rem(g, plan.split)
    me = l * subs + s

    def at(dg=0, dl=0, ds=0):
        return {"gene": lax.rem(g + dg, genes), "lat": lax.rem(l + dl, lats), "sub": lax.rem(s + ds, subs)}

    def send(src, dst, sems, k, device):
        return pltpu.make_async_remote_copy(
            src_ref=src,
            dst_ref=dst,
            send_sem=sems.at[(0, *k)],
            recv_sem=sems.at[(1, *k)],
            device_id=device,
            device_id_type=pl.DeviceIdType.MESH,
        )

    if plan.sliced:
        points_src, weight_src = points_hbm, weight_hbm
    else:
        mine = pl.ds(pl.multiple_of(owner * share, 8), share)
        cut = pl.ds(pl.multiple_of(slab * plan.points, 128), plan.points)
        points_src, weight_src = points_hbm.at[:, mine, cut], weight_hbm.at[mine, cut]
    loads = [
        pltpu.make_async_copy(points_src, points_ref, load_sem.at[0]),
        pltpu.make_async_copy(weight_src, weight_ref, load_sem.at[1]),
        pltpu.make_async_copy(expr_hbm, expr_ref, load_sem.at[2]),
        pltpu.make_async_copy(mixing_hbm, mixing_ref, load_sem.at[3]),
        pltpu.make_async_copy(noise_hbm, noise_ref, load_sem.at[4]),
    ]
    for load in loads[:2]:
        load.start()

    far = [(dg, dl, 0) for dg in range(genes) for dl in range(lats) if dg or dl]
    flat = [(0, dl, ds) for dl in range(lats) for ds in range(subs) if dl or ds]
    peers = sorted(set(far) | set(flat))
    barrier = pltpu.get_barrier_semaphore()
    for peer in peers:
        pl.semaphore_signal(barrier, inc=1, device_id=at(*peer), device_id_type=pl.DeviceIdType.MESH)

    pick = lax.broadcasted_iota(jnp.int32, (plan.table, rows), 0) == index_ref[...]
    pick_ref[...] = pick.astype(F32).astype(BF16)
    local = jnp.zeros((2, rows), F32)
    for piece in pieces(coords_ref[...]):
        local = local + jnp.dot(piece.astype(BF16), pick_ref[...], preferred_element_type=F32)
    xy_ref[me] = local
    side_ref[...] = jnp.zeros_like(side_ref)
    side_ref[18:21, :] = jnp.ones((3, rows), F32)
    cell_features(plan, me, xy_ref, side_ref, feat_ref)

    lane = lax.broadcasted_iota(jnp.int32, (share, plan.lats), 1)
    chosen = lane == lax.broadcasted_iota(jnp.int32, (share, plan.lats), 0) + owner * share
    length = jnp.sum(jnp.where(chosen, length_ref[...], 0.0), axis=1, keepdims=True)
    height = jnp.sum(jnp.where(chosen, height_ref[...], 0.0), axis=1, keepdims=True)
    loads[0].wait()
    loads[1].wait()
    for load in loads[2:]:
        load.start()
    point_features(plan, (0.5 * LOG2E) / (length * length), points_ref, weight_ref, table_ref)

    def ring(k):
        return lax.rem(me + k, blocks)

    def flush(part):
        lane = lax.broadcasted_iota(jnp.int32, (half, 128), 1)
        for k in range(blocks):
            sums = jnp.zeros((half, 128), F32)
            for j in range(share):
                column = jnp.sum(total_ref[j, 2 * k + part], axis=1, keepdims=True)
                sums = jnp.where(lane == j, column, sums)
            part_ref[part, lax.rem(ring(k), subs), ring(k) // subs] = sums.T[:share, :]
        start(near_copies(part))

    def forward(units, stages):
        def step(j, carry):
            for when, stage in stages:
                pl.when(j == when)(stage)
            for k, part in units:
                place = pl.multiple_of(ring(k) * rows + part * half, half)
                feat = feat_ref[pl.ds(place, half), :]
                total = jnp.zeros((half, 128), F32)
                for start in range(0, plan.points, plan.tile):
                    cols = slice(start, start + plan.tile)
                    value = jnp.exp2(
                        jnp.dot(feat, table_ref[j, :, cols].astype(BF16), preferred_element_type=F32)
                    )
                    if part == 1 and start // plan.tile < plan.cached:
                        cache_ref[j, k, start // plan.tile] = value
                    for first in range(0, plan.tile, 128):
                        w = table_ref[j, SPARE : SPARE + 1, start + first : start + first + 128]
                        total = total + value[:, first : first + 128] * w
                total_ref[j, 2 * k + part] = total
            return carry

        lax.fori_loop(0, share, step, 0)

    forward([(0, 0)], [])

    pl.semaphore_wait(barrier, len(peers))
    copies = []
    for k, peer in enumerate(flat):
        copies.append(send(xy_ref.at[me], xy_ref.at[me], xy_sem, (k,), at(*peer)))
        copies[-1].start()
    forward([(0, 1)], [])
    for load in loads[2:]:
        load.wait()
    gene_tiles = [slice(first, first + plan.wide) for first in range(0, plan.genes, plan.wide)]
    for cols in gene_tiles:
        seen = lax.dot_general(
            pick_ref[...], expr_ref[:, cols], (((0,), (0,)), ((), ())), preferred_element_type=F32
        )
        seen_ref[:, cols] = seen.astype(BF16)
    for copy in copies:
        copy.wait()
    for k in range(1, blocks):
        cell_features(plan, ring(k), xy_ref, side_ref, feat_ref)

    def near_copies(part):
        return [
            send(part_ref.at[part, lax.rem(s + ds, subs)], near_ref.at[part, ds - 1], near_sem, (part, ds - 1), at(ds=ds))
            for ds in range(1, subs)
        ]

    def latent_copies(part):
        out = []
        for k, peer in enumerate(far):
            target = at(*peer)
            out.append(
                send(final_ref.at[part, target["lat"]], latent_recv.at[part, g, l], latent_sem, (part, k), target)
            )
        return out

    def rs_copies(part):
        out = []
        for dg in range(1, genes):
            target = at(dg=dg)
            source = chunk_ref.at[part, target["gene"] // plan.split]
            out.append(send(source, rs_ref.at[part, dg - 1], rs_sem, (part, dg - 1), target))
        return out

    def lg_copies(part):
        out = []
        for k, peer in enumerate(flat):
            target = at(*peer)
            out.append(send(own_ref.at[part, target["lat"]], lg_ref.at[part, me], lg_sem, (part, k), target))
        return out

    def start(copies):
        for copy in copies:
            copy.start()

    def wait(copies):
        for copy in copies:
            copy.wait()

    def sum_near(part):
        wait(near_copies(part))
        value = part_ref[part, s]
        for ds in range(1, subs):
            value = value + near_ref[part, ds - 1]
        value = value * height[None]
        final_ref[part] = value.astype(final_ref.dtype)
        start(latent_copies(part))
        latent_recv[part, g, l] = final_ref[part, l]

    def middle(part):
        wait(latent_copies(part))
        for lat in range(lats):
            for own in range(plan.owners):
                first = own * plan.split
                value = latent_recv[part, first, lat].astype(F32)
                for other in range(1, plan.split):
                    value = value + latent_recv[part, first + other, lat].astype(F32)
                base = lat * plan.lats + own * share
                side_lat_ref[base : base + share, :] = value
        cells = slice(part * half, (part + 1) * half)
        latent_ref[:, cells] = side_lat_ref[...].astype(BF16)
        turned = side_lat_ref[...].T.astype(BF16)
        cell = jnp.zeros((plan.total, half), F32)
        for cols in gene_tiles:
            mixing = mixing_ref[:, cols]
            predicted = jnp.dot(turned, mixing, preferred_element_type=F32)
            weighted = (noise_ref[:, cols] * (seen_ref[cells, cols].astype(F32) - predicted)).astype(BF16)
            seen_ref[cells, cols] = weighted
            cell = cell + lax.dot_general(
                mixing, weighted, (((1,), (1,)), ((), ())), preferred_element_type=F32
            )
        cell_ref[...] = cell
        for own in range(plan.owners):
            for lat in range(lats):
                base = lat * plan.lats + own * share
                chunk_ref[part, own, lat] = plan.scale * cell_ref[base : base + share, :]
        start(rs_copies(part))

    def sum_gene(part):
        wait(rs_copies(part))
        value = chunk_ref[part, owner]
        for dg in range(1, genes):
            value = value + rs_ref[part, dg - 1]
        own_ref[part] = value
        start(lg_copies(part))
        lg_ref[part, me] = own_ref[part, l]

    def turn(part):
        wait(lg_copies(part))
        for block in range(blocks):
            for p, piece in enumerate(pieces(lg_ref[part, block] * height)):
                lgside_ref[p * share : (p + 1) * share, :] = piece
            lgt_ref[block * half : (block + 1) * half, :] = (
                lgside_ref[...].T[:, : plan.turned].astype(BF16)
            )

    def mix_near_copies():
        return [
            send(mix_ref.at[lax.rem(s + ds, subs)], mix_near.at[ds - 1], mix_sem, (0, ds - 1, 0), at(ds=ds))
            for ds in range(1, subs)
        ]

    def mix_lat_copies(p):
        return [send(mix_all.at[l, p], mix_all.at[l, p], mix_sem, (1, dl - 1, p), at(dl=dl)) for dl in range(1, lats)]

    def mix_back_copies(p):
        return [send(mix_sum.at[p], mix_out.at[s, p], mix_sem, (2, ds - 1, p), at(ds=ds)) for ds in range(1, subs)]

    def mix_keep(p):
        return pltpu.make_async_copy(mix_sum.at[p], mix_out.at[s, p], keep_sem.at[p])

    def mix_part():
        depth = mix_ref.shape[2]
        for cols in gene_tiles:
            value = plan.scale * jnp.dot(latent_ref[...], seen_ref[:, cols], preferred_element_type=F32)
            for sub in range(subs):
                for p in range(lats):
                    base = (sub * lats + p) * depth
                    mix_ref[sub, p, :, cols] = value[base : base + depth, :]
        start(mix_near_copies())

    def mix_sub():
        wait(mix_near_copies())
        for p in range(lats):
            value = mix_ref[s, p]
            for ds in range(1, subs):
                value = value + mix_near[ds - 1, p]
            mix_all[l, p] = code(value)
            start(mix_lat_copies(p))

    def mix_lat(p):
        wait(mix_lat_copies(p))
        value = decode(mix_all[0, p])
        for lat in range(1, lats):
            value = value + decode(mix_all[lat, p])
        mix_sum[p] = value
        start(mix_back_copies(p))
        mix_keep(p).start()

    def gather_copies(j):
        return [
            send(all_ref.at[j], all_out.at[g, j], all_sem, (j, dg - 1), at(dg=dg)) for dg in range(1, genes)
        ] + [pltpu.make_async_copy(all_ref.at[j], all_out.at[g, j], all_keep.at[j])]

    def backward(part, stages):
        def step(j, carry):
            for when, stage in stages:
                pl.when(j == when)(stage)
            row = lax.broadcasted_iota(jnp.int32, (plan.turned, 128), 0)
            select = (lax.rem(row, share) == j).astype(F32).astype(BF16)
            for k in range(blocks):
                place = pl.multiple_of(ring(k) * half, half)
                turned = lgt_ref[pl.ds(place, half), :]
                wide_ref[k] = jnp.dot(turned, select, preferred_element_type=F32)
            tiles = list(range(plan.points // plan.tile))
            kept = tiles[: plan.cached] if part == 1 else []
            fresh = tiles[len(kept) :]
            lanes = plan.tile // 128
            held = [(t, f) for t in kept for f in range(lanes)]
            held_sums = [None] * len(held)
            groups = [(k, r) for k in range(blocks) for r in range(0, half, 8)] if held else []
            steps = len(fresh) * blocks
            pace = -(-len(groups) // max(1, steps))

            def settle(sums, t, f):
                r = t * lanes + f
                here = slice(r * 128, (r + 1) * 128)
                if part == 0:
                    sum_ref[j, :, here] = sums
                else:
                    row_ref[r : r + 1, :] = jnp.sum(sum_ref[j, :, here] + sums, axis=0, keepdims=True)

            def spend(groups):
                for k, r in groups:
                    wide = wide_ref[k, r : r + 8, :]
                    for i, (t, f) in enumerate(held):
                        term = cache_ref[j, k, t, r : r + 8, f * 128 : (f + 1) * 128] * wide
                        held_sums[i] = term if held_sums[i] is None else held_sums[i] + term

            for t in fresh:
                points = table_ref[j, :, t * plan.tile : (t + 1) * plan.tile].astype(BF16)
                sums = [None] * lanes
                for k in range(blocks):
                    place = pl.multiple_of(ring(k) * rows + part * half, half)
                    value = jnp.exp2(
                        jnp.dot(feat_ref[pl.ds(place, half), :], points, preferred_element_type=F32)
                    )
                    for f in range(lanes):
                        term = value[:, f * 128 : (f + 1) * 128] * wide_ref[k]
                        term = jnp.sum(term.reshape(half // 8, 8, 128), axis=0)
                        sums[f] = term if sums[f] is None else sums[f] + term
                    spend(groups[:pace])
                    groups = groups[pace:]
                for f in range(lanes):
                    settle(sums[f], t, f)
            spend(groups)
            for (t, f), sums in zip(held, held_sums):
                settle(sums, t, f)
            if part == 1:
                all_ref[j] = code(row_ref[...])
                start(gather_copies(j))
            return carry

        lax.fori_loop(0, share, step, 0)

    def when(k):
        return k * share // 8

    forward([(k, 0) for k in range(1, blocks)], [])
    flush(0)
    forward(
        [(k, 1) for k in range(1, blocks)],
        [
            (when(1), lambda: sum_near(0)),
            (when(5), lambda: middle(0)),
            (when(7), lambda: sum_gene(0)),
        ],
    )
    flush(1)
    lgside_ref[...] = jnp.zeros_like(lgside_ref)
    turn(0)
    backward(
        0,
        [
            (when(1), lambda: sum_near(1)),
            (when(4), lambda: middle(1)),
            (when(4), mix_part),
            (when(6), lambda: sum_gene(1)),
            (when(6), mix_sub),
        ],
    )
    turn(1)
    early = max(1, lats // 2)

    def first_parts():
        for p in range(early):
            mix_lat(p)

    backward(1, [(when(6), first_parts)])
    for p in range(early, lats):
        mix_lat(p)

    def finish(j, carry):
        wait(gather_copies(j))
        return carry

    lax.fori_loop(0, share, finish, 0)
    for p in range(lats):
        wait(mix_back_copies(p))
        mix_keep(p).wait()


def lay_body(plan, mix_hbm, all_hbm, mix_out, ind_out, mix_ref, all_ref, row_ref, ind_ref, in_sem, out_sem):
    subs, lats, depth, _ = mix_hbm.shape
    parts = [(sub, p) for sub in range(subs) for p in range(lats)]
    mixes = [
        pltpu.make_async_copy(mix_hbm.at[sub, p], mix_ref.at[i], in_sem.at[i]) for i, (sub, p) in enumerate(parts)
    ]
    outs = [
        pltpu.make_async_copy(mix_ref.at[i], mix_out.at[pl.ds(i * depth, depth)], out_sem.at[i])
        for i in range(len(parts))
    ]
    whole = pltpu.make_async_copy(all_hbm, all_ref, in_sem.at[len(parts)])
    for copy in [whole] + mixes:
        copy.start()
    whole.wait()
    last = []
    for owner in range(plan.owners):
        base = owner * plan.share
        for slab in range(plan.split):
            gene = owner * plan.split + slab
            for j in range(plan.share):
                row_ref[gene, j] = decode(all_ref[gene, j])
            for r in range(plan.points // 128):
                first = slab * plan.points + r * 128
                ind_ref[base : base + plan.share, first : first + 128] = row_ref[gene, :, r, :]
        if plan.share % 8 == 0:
            rows = pl.ds(base, plan.share)
            last.append(pltpu.make_async_copy(ind_ref.at[rows], ind_out.at[rows], out_sem.at[len(parts) + owner]))
            last[-1].start()
    if plan.share % 8:
        last.append(pltpu.make_async_copy(ind_ref, ind_out, out_sem.at[len(parts)]))
        last[-1].start()
    for copy, out in zip(mixes, outs):
        copy.wait()
        out.start()
    for copy in outs + last:
        copy.wait()


def lay(plan, mix, codes):
    subs, lats, depth, genes = mix.shape
    parts = subs * lats
    anywhere = pl.BlockSpec(memory_space=pl.ANY)
    return pl.pallas_call(
        functools.partial(lay_body, plan),
        in_specs=[anywhere] * 2,
        out_specs=[anywhere] * 2,
        out_shape=[
            jax.ShapeDtypeStruct((plan.total, genes), F32),
            jax.ShapeDtypeStruct((plan.lats, plan.count), F32),
        ],
        scratch_shapes=[
            pltpu.VMEM((parts, depth, genes), F32),
            pltpu.VMEM(codes.shape, jnp.int16),
            pltpu.VMEM((plan.gene, plan.share, plan.points // 128, 128), F32),
            pltpu.VMEM((plan.lats, plan.count), F32),
            pltpu.SemaphoreType.DMA((parts + 1,)),
            pltpu.SemaphoreType.DMA((parts + plan.owners,)),
        ],
        compiler_params=pltpu.CompilerParams(vmem_limit_bytes=60 * 2**20),
    )(mix, codes)


def fused(plan, *args):
    genes, lats, subs = plan.gene, plan.lat, plan.sub
    rows, half, share, blocks = plan.rows, plan.half, plan.share, plan.blocks
    depth = plan.total // (lats * subs)
    sent = BF16 if plan.split == 1 else F32
    dma = pltpu.SemaphoreType.DMA
    far = genes * lats - 1
    flat = blocks - 1
    vmem = pl.BlockSpec(memory_space=pltpu.VMEM)
    anywhere = pl.BlockSpec(memory_space=pl.ANY)
    scratch = [
        pltpu.VMEM((plan.table, plan.genes), BF16),
        pltpu.VMEM((2, share, plan.points), F32),
        pltpu.VMEM((share, plan.points), F32),
        pltpu.VMEM((plan.total, plan.genes), BF16),
        pltpu.VMEM((1, plan.genes), F32),
        pltpu.VMEM((plan.table, rows), BF16),
        pltpu.VMEM((blocks, 2, rows), F32),
        pltpu.VMEM((128, rows), F32),
        pltpu.VMEM((blocks * rows, DEPTH), BF16),
        pltpu.VMEM((share, DEPTH, plan.points), F32),
        pltpu.VMEM((share, 2 * blocks, half, 128), F32),
        pltpu.VMEM((2, subs, lats, share, half), F32),
        pltpu.VMEM((2, max(1, subs - 1), lats, share, half), F32),
        pltpu.VMEM((2, lats, share, half), sent),
        pltpu.VMEM((2, genes, lats, share, half), sent),
        pltpu.VMEM((plan.total, rows), BF16),
        pltpu.VMEM((plan.total, half), F32),
        pltpu.VMEM((rows, plan.genes), BF16),
        pltpu.VMEM((plan.total, half), F32),
        pltpu.VMEM((2, plan.owners, lats, share, half), F32),
        pltpu.VMEM((2, max(1, genes - 1), lats, share, half), F32),
        pltpu.VMEM((2, lats, share, half), F32),
        pltpu.VMEM((2, blocks, share, half), F32),
        pltpu.VMEM((128, half), F32),
        pltpu.VMEM((blocks * half, plan.turned), BF16),
        pltpu.VMEM((blocks, half, 128), F32),
        pltpu.VMEM((subs, lats, depth, plan.genes), F32),
        pltpu.VMEM((max(1, subs - 1), lats, depth, plan.genes), F32),
        pltpu.VMEM((lats, lats, depth, plan.genes), jnp.int16),
        pltpu.VMEM((lats, depth, plan.genes), F32),
        pltpu.VMEM((share, 8, plan.points), F32),
        pltpu.VMEM((plan.points // 128, 128), F32),
        pltpu.VMEM((share, plan.points // 128, 128), jnp.int16),
        pltpu.VMEM((share, blocks, max(1, plan.cached), half, plan.tile), F32),
        dma((5,)),
        dma((2, max(1, flat))),
        dma((2, 2, max(1, subs - 1))),
        dma((2, 2, max(1, far))),
        dma((2, 2, max(1, genes - 1))),
        dma((2, 2, max(1, flat))),
        dma((2, 3, max(1, subs - 1, lats - 1), lats)),
        dma((2, share, max(1, genes - 1))),
        dma((share,)),
        dma((lats,)),
    ]
    return pl.pallas_call(
        functools.partial(body, plan),
        in_specs=[vmem] * 4 + [anywhere] * 5,
        out_specs=[anywhere] * 2,
        out_shape=[
            jax.ShapeDtypeStruct((subs, lats, depth, plan.genes), F32),
            jax.ShapeDtypeStruct((genes, share, plan.points // 128, 128), jnp.int16),
        ],
        scratch_shapes=scratch,
        compiler_params=pltpu.CompilerParams(
            collective_id=0, has_side_effects=True, vmem_limit_bytes=67043328
        ),
    )(*args)


def on_device(
    cell_index,
    coords_table,
    expr_table,
    inducing,
    ind_weights,
    lengthscale,
    variance,
    mixing,
    noise_prec,
):
    genes, lats, subs = (lax.axis_size(axis) for axis in ("gene", "lat", "sub"))
    latents, count = ind_weights.shape
    owners = math.gcd(genes, latents)
    split = genes // owners
    share = latents // owners
    plan = Plan(
        gene=genes,
        lat=lats,
        sub=subs,
        rows=cell_index.shape[0],
        table=coords_table.shape[1],
        lats=latents,
        count=count,
        genes=expr_table.shape[1],
        share=share,
        split=split,
        sliced=share % 8 != 0,
        scale=-1.0 / math.sqrt(cell_index.shape[0] * lats * subs),
    )
    if plan.sliced:
        place = lax.axis_index("gene")
        first, cut = place // split * share, lax.rem(place, split) * plan.points
        inducing = lax.dynamic_slice(inducing, (0, first, cut), (2, share, plan.points))
        ind_weights = lax.dynamic_slice(ind_weights, (first, cut), (share, plan.points))
    mix, codes = fused(
        plan,
        cell_index[None, :],
        coords_table,
        lengthscale[None, :],
        variance[None, :],
        expr_table,
        inducing,
        ind_weights,
        mixing,
        noise_prec[None, :],
    )
    return lay(plan, mix, codes)


def solution(mesh):
    in_specs = (
        P(("group", "lat", "sub")),
        P("group", ("lat", "sub")),
        P(("group", "lat", "sub"), "gene"),
        P("group", "lat", "sub"),
        P(("group", "lat"), "sub"),
        P(("group", "lat")),
        P(("group", "lat")),
        P("group", "gene"),
        P(("group", "gene")),
    )
    out_specs = (P("group", "gene"), P(("group", "lat"), "sub"))
    return jax.shard_map(
        on_device, mesh=mesh, in_specs=in_specs, out_specs=out_specs, check_vma=False
    )
```

```python
import functools
import math
from typing import NamedTuple

import jax
import jax.numpy as jnp
from jax import lax
from jax.experimental import pallas as pl
from jax.experimental.pallas import tpu as pltpu
from jax.sharding import PartitionSpec as P

F32 = jnp.float32
BF16 = jnp.bfloat16
DEPTH = 24
SPARE = 21
CENTER = 0.5
LOG2E = math.log2(math.e)
PACK = 20
CACHE = 40 * 2**20
LEFT = (0, 0, 1, 1, 0, 2)
RIGHT = (0, 1, 0, 1, 2, 0)


class Plan(NamedTuple):
    gene: int
    lat: int
    sub: int
    rows: int
    table: int
    lats: int
    count: int
    genes: int
    share: int
    split: int
    sliced: bool
    scale: float

    @property
    def blocks(self):
        return self.lat * self.sub

    @property
    def points(self):
        return self.count // self.split

    @property
    def owners(self):
        return self.gene // self.split

    @property
    def total(self):
        return self.lat * self.lats

    @property
    def half(self):
        return self.rows // 2

    @property
    def turned(self):
        return -(-3 * self.share // 8) * 8

    @property
    def tile(self):
        return min(256, self.points)

    @property
    def cached(self):
        return min(self.points // self.tile, CACHE // (self.share * self.blocks * self.half * self.tile * 4))

    @property
    def wide(self):
        return min(512, self.genes)


BIAS = 128
LEAST = 2.0**-120


def bit_rows(shape):
    row = lax.broadcasted_iota(jnp.int32, shape, 0)
    return row, row < 8


def code(value):
    top = jnp.maximum(jnp.max(jnp.abs(value), axis=0, keepdims=True), LEAST)
    power = jnp.floor(jnp.log(top) * LOG2E + 1e-5) + 1.0
    row, marked = bit_rows(value.shape)
    scaled = value * jnp.exp2(15.0 - power)
    fine = jnp.clip(jnp.floor(scaled + 0.5), -32767.0, 32767.0).astype(jnp.int32)
    coarse = jnp.clip(jnp.floor(scaled * 0.5 + 0.5), -16383.0, 16383.0).astype(jnp.int32) * 2
    place = jnp.where(marked, row, 0)
    bit = jnp.bitwise_and(jnp.right_shift(power.astype(jnp.int32) + BIAS, place), 1)
    return jnp.where(marked, coarse + bit, fine).astype(jnp.int16)


def decode(codes):
    codes = codes.astype(jnp.int32)
    row, marked = bit_rows(codes.shape)
    bit = jnp.where(marked, jnp.bitwise_and(codes, 1), 0)
    weight = jnp.left_shift(bit, jnp.where(marked, row, 0)).astype(F32)
    power = jnp.sum(weight, axis=0, keepdims=True) - float(BIAS)
    return (codes - bit).astype(F32) * jnp.exp2(power - 15.0)


def pieces(value):
    high = value.astype(BF16).astype(F32)
    rest = value - high
    middle = rest.astype(BF16).astype(F32)
    low = (rest - middle).astype(BF16).astype(F32)
    return high, middle, low


def point_features(plan, scale, points_ref, weight_ref, table_ref):
    step = min(512, plan.points)

    def part(i, carry):
        cols = pl.ds(pl.multiple_of(i * step, 128), step)
        x = points_ref[0, :, cols] - CENTER
        y = points_ref[1, :, cols] - CENTER
        px = pieces(x * (2.0 * scale))
        py = pieces(y * (2.0 * scale))
        ps = pieces(jnp.broadcast_to(-scale, x.shape))
        pn = pieces((x * x + y * y) * -scale)
        rows = [px[k] for k in RIGHT] + [py[k] for k in RIGHT] + [ps[k] for k in RIGHT]
        rows += list(pn) + [weight_ref[:, cols]] + [jnp.zeros_like(x)] * (DEPTH - SPARE - 1)
        for place, row in enumerate(rows):
            for lane in range(plan.share):
                table_ref[lane, place : place + 1, cols] = row[lane : lane + 1, :]
        return carry

    lax.fori_loop(0, plan.points // step, part, 0)


def cell_features(plan, block, xy_ref, side_ref, feat_ref):
    x = xy_ref[block, 0:1, :] - CENTER
    y = xy_ref[block, 1:2, :] - CENTER
    px, py, pn = pieces(x), pieces(y), pieces(x * x + y * y)
    rows = [px[k] for k in LEFT] + [py[k] for k in LEFT] + [pn[k] for k in LEFT]
    for place, row in enumerate(rows):
        side_ref[place : place + 1, :] = row
    place = pl.ds(pl.multiple_of(block * plan.rows, plan.rows), plan.rows)
    feat_ref[place, :] = side_ref[...].T[:, :DEPTH].astype(BF16)


def body(
    plan,
    index_hbm,
    coords_hbm,
    length_hbm,
    height_hbm,
    expr_hbm,
    points_hbm,
    weight_hbm,
    mixing_hbm,
    noise_hbm,
    mix_out,
    all_out,
    index_ref,
    coords_ref,
    length_ref,
    height_ref,
    expr_ref,
    points_ref,
    weight_ref,
    mixing_ref,
    noise_ref,
    pick_ref,
    xy_ref,
    side_ref,
    feat_ref,
    table_ref,
    total_ref,
    part_ref,
    near_ref,
    final_ref,
    latent_recv,
    latent_ref,
    side_lat_ref,
    seen_ref,
    cell_ref,
    chunk_ref,
    rs_ref,
    own_ref,
    lg_ref,
    lgside_ref,
    lgt_ref,
    wide_ref,
    mix_ref,
    mix_near,
    mix_all,
    mix_sum,
    sum_ref,
    row_ref,
    all_ref,
    cache_ref,
    load_sem,
    xy_sem,
    near_sem,
    latent_sem,
    rs_sem,
    lg_sem,
    mix_sem,
    all_sem,
    all_keep,
    keep_sem,
):
    genes, lats, subs, blocks = plan.gene, plan.lat, plan.sub, plan.blocks
    rows, half, share = plan.rows, plan.half, plan.share
    g, l, s = lax.axis_index("gene"), lax.axis_index("lat"), lax.axis_index("sub")
    owner, slab = g // plan.split, lax.rem(g, plan.split)
    me = l * subs + s

    def at(dg=0, dl=0, ds=0):
        return {"gene": lax.rem(g + dg, genes), "lat": lax.rem(l + dl, lats), "sub": lax.rem(s + ds, subs)}

    def send(src, dst, sems, k, device):
        return pltpu.make_async_remote_copy(
            src_ref=src,
            dst_ref=dst,
            send_sem=sems.at[(0, *k)],
            recv_sem=sems.at[(1, *k)],
            device_id=device,
            device_id_type=pl.DeviceIdType.MESH,
        )

    if plan.sliced:
        points_src, weight_src = points_hbm, weight_hbm
    else:
        mine = pl.ds(pl.multiple_of(owner * share, 8), share)
        cut = pl.ds(pl.multiple_of(slab * plan.points, 128), plan.points)
        points_src, weight_src = points_hbm.at[:, mine, cut], weight_hbm.at[mine, cut]
    loads = [
        pltpu.make_async_copy(points_src, points_ref, load_sem.at[0]),
        pltpu.make_async_copy(weight_src, weight_ref, load_sem.at[1]),
        pltpu.make_async_copy(expr_hbm, expr_ref, load_sem.at[2]),
        pltpu.make_async_copy(mixing_hbm, mixing_ref, load_sem.at[3]),
        pltpu.make_async_copy(noise_hbm, noise_ref, load_sem.at[4]),
    ]
    small = [
        pltpu.make_async_copy(index_hbm, index_ref, load_sem.at[5]),
        pltpu.make_async_copy(coords_hbm, coords_ref, load_sem.at[6]),
        pltpu.make_async_copy(length_hbm, length_ref, load_sem.at[7]),
        pltpu.make_async_copy(height_hbm, height_ref, load_sem.at[8]),
    ]
    for load in small + loads[:2]:
        load.start()

    far = [(dg, dl, 0) for dg in range(genes) for dl in range(lats) if dg or dl]
    flat = [(0, dl, ds) for dl in range(lats) for ds in range(subs) if dl or ds]
    peers = sorted(set(far) | set(flat))
    barrier = pltpu.get_barrier_semaphore()
    for peer in peers:
        pl.semaphore_signal(barrier, inc=1, device_id=at(*peer), device_id_type=pl.DeviceIdType.MESH)

    for load in small:
        load.wait()
    pick = lax.broadcasted_iota(jnp.int32, (plan.table, rows), 0) == index_ref[...]
    pick_ref[...] = pick.astype(F32).astype(BF16)
    local = jnp.zeros((2, rows), F32)
    for piece in pieces(coords_ref[...]):
        local = local + jnp.dot(piece.astype(BF16), pick_ref[...], preferred_element_type=F32)
    xy_ref[me] = local
    side_ref[...] = jnp.zeros_like(side_ref)
    side_ref[18:21, :] = jnp.ones((3, rows), F32)
    cell_features(plan, me, xy_ref, side_ref, feat_ref)

    lane = lax.broadcasted_iota(jnp.int32, (share, plan.lats), 1)
    chosen = lane == lax.broadcasted_iota(jnp.int32, (share, plan.lats), 0) + owner * share
    length = jnp.sum(jnp.where(chosen, length_ref[...], 0.0), axis=1, keepdims=True)
    height = jnp.sum(jnp.where(chosen, height_ref[...], 0.0), axis=1, keepdims=True)
    loads[0].wait()
    loads[1].wait()
    for load in loads[2:]:
        load.start()
    point_features(plan, (0.5 * LOG2E) / (length * length), points_ref, weight_ref, table_ref)

    def ring(k):
        return lax.rem(me + k, blocks)

    def flush(part):
        lane = lax.broadcasted_iota(jnp.int32, (half, 128), 1)
        for k in range(blocks):
            sums = jnp.zeros((half, 128), F32)
            for j in range(share):
                column = jnp.sum(total_ref[j, 2 * k + part], axis=1, keepdims=True)
                sums = jnp.where(lane == j, column, sums)
            part_ref[part, lax.rem(ring(k), subs), ring(k) // subs] = sums.T[:share, :]
        start(near_copies(part))

    def forward(units, stages=(), low=0, high=share, step=1):
        step = math.gcd(step, high - low) if high > low else 1

        def products(i, carry):
            for when, stage in stages:
                pl.when(i == (when - low) // step)(stage)
            for j in [low + i * step + d for d in range(step)]:
                for k, part in units:
                    place = pl.multiple_of(ring(k) * rows + part * half, half)
                    feat = feat_ref[pl.ds(place, half), :]
                    total = jnp.zeros((half, 128), F32)
                    for start in range(0, plan.points, plan.tile):
                        cols = slice(start, start + plan.tile)
                        value = jnp.exp2(
                            jnp.dot(feat, table_ref[j, :, cols].astype(BF16), preferred_element_type=F32)
                        )
                        if part == 1 and start // plan.tile < plan.cached:
                            cache_ref[j, k, start // plan.tile] = value
                        for first in range(0, plan.tile, 128):
                            w = table_ref[j, SPARE : SPARE + 1, start + first : start + first + 128]
                            total = total + value[:, first : first + 128] * w
                    total_ref[j, 2 * k + part] = total
            return carry

        lax.fori_loop(0, (high - low) // step, products, 0)

    def when(k):
        return k * share // 8

    forward([(0, 0)], step=4)

    pl.semaphore_wait(barrier, len(peers))
    copies = []
    for k, peer in enumerate(flat):
        copies.append(send(xy_ref.at[me], xy_ref.at[me], xy_sem, (k,), at(*peer)))
        copies[-1].start()
    forward([(0, 1)], high=when(4), step=4)
    for load in loads[2:]:
        load.wait()
    gene_tiles = [slice(first, first + plan.wide) for first in range(0, plan.genes, plan.wide)]
    for cols in gene_tiles:
        seen = lax.dot_general(
            pick_ref[...], expr_ref[:, cols], (((0,), (0,)), ((), ())), preferred_element_type=F32
        )
        seen_ref[:, cols] = seen.astype(BF16)
    for copy in copies:
        copy.wait()
    for k in range(1, blocks):
        cell_features(plan, ring(k), xy_ref, side_ref, feat_ref)

    def near_copies(part):
        return [
            send(part_ref.at[part, lax.rem(s + ds, subs)], near_ref.at[part, ds - 1], near_sem, (part, ds - 1), at(ds=ds))
            for ds in range(1, subs)
        ]

    def latent_copies(part):
        out = []
        for k, peer in enumerate(far):
            target = at(*peer)
            out.append(
                send(final_ref.at[part, target["lat"]], latent_recv.at[part, g, l], latent_sem, (part, k), target)
            )
        return out

    def rs_copies(part):
        out = []
        for dg in range(1, genes):
            target = at(dg=dg)
            source = chunk_ref.at[part, target["gene"] // plan.split]
            out.append(send(source, rs_ref.at[part, dg - 1], rs_sem, (part, dg - 1), target))
        return out

    def lg_copies(part):
        out = []
        for k, peer in enumerate(flat):
            target = at(*peer)
            out.append(send(own_ref.at[part, target["lat"]], lg_ref.at[part, me], lg_sem, (part, k), target))
        return out

    def start(copies):
        for copy in copies:
            copy.start()

    def wait(copies):
        for copy in copies:
            copy.wait()

    def sum_near(part):
        wait(near_copies(part))
        value = part_ref[part, s]
        for ds in range(1, subs):
            value = value + near_ref[part, ds - 1]
        value = value * height[None]
        final_ref[part] = value.astype(final_ref.dtype)
        start(latent_copies(part))
        latent_recv[part, g, l] = final_ref[part, l]

    def middle(part):
        wait(latent_copies(part))
        for lat in range(lats):
            for own in range(plan.owners):
                first = own * plan.split
                value = latent_recv[part, first, lat].astype(F32)
                for other in range(1, plan.split):
                    value = value + latent_recv[part, first + other, lat].astype(F32)
                base = lat * plan.lats + own * share
                side_lat_ref[base : base + share, :] = value
        cells = slice(part * half, (part + 1) * half)
        latent_ref[:, cells] = side_lat_ref[...].astype(BF16)
        turned = side_lat_ref[...].T.astype(BF16)
        cell = jnp.zeros((plan.total, half), F32)
        for cols in gene_tiles:
            mixing = mixing_ref[:, cols]
            predicted = jnp.dot(turned, mixing, preferred_element_type=F32)
            weighted = (noise_ref[:, cols] * (seen_ref[cells, cols].astype(F32) - predicted)).astype(BF16)
            seen_ref[cells, cols] = weighted
            cell = cell + lax.dot_general(
                mixing, weighted, (((1,), (1,)), ((), ())), preferred_element_type=F32
            )
        cell_ref[...] = cell
        for own in range(plan.owners):
            for lat in range(lats):
                base = lat * plan.lats + own * share
                chunk_ref[part, own, lat] = plan.scale * cell_ref[base : base + share, :]
        start(rs_copies(part))

    def sum_gene(part):
        wait(rs_copies(part))
        value = chunk_ref[part, owner]
        for dg in range(1, genes):
            value = value + rs_ref[part, dg - 1]
        own_ref[part] = value
        start(lg_copies(part))
        lg_ref[part, me] = own_ref[part, l]

    def turn(part):
        wait(lg_copies(part))
        for block in range(blocks):
            for p, piece in enumerate(pieces(lg_ref[part, block] * height)):
                lgside_ref[p * share : (p + 1) * share, :] = piece
            lgt_ref[block * half : (block + 1) * half, :] = (
                lgside_ref[...].T[:, : plan.turned].astype(BF16)
            )

    def mix_near_copies():
        return [
            send(mix_ref.at[lax.rem(s + ds, subs)], mix_near.at[ds - 1], mix_sem, (0, ds - 1, 0), at(ds=ds))
            for ds in range(1, subs)
        ]

    def mix_lat_copies(p):
        return [send(mix_all.at[l, p], mix_all.at[l, p], mix_sem, (1, dl - 1, p), at(dl=dl)) for dl in range(1, lats)]

    def mix_back_copies(p):
        return [send(mix_sum.at[p], mix_out.at[s, p], mix_sem, (2, ds - 1, p), at(ds=ds)) for ds in range(1, subs)]

    def mix_keep(p):
        return pltpu.make_async_copy(mix_sum.at[p], mix_out.at[s, p], keep_sem.at[p])

    def mix_part():
        depth = mix_ref.shape[2]
        for cols in gene_tiles:
            value = plan.scale * jnp.dot(latent_ref[...], seen_ref[:, cols], preferred_element_type=F32)
            for sub in range(subs):
                for p in range(lats):
                    base = (sub * lats + p) * depth
                    mix_ref[sub, p, :, cols] = value[base : base + depth, :]
        start(mix_near_copies())

    def mix_sub():
        wait(mix_near_copies())
        for p in range(lats):
            value = mix_ref[s, p]
            for ds in range(1, subs):
                value = value + mix_near[ds - 1, p]
            mix_all[l, p] = code(value)
            start(mix_lat_copies(p))

    def mix_lat(p):
        wait(mix_lat_copies(p))
        value = decode(mix_all[0, p])
        for lat in range(1, lats):
            value = value + decode(mix_all[lat, p])
        mix_sum[p] = value
        start(mix_back_copies(p))
        mix_keep(p).start()

    def gather_copies(j):
        return [
            send(all_ref.at[j], all_out.at[g, j], all_sem, (j, dg - 1), at(dg=dg)) for dg in range(1, genes)
        ] + [pltpu.make_async_copy(all_ref.at[j], all_out.at[g, j], all_keep.at[j])]

    def backward(part, stages):
        def step(j, carry):
            for when, stage in stages:
                pl.when(j == when)(stage)
            row = lax.broadcasted_iota(jnp.int32, (plan.turned, 128), 0)
            select = (lax.rem(row, share) == j).astype(F32).astype(BF16)
            for k in range(blocks):
                place = pl.multiple_of(ring(k) * half, half)
                turned = lgt_ref[pl.ds(place, half), :]
                wide_ref[k] = jnp.dot(turned, select, preferred_element_type=F32)
            tiles = list(range(plan.points // plan.tile))
            kept = tiles[: plan.cached] if part == 1 else []
            fresh = tiles[len(kept) :]
            lanes = plan.tile // 128
            held = [(t, f) for t in kept for f in range(lanes)]
            held_sums = [None] * len(held)
            packs = [range(i, min(i + PACK, len(held))) for i in range(0, len(held), PACK)]
            groups = [(pack, k, r) for pack in packs for k in range(blocks) for r in range(0, half, 8)]
            steps = len(fresh) * blocks
            pace = -(-len(groups) // max(1, steps))

            def settle(sums, t, f):
                r = t * lanes + f
                here = slice(r * 128, (r + 1) * 128)
                if part == 0:
                    sum_ref[j, :, here] = sums
                else:
                    row_ref[r : r + 1, :] = jnp.sum(sum_ref[j, :, here] + sums, axis=0, keepdims=True)

            def spend(groups):
                for pack, k, r in groups:
                    wide = wide_ref[k, r : r + 8, :]
                    for i in pack:
                        t, f = held[i]
                        term = cache_ref[j, k, t, r : r + 8, f * 128 : (f + 1) * 128] * wide
                        held_sums[i] = term if held_sums[i] is None else held_sums[i] + term

            for t in fresh:
                points = table_ref[j, :, t * plan.tile : (t + 1) * plan.tile].astype(BF16)
                sums = [None] * lanes
                for k in range(blocks):
                    place = pl.multiple_of(ring(k) * rows + part * half, half)
                    value = jnp.exp2(
                        jnp.dot(feat_ref[pl.ds(place, half), :], points, preferred_element_type=F32)
                    )
                    for f in range(lanes):
                        term = value[:, f * 128 : (f + 1) * 128] * wide_ref[k]
                        term = jnp.sum(term.reshape(half // 8, 8, 128), axis=0)
                        sums[f] = term if sums[f] is None else sums[f] + term
                    spend(groups[:pace])
                    groups = groups[pace:]
                for f in range(lanes):
                    settle(sums[f], t, f)
            spend(groups)
            for (t, f), sums in zip(held, held_sums):
                settle(sums, t, f)
            if part == 1:
                all_ref[j] = code(row_ref[...])
                start(gather_copies(j))
            return carry

        lax.fori_loop(0, share, step, 0)

    forward([(k, 0) for k in range(1, blocks)], step=2)
    flush(0)
    forward([(0, 1)], low=when(4), high=when(6), step=2)
    sum_near(0)
    forward([(0, 1)], low=when(6), step=2)
    forward(
        [(k, 1) for k in range(1, blocks)],
        [(when(3), lambda: middle(0)), (when(7), lambda: sum_gene(0))],
    )
    flush(1)
    lgside_ref[...] = jnp.zeros_like(lgside_ref)
    turn(0)
    backward(
        0,
        [
            (when(0), lambda: sum_near(1)),
            (when(3), lambda: middle(1)),
            (when(3), mix_part),
            (when(5), lambda: sum_gene(1)),
            (when(5), mix_sub),
        ],
    )
    turn(1)
    early = max(1, lats // 2)

    def first_parts():
        for p in range(early):
            mix_lat(p)

    backward(1, [(when(6), first_parts)])
    for p in range(early, lats):
        mix_lat(p)

    def finish(j, carry):
        wait(gather_copies(j))
        return carry

    lax.fori_loop(0, share, finish, 0)
    for p in range(lats):
        wait(mix_back_copies(p))
        mix_keep(p).wait()


def lay_body(plan, mix_hbm, all_hbm, mix_out, ind_out, mix_ref, all_ref, row_ref, ind_ref, in_sem, out_sem):
    subs, lats, depth, _ = mix_hbm.shape
    parts = [(sub, p) for sub in range(subs) for p in range(lats)]
    mixes = [
        pltpu.make_async_copy(mix_hbm.at[sub, p], mix_ref.at[i], in_sem.at[i]) for i, (sub, p) in enumerate(parts)
    ]
    outs = [
        pltpu.make_async_copy(mix_ref.at[i], mix_out.at[pl.ds(i * depth, depth)], out_sem.at[i])
        for i in range(len(parts))
    ]
    whole = pltpu.make_async_copy(all_hbm, all_ref, in_sem.at[len(parts)])
    for copy in [whole] + mixes:
        copy.start()
    whole.wait()
    last = []
    for owner in range(plan.owners):
        base = owner * plan.share
        for slab in range(plan.split):
            gene = owner * plan.split + slab
            for j in range(plan.share):
                row_ref[gene, j] = decode(all_ref[gene, j])
            for r in range(plan.points // 128):
                first = slab * plan.points + r * 128
                ind_ref[base : base + plan.share, first : first + 128] = row_ref[gene, :, r, :]
        if plan.share % 8 == 0:
            rows = pl.ds(base, plan.share)
            last.append(pltpu.make_async_copy(ind_ref.at[rows], ind_out.at[rows], out_sem.at[len(parts) + owner]))
            last[-1].start()
    if plan.share % 8:
        last.append(pltpu.make_async_copy(ind_ref, ind_out, out_sem.at[len(parts)]))
        last[-1].start()
    for copy, out in zip(mixes, outs):
        copy.wait()
        out.start()
    for copy in outs + last:
        copy.wait()


def lay(plan, mix, codes):
    subs, lats, depth, genes = mix.shape
    parts = subs * lats
    anywhere = pl.BlockSpec(memory_space=pl.ANY)
    return pl.pallas_call(
        functools.partial(lay_body, plan),
        in_specs=[anywhere] * 2,
        out_specs=[anywhere] * 2,
        out_shape=[
            jax.ShapeDtypeStruct((plan.total, genes), F32),
            jax.ShapeDtypeStruct((plan.lats, plan.count), F32),
        ],
        scratch_shapes=[
            pltpu.VMEM((parts, depth, genes), F32),
            pltpu.VMEM(codes.shape, jnp.int16),
            pltpu.VMEM((plan.gene, plan.share, plan.points // 128, 128), F32),
            pltpu.VMEM((plan.lats, plan.count), F32),
            pltpu.SemaphoreType.DMA((parts + 1,)),
            pltpu.SemaphoreType.DMA((parts + plan.owners,)),
        ],
        compiler_params=pltpu.CompilerParams(vmem_limit_bytes=60 * 2**20),
    )(mix, codes)


def fused(plan, *args):
    genes, lats, subs = plan.gene, plan.lat, plan.sub
    rows, half, share, blocks = plan.rows, plan.half, plan.share, plan.blocks
    depth = plan.total // (lats * subs)
    sent = BF16 if plan.split == 1 else F32
    dma = pltpu.SemaphoreType.DMA
    far = genes * lats - 1
    flat = blocks - 1
    anywhere = pl.BlockSpec(memory_space=pl.ANY)
    scratch = [
        pltpu.VMEM((1, rows), jnp.int32),
        pltpu.VMEM((2, plan.table), F32),
        pltpu.VMEM((1, plan.lats), F32),
        pltpu.VMEM((1, plan.lats), F32),
        pltpu.VMEM((plan.table, plan.genes), BF16),
        pltpu.VMEM((2, share, plan.points), F32),
        pltpu.VMEM((share, plan.points), F32),
        pltpu.VMEM((plan.total, plan.genes), BF16),
        pltpu.VMEM((1, plan.genes), F32),
        pltpu.VMEM((plan.table, rows), BF16),
        pltpu.VMEM((blocks, 2, rows), F32),
        pltpu.VMEM((128, rows), F32),
        pltpu.VMEM((blocks * rows, DEPTH), BF16),
        pltpu.VMEM((share, DEPTH, plan.points), F32),
        pltpu.VMEM((share, 2 * blocks, half, 128), F32),
        pltpu.VMEM((2, subs, lats, share, half), F32),
        pltpu.VMEM((2, max(1, subs - 1), lats, share, half), F32),
        pltpu.VMEM((2, lats, share, half), sent),
        pltpu.VMEM((2, genes, lats, share, half), sent),
        pltpu.VMEM((plan.total, rows), BF16),
        pltpu.VMEM((plan.total, half), F32),
        pltpu.VMEM((rows, plan.genes), BF16),
        pltpu.VMEM((plan.total, half), F32),
        pltpu.VMEM((2, plan.owners, lats, share, half), F32),
        pltpu.VMEM((2, max(1, genes - 1), lats, share, half), F32),
        pltpu.VMEM((2, lats, share, half), F32),
        pltpu.VMEM((2, blocks, share, half), F32),
        pltpu.VMEM((128, half), F32),
        pltpu.VMEM((blocks * half, plan.turned), BF16),
        pltpu.VMEM((blocks, half, 128), F32),
        pltpu.VMEM((subs, lats, depth, plan.genes), F32),
        pltpu.VMEM((max(1, subs - 1), lats, depth, plan.genes), F32),
        pltpu.VMEM((lats, lats, depth, plan.genes), jnp.int16),
        pltpu.VMEM((lats, depth, plan.genes), F32),
        pltpu.VMEM((share, 8, plan.points), F32),
        pltpu.VMEM((plan.points // 128, 128), F32),
        pltpu.VMEM((share, plan.points // 128, 128), jnp.int16),
        pltpu.VMEM((share, blocks, max(1, plan.cached), half, plan.tile), F32),
        dma((9,)),
        dma((2, max(1, flat))),
        dma((2, 2, max(1, subs - 1))),
        dma((2, 2, max(1, far))),
        dma((2, 2, max(1, genes - 1))),
        dma((2, 2, max(1, flat))),
        dma((2, 3, max(1, subs - 1, lats - 1), lats)),
        dma((2, share, max(1, genes - 1))),
        dma((share,)),
        dma((lats,)),
    ]
    return pl.pallas_call(
        functools.partial(body, plan),
        in_specs=[anywhere] * 9,
        out_specs=[anywhere] * 2,
        out_shape=[
            jax.ShapeDtypeStruct((subs, lats, depth, plan.genes), F32),
            jax.ShapeDtypeStruct((genes, share, plan.points // 128, 128), jnp.int16),
        ],
        scratch_shapes=scratch,
        compiler_params=pltpu.CompilerParams(
            collective_id=0, has_side_effects=True, vmem_limit_bytes=67043328
        ),
    )(*args)


def on_device(
    cell_index,
    coords_table,
    expr_table,
    inducing,
    ind_weights,
    lengthscale,
    variance,
    mixing,
    noise_prec,
):
    genes, lats, subs = (lax.axis_size(axis) for axis in ("gene", "lat", "sub"))
    latents, count = ind_weights.shape
    owners = math.gcd(genes, latents)
    split = genes // owners
    share = latents // owners
    plan = Plan(
        gene=genes,
        lat=lats,
        sub=subs,
        rows=cell_index.shape[0],
        table=coords_table.shape[1],
        lats=latents,
        count=count,
        genes=expr_table.shape[1],
        share=share,
        split=split,
        sliced=share % 8 != 0,
        scale=-1.0 / math.sqrt(cell_index.shape[0] * lats * subs),
    )
    if plan.sliced:
        place = lax.axis_index("gene")
        first, cut = place // split * share, lax.rem(place, split) * plan.points
        inducing = lax.dynamic_slice(inducing, (0, first, cut), (2, share, plan.points))
        ind_weights = lax.dynamic_slice(ind_weights, (first, cut), (share, plan.points))
    mix, codes = fused(
        plan,
        cell_index[None, :],
        coords_table,
        lengthscale[None, :],
        variance[None, :],
        expr_table,
        inducing,
        ind_weights,
        mixing,
        noise_prec[None, :],
    )
    return lay(plan, mix, codes)


def solution(mesh):
    in_specs = (
        P(("group", "lat", "sub")),
        P("group", ("lat", "sub")),
        P(("group", "lat", "sub"), "gene"),
        P("group", "lat", "sub"),
        P(("group", "lat"), "sub"),
        P(("group", "lat")),
        P(("group", "lat")),
        P("group", "gene"),
        P(("group", "gene")),
    )
    out_specs = (P("group", "gene"), P(("group", "lat"), "sub"))
    return jax.shard_map(
        on_device, mesh=mesh, in_specs=in_specs, out_specs=out_specs, check_vma=False
    )
```

```python
import functools
import math
from typing import NamedTuple

import jax
import jax.numpy as jnp
from jax import lax
from jax.experimental import pallas as pl
from jax.experimental.pallas import tpu as pltpu
from jax.sharding import PartitionSpec as P

F32 = jnp.float32
BF16 = jnp.bfloat16
DEPTH = 24
SPARE = 21
CENTER = 0.5
LOG2E = math.log2(math.e)
PACK = 20
CACHE = 40 * 2**20
LEFT = (0, 0, 1, 1, 0, 2)
RIGHT = (0, 1, 0, 1, 2, 0)


class Plan(NamedTuple):
    gene: int
    lat: int
    sub: int
    rows: int
    table: int
    lats: int
    count: int
    genes: int
    share: int
    split: int
    sliced: bool
    scale: float

    @property
    def blocks(self):
        return self.lat * self.sub

    @property
    def points(self):
        return self.count // self.split

    @property
    def owners(self):
        return self.gene // self.split

    @property
    def total(self):
        return self.lat * self.lats

    @property
    def half(self):
        return self.rows // 2

    @property
    def turned(self):
        return -(-3 * self.share // 8) * 8

    @property
    def tile(self):
        return min(256, self.points)

    @property
    def cached(self):
        return min(self.points // self.tile, CACHE // (self.share * self.blocks * self.half * self.tile * 4))

    @property
    def wide(self):
        return min(512, self.genes)


BIAS = 128
LEAST = 2.0**-120


def bit_rows(shape):
    row = lax.broadcasted_iota(jnp.int32, shape, 0)
    return row, row < 8


def code(value):
    top = jnp.maximum(jnp.max(jnp.abs(value), axis=0, keepdims=True), LEAST)
    power = jnp.floor(jnp.log(top) * LOG2E + 1e-5) + 1.0
    row, marked = bit_rows(value.shape)
    scaled = value * jnp.exp2(15.0 - power)
    fine = jnp.clip(jnp.floor(scaled + 0.5), -32767.0, 32767.0).astype(jnp.int32)
    coarse = jnp.clip(jnp.floor(scaled * 0.5 + 0.5), -16383.0, 16383.0).astype(jnp.int32) * 2
    place = jnp.where(marked, row, 0)
    bit = jnp.bitwise_and(jnp.right_shift(power.astype(jnp.int32) + BIAS, place), 1)
    return jnp.where(marked, coarse + bit, fine).astype(jnp.int16)


def decode(codes):
    codes = codes.astype(jnp.int32)
    row, marked = bit_rows(codes.shape)
    bit = jnp.where(marked, jnp.bitwise_and(codes, 1), 0)
    weight = jnp.left_shift(bit, jnp.where(marked, row, 0)).astype(F32)
    power = jnp.sum(weight, axis=0, keepdims=True) - float(BIAS)
    return (codes - bit).astype(F32) * jnp.exp2(power - 15.0)


def pieces(value):
    high = value.astype(BF16).astype(F32)
    rest = value - high
    middle = rest.astype(BF16).astype(F32)
    low = (rest - middle).astype(BF16).astype(F32)
    return high, middle, low


def point_features(plan, scale, points_ref, weight_ref, table_ref):
    step = min(512, plan.points)

    def part(i, carry):
        cols = pl.ds(pl.multiple_of(i * step, 128), step)
        x = points_ref[0, :, cols] - CENTER
        y = points_ref[1, :, cols] - CENTER
        px = pieces(x * (2.0 * scale))
        py = pieces(y * (2.0 * scale))
        ps = pieces(jnp.broadcast_to(-scale, x.shape))
        pn = pieces((x * x + y * y) * -scale)
        rows = [px[k] for k in RIGHT] + [py[k] for k in RIGHT] + [ps[k] for k in RIGHT]
        rows += list(pn) + [weight_ref[:, cols]] + [jnp.zeros_like(x)] * (DEPTH - SPARE - 1)
        for place, row in enumerate(rows):
            for lane in range(plan.share):
                table_ref[lane, place : place + 1, cols] = row[lane : lane + 1, :]
        return carry

    lax.fori_loop(0, plan.points // step, part, 0)


def cell_features(plan, block, xy_ref, side_ref, feat_ref):
    x = xy_ref[block, 0:1, :] - CENTER
    y = xy_ref[block, 1:2, :] - CENTER
    px, py, pn = pieces(x), pieces(y), pieces(x * x + y * y)
    rows = [px[k] for k in LEFT] + [py[k] for k in LEFT] + [pn[k] for k in LEFT]
    for place, row in enumerate(rows):
        side_ref[place : place + 1, :] = row
    place = pl.ds(pl.multiple_of(block * plan.rows, plan.rows), plan.rows)
    feat_ref[place, :] = side_ref[...].T[:, :DEPTH].astype(BF16)


def body(
    plan,
    index_hbm,
    coords_hbm,
    length_hbm,
    height_hbm,
    expr_hbm,
    points_hbm,
    weight_hbm,
    mixing_hbm,
    noise_hbm,
    mix_out,
    all_out,
    index_ref,
    coords_ref,
    length_ref,
    height_ref,
    expr_ref,
    points_ref,
    weight_ref,
    mixing_ref,
    noise_ref,
    pick_ref,
    xy_ref,
    side_ref,
    feat_ref,
    table_ref,
    total_ref,
    part_ref,
    near_ref,
    final_ref,
    latent_recv,
    latent_ref,
    side_lat_ref,
    seen_ref,
    cell_ref,
    chunk_ref,
    rs_ref,
    own_ref,
    lg_ref,
    lgside_ref,
    lgt_ref,
    wide_ref,
    mix_ref,
    mix_near,
    mix_all,
    mix_sum,
    sum_ref,
    row_ref,
    all_ref,
    cache_ref,
    far_ref,
    load_sem,
    xy_sem,
    near_sem,
    latent_sem,
    rs_sem,
    lg_sem,
    mix_sem,
    all_sem,
    keep_sem,
):
    genes, lats, subs, blocks = plan.gene, plan.lat, plan.sub, plan.blocks
    rows, half, share = plan.rows, plan.half, plan.share
    g, l, s = lax.axis_index("gene"), lax.axis_index("lat"), lax.axis_index("sub")
    owner, slab = g // plan.split, lax.rem(g, plan.split)
    me = l * subs + s

    def at(dg=0, dl=0, ds=0):
        return {"gene": lax.rem(g + dg, genes), "lat": lax.rem(l + dl, lats), "sub": lax.rem(s + ds, subs)}

    def send(src, dst, sems, k, device):
        return pltpu.make_async_remote_copy(
            src_ref=src,
            dst_ref=dst,
            send_sem=sems.at[(0, *k)],
            recv_sem=sems.at[(1, *k)],
            device_id=device,
            device_id_type=pl.DeviceIdType.MESH,
        )

    def drain(sems, k, sent, got):
        if sent is not None:
            pltpu.make_async_copy(sent, sent, sems.at[(0, *k)]).wait()
        pltpu.make_async_copy(got, got, sems.at[(1, *k)]).wait()

    if plan.sliced:
        points_src, weight_src = points_hbm, weight_hbm
    else:
        mine = pl.ds(pl.multiple_of(owner * share, 8), share)
        cut = pl.ds(pl.multiple_of(slab * plan.points, 128), plan.points)
        points_src, weight_src = points_hbm.at[:, mine, cut], weight_hbm.at[mine, cut]
    loads = [
        pltpu.make_async_copy(points_src, points_ref, load_sem.at[0]),
        pltpu.make_async_copy(weight_src, weight_ref, load_sem.at[1]),
        pltpu.make_async_copy(expr_hbm, expr_ref, load_sem.at[2]),
        pltpu.make_async_copy(mixing_hbm, mixing_ref, load_sem.at[3]),
        pltpu.make_async_copy(noise_hbm, noise_ref, load_sem.at[4]),
    ]
    small = [
        pltpu.make_async_copy(index_hbm, index_ref, load_sem.at[5]),
        pltpu.make_async_copy(coords_hbm, coords_ref, load_sem.at[6]),
        pltpu.make_async_copy(length_hbm, length_ref, load_sem.at[7]),
        pltpu.make_async_copy(height_hbm, height_ref, load_sem.at[8]),
    ]
    for load in small + loads[:2]:
        load.start()

    far = [(dg, dl, 0) for dg in range(genes) for dl in range(lats) if dg or dl]
    flat = [(0, dl, ds) for dl in range(lats) for ds in range(subs) if dl or ds]
    peers = sorted(set(far) | set(flat))
    barrier = pltpu.get_barrier_semaphore()
    for peer in peers:
        pl.semaphore_signal(barrier, inc=1, device_id=at(*peer), device_id_type=pl.DeviceIdType.MESH)

    for load in small:
        load.wait()
    pick = lax.broadcasted_iota(jnp.int32, (plan.table, rows), 0) == index_ref[...]
    pick_ref[...] = pick.astype(F32).astype(BF16)
    local = jnp.zeros((2, rows), F32)
    for piece in pieces(coords_ref[...]):
        local = local + jnp.dot(piece.astype(BF16), pick_ref[...], preferred_element_type=F32)
    xy_ref[me] = local
    side_ref[...] = jnp.zeros_like(side_ref)
    side_ref[18:21, :] = jnp.ones((3, rows), F32)
    cell_features(plan, me, xy_ref, side_ref, feat_ref)

    lane = lax.broadcasted_iota(jnp.int32, (share, plan.lats), 1)
    chosen = lane == lax.broadcasted_iota(jnp.int32, (share, plan.lats), 0) + owner * share
    length = jnp.sum(jnp.where(chosen, length_ref[...], 0.0), axis=1, keepdims=True)
    height = jnp.sum(jnp.where(chosen, height_ref[...], 0.0), axis=1, keepdims=True)
    loads[0].wait()
    loads[1].wait()
    for load in loads[2:]:
        load.start()
    point_features(plan, (0.5 * LOG2E) / (length * length), points_ref, weight_ref, table_ref)

    def ring(k):
        return lax.rem(me + k, blocks)

    def flush(part):
        lane = lax.broadcasted_iota(jnp.int32, (half, 128), 1)
        for k in range(blocks):
            sums = jnp.zeros((half, 128), F32)
            for j in range(share):
                column = jnp.sum(total_ref[j, 2 * k + part], axis=1, keepdims=True)
                sums = jnp.where(lane == j, column, sums)
            part_ref[part, lax.rem(ring(k), subs), ring(k) // subs] = sums.T[:share, :]
        start(near_copies(part))

    def forward(units, stages=(), low=0, high=share, step=1):
        step = math.gcd(step, high - low) if high > low else 1

        def products(i, carry):
            for when, stage in stages:
                pl.when(i == (when - low) // step)(stage)
            for j in [low + i * step + d for d in range(step)]:
                for k, part in units:
                    place = pl.multiple_of(ring(k) * rows + part * half, half)
                    feat = feat_ref[pl.ds(place, half), :]
                    total = jnp.zeros((half, 128), F32)
                    for start in range(0, plan.points, plan.tile):
                        cols = slice(start, start + plan.tile)
                        value = jnp.exp2(
                            jnp.dot(feat, table_ref[j, :, cols].astype(BF16), preferred_element_type=F32)
                        )
                        if part == 1 and start // plan.tile < plan.cached:
                            cache_ref[j, k, start // plan.tile] = value
                        for first in range(0, plan.tile, 128):
                            w = table_ref[j, SPARE : SPARE + 1, start + first : start + first + 128]
                            total = total + value[:, first : first + 128] * w
                    total_ref[j, 2 * k + part] = total
            return carry

        lax.fori_loop(0, (high - low) // step, products, 0)

    def when(k):
        return k * share // 8

    forward([(0, 0)], step=4)

    pl.semaphore_wait(barrier, len(peers))
    for peer in flat:
        send(xy_ref.at[me], xy_ref.at[me], xy_sem, (), at(*peer)).start()
    forward([(0, 1)], high=when(4), step=4)
    for load in loads[2:]:
        load.wait()
    gene_tiles = [slice(first, first + plan.wide) for first in range(0, plan.genes, plan.wide)]
    for cols in gene_tiles:
        seen = lax.dot_general(
            pick_ref[...], expr_ref[:, cols], (((0,), (0,)), ((), ())), preferred_element_type=F32
        )
        seen_ref[:, cols] = seen.astype(BF16)
    if flat:
        others = xy_ref.at[pl.ds(0, blocks - 1)]
        drain(xy_sem, (), others, others)
    for k in range(1, blocks):
        cell_features(plan, ring(k), xy_ref, side_ref, feat_ref)

    def near_copies(part):
        return [
            send(part_ref.at[part, lax.rem(s + ds, subs)], near_ref.at[part, ds - 1], near_sem, (part, ds - 1), at(ds=ds))
            for ds in range(1, subs)
        ]

    def latent_copies(part):
        out = []
        for peer in far:
            target = at(*peer)
            out.append(
                send(final_ref.at[part, target["lat"]], latent_recv.at[part, g, l], latent_sem, (part,), target)
            )
        return out

    def rs_copies(part):
        out = []
        for dg in range(1, genes):
            target = at(dg=dg)
            source = chunk_ref.at[part, target["gene"] // plan.split]
            out.append(send(source, rs_ref.at[part, dg - 1], rs_sem, (part,), target))
        return out

    def lg_copies(part):
        out = []
        for peer in flat:
            target = at(*peer)
            out.append(send(own_ref.at[part, target["lat"]], lg_ref.at[part, me], lg_sem, (part,), target))
        return out

    def start(copies):
        for copy in copies:
            copy.start()

    def wait(copies):
        for copy in copies:
            copy.wait()

    def sum_near(part):
        wait(near_copies(part))
        value = part_ref[part, s]
        for ds in range(1, subs):
            value = value + near_ref[part, ds - 1]
        value = value * height[None]
        final_ref[part] = value.astype(final_ref.dtype)
        start(latent_copies(part))
        pltpu.make_async_copy(final_ref.at[part, l], latent_recv.at[part, g, l], latent_sem.at[1, part]).start()

    def middle(part):
        drain(latent_sem, (part,), far_ref if far else None, latent_recv.at[part])
        for lat in range(lats):
            for own in range(plan.owners):
                first = own * plan.split
                value = latent_recv[part, first, lat].astype(F32)
                for other in range(1, plan.split):
                    value = value + latent_recv[part, first + other, lat].astype(F32)
                base = lat * plan.lats + own * share
                side_lat_ref[base : base + share, :] = value
        cells = slice(part * half, (part + 1) * half)
        latent_ref[:, cells] = side_lat_ref[...].astype(BF16)
        turned = side_lat_ref[...].T.astype(BF16)
        cell = jnp.zeros((plan.total, half), F32)
        for cols in gene_tiles:
            mixing = mixing_ref[:, cols]
            predicted = jnp.dot(turned, mixing, preferred_element_type=F32)
            weighted = (noise_ref[:, cols] * (seen_ref[cells, cols].astype(F32) - predicted)).astype(BF16)
            seen_ref[cells, cols] = weighted
            cell = cell + lax.dot_general(
                mixing, weighted, (((1,), (1,)), ((), ())), preferred_element_type=F32
            )
        cell_ref[...] = cell
        for own in range(plan.owners):
            for lat in range(lats):
                base = lat * plan.lats + own * share
                chunk_ref[part, own, lat] = plan.scale * cell_ref[base : base + share, :]
        start(rs_copies(part))

    def sum_gene(part):
        if genes > 1:
            drain(rs_sem, (part,), rs_ref.at[part], rs_ref.at[part])
        value = chunk_ref[part, owner]
        for dg in range(1, genes):
            value = value + rs_ref[part, dg - 1]
        own_ref[part] = value
        start(lg_copies(part))
        pltpu.make_async_copy(own_ref.at[part, l], lg_ref.at[part, me], lg_sem.at[1, part]).start()

    def turn(part):
        drain(lg_sem, (part,), lg_ref.at[part, pl.ds(0, blocks - 1)] if flat else None, lg_ref.at[part])
        for block in range(blocks):
            for p, piece in enumerate(pieces(lg_ref[part, block] * height)):
                lgside_ref[p * share : (p + 1) * share, :] = piece
            lgt_ref[block * half : (block + 1) * half, :] = (
                lgside_ref[...].T[:, : plan.turned].astype(BF16)
            )

    def mix_near_copies():
        return [
            send(mix_ref.at[lax.rem(s + ds, subs)], mix_near.at[ds - 1], mix_sem, (0, ds - 1, 0), at(ds=ds))
            for ds in range(1, subs)
        ]

    def mix_lat_copies(p):
        return [send(mix_all.at[l, p], mix_all.at[l, p], mix_sem, (1, dl - 1, p), at(dl=dl)) for dl in range(1, lats)]

    def mix_back_copies(p):
        return [send(mix_sum.at[p], mix_out.at[s, p], mix_sem, (2, ds - 1, p), at(ds=ds)) for ds in range(1, subs)]

    def mix_keep(p):
        return pltpu.make_async_copy(mix_sum.at[p], mix_out.at[s, p], keep_sem.at[p])

    def mix_part():
        depth = mix_ref.shape[2]
        for cols in gene_tiles:
            value = plan.scale * jnp.dot(latent_ref[...], seen_ref[:, cols], preferred_element_type=F32)
            for sub in range(subs):
                for p in range(lats):
                    base = (sub * lats + p) * depth
                    mix_ref[sub, p, :, cols] = value[base : base + depth, :]
        start(mix_near_copies())

    def mix_sub():
        wait(mix_near_copies())
        for p in range(lats):
            value = mix_ref[s, p]
            for ds in range(1, subs):
                value = value + mix_near[ds - 1, p]
            mix_all[l, p] = code(value)
            start(mix_lat_copies(p))

    def mix_lat(p):
        wait(mix_lat_copies(p))
        value = decode(mix_all[0, p])
        for lat in range(1, lats):
            value = value + decode(mix_all[lat, p])
        mix_sum[p] = value
        start(mix_back_copies(p))
        mix_keep(p).start()

    def gather_copies(j):
        return [
            send(all_ref.at[j], all_out.at[g, j], all_sem, (), at(dg=dg)) for dg in range(1, genes)
        ] + [pltpu.make_async_copy(all_ref.at[j], all_out.at[g, j], all_sem.at[1])]

    def backward(part, stages):
        def step(j, carry):
            for when, stage in stages:
                pl.when(j == when)(stage)
            row = lax.broadcasted_iota(jnp.int32, (plan.turned, 128), 0)
            select = (lax.rem(row, share) == j).astype(F32).astype(BF16)
            for k in range(blocks):
                place = pl.multiple_of(ring(k) * half, half)
                turned = lgt_ref[pl.ds(place, half), :]
                wide_ref[k] = jnp.dot(turned, select, preferred_element_type=F32)
            tiles = list(range(plan.points // plan.tile))
            kept = tiles[: plan.cached] if part == 1 else []
            fresh = tiles[len(kept) :]
            lanes = plan.tile // 128
            held = [(t, f) for t in kept for f in range(lanes)]
            held_sums = [None] * len(held)
            packs = [range(i, min(i + PACK, len(held))) for i in range(0, len(held), PACK)]
            groups = [(pack, k, r) for pack in packs for k in range(blocks) for r in range(0, half, 8)]
            steps = len(fresh) * blocks
            pace = -(-len(groups) // max(1, steps))

            def settle(sums, t, f):
                r = t * lanes + f
                here = slice(r * 128, (r + 1) * 128)
                if part == 0:
                    sum_ref[j, :, here] = sums
                else:
                    row_ref[r : r + 1, :] = jnp.sum(sum_ref[j, :, here] + sums, axis=0, keepdims=True)

            def spend(groups):
                for pack, k, r in groups:
                    wide = wide_ref[k, r : r + 8, :]
                    for i in pack:
                        t, f = held[i]
                        term = cache_ref[j, k, t, r : r + 8, f * 128 : (f + 1) * 128] * wide
                        held_sums[i] = term if held_sums[i] is None else held_sums[i] + term

            for t in fresh:
                points = table_ref[j, :, t * plan.tile : (t + 1) * plan.tile].astype(BF16)
                sums = [None] * lanes
                for k in range(blocks):
                    place = pl.multiple_of(ring(k) * rows + part * half, half)
                    value = jnp.exp2(
                        jnp.dot(feat_ref[pl.ds(place, half), :], points, preferred_element_type=F32)
                    )
                    for f in range(lanes):
                        term = value[:, f * 128 : (f + 1) * 128] * wide_ref[k]
                        term = jnp.sum(term.reshape(half // 8, 8, 128), axis=0)
                        sums[f] = term if sums[f] is None else sums[f] + term
                    spend(groups[:pace])
                    groups = groups[pace:]
                for f in range(lanes):
                    settle(sums[f], t, f)
            spend(groups)
            for (t, f), sums in zip(held, held_sums):
                settle(sums, t, f)
            if part == 1:
                all_ref[j] = code(row_ref[...])
                start(gather_copies(j))
            return carry

        lax.fori_loop(0, share, step, 0)

    forward([(k, 0) for k in range(1, blocks)], step=2)
    flush(0)
    forward([(0, 1)], low=when(4), high=when(6), step=2)
    sum_near(0)
    forward([(0, 1)], low=when(6), step=2)
    forward(
        [(k, 1) for k in range(1, blocks)],
        [(when(3), lambda: middle(0)), (when(7), lambda: sum_gene(0))],
    )
    flush(1)
    lgside_ref[...] = jnp.zeros_like(lgside_ref)
    turn(0)
    backward(
        0,
        [
            (when(0), lambda: sum_near(1)),
            (when(3), lambda: middle(1)),
            (when(3), mix_part),
            (when(5), lambda: sum_gene(1)),
            (when(5), mix_sub),
        ],
    )
    turn(1)
    early = max(1, lats // 2)

    def first_parts():
        for p in range(early):
            mix_lat(p)

    backward(1, [(when(6), first_parts)])
    for p in range(early, lats):
        mix_lat(p)

    drain(all_sem, (), all_out.at[pl.ds(0, genes - 1)] if genes > 1 else None, all_out)
    for p in range(lats):
        wait(mix_back_copies(p))
        mix_keep(p).wait()


def lay_body(plan, mix_hbm, all_hbm, mix_out, ind_out, mix_ref, all_ref, row_ref, ind_ref, in_sem, out_sem):
    codes = pltpu.make_async_copy(all_hbm, all_ref, in_sem.at[0])
    mix_in = pltpu.make_async_copy(mix_hbm, mix_ref, in_sem.at[1])
    mix_back = pltpu.make_async_copy(mix_ref, mix_out, out_sem.at[1])
    codes.start()
    mix_in.start()
    codes.wait()
    for owner in range(plan.owners):
        base = owner * plan.share
        for slab in range(plan.split):
            gene = owner * plan.split + slab
            for j in range(plan.share):
                row_ref[gene, j] = decode(all_ref[gene, j])
            for r in range(plan.points // 128):
                first = slab * plan.points + r * 128
                ind_ref[base : base + plan.share, first : first + 128] = row_ref[gene, :, r, :]
    ind_back = pltpu.make_async_copy(ind_ref, ind_out, out_sem.at[0])
    ind_back.start()
    mix_in.wait()
    mix_back.start()
    ind_back.wait()
    mix_back.wait()


def lay(plan, mix, codes):
    anywhere = pl.BlockSpec(memory_space=pl.ANY)
    return pl.pallas_call(
        functools.partial(lay_body, plan),
        in_specs=[anywhere] * 2,
        out_specs=[anywhere] * 2,
        out_shape=[
            jax.ShapeDtypeStruct(mix.shape, F32),
            jax.ShapeDtypeStruct((plan.lats, plan.count), F32),
        ],
        scratch_shapes=[
            pltpu.VMEM(mix.shape, F32),
            pltpu.VMEM(codes.shape, jnp.int16),
            pltpu.VMEM((plan.gene, plan.share, plan.points // 128, 128), F32),
            pltpu.VMEM((plan.lats, plan.count), F32),
            pltpu.SemaphoreType.DMA((2,)),
            pltpu.SemaphoreType.DMA((2,)),
        ],
        compiler_params=pltpu.CompilerParams(vmem_limit_bytes=60 * 2**20),
    )(mix, codes)


def fused(plan, *args):
    genes, lats, subs = plan.gene, plan.lat, plan.sub
    rows, half, share, blocks = plan.rows, plan.half, plan.share, plan.blocks
    depth = plan.total // (lats * subs)
    sent = BF16 if plan.split == 1 else F32
    dma = pltpu.SemaphoreType.DMA
    far = genes * lats - 1
    flat = blocks - 1
    anywhere = pl.BlockSpec(memory_space=pl.ANY)
    scratch = [
        pltpu.VMEM((1, rows), jnp.int32),
        pltpu.VMEM((2, plan.table), F32),
        pltpu.VMEM((1, plan.lats), F32),
        pltpu.VMEM((1, plan.lats), F32),
        pltpu.VMEM((plan.table, plan.genes), BF16),
        pltpu.VMEM((2, share, plan.points), F32),
        pltpu.VMEM((share, plan.points), F32),
        pltpu.VMEM((plan.total, plan.genes), BF16),
        pltpu.VMEM((1, plan.genes), F32),
        pltpu.VMEM((plan.table, rows), BF16),
        pltpu.VMEM((blocks, 2, rows), F32),
        pltpu.VMEM((128, rows), F32),
        pltpu.VMEM((blocks * rows, DEPTH), BF16),
        pltpu.VMEM((share, DEPTH, plan.points), F32),
        pltpu.VMEM((share, 2 * blocks, half, 128), F32),
        pltpu.VMEM((2, subs, lats, share, half), F32),
        pltpu.VMEM((2, max(1, subs - 1), lats, share, half), F32),
        pltpu.VMEM((2, lats, share, half), sent),
        pltpu.VMEM((2, genes, lats, share, half), sent),
        pltpu.VMEM((plan.total, rows), BF16),
        pltpu.VMEM((plan.total, half), F32),
        pltpu.VMEM((rows, plan.genes), BF16),
        pltpu.VMEM((plan.total, half), F32),
        pltpu.VMEM((2, plan.owners, lats, share, half), F32),
        pltpu.VMEM((2, max(1, genes - 1), lats, share, half), F32),
        pltpu.VMEM((2, lats, share, half), F32),
        pltpu.VMEM((2, blocks, share, half), F32),
        pltpu.VMEM((128, half), F32),
        pltpu.VMEM((blocks * half, plan.turned), BF16),
        pltpu.VMEM((blocks, half, 128), F32),
        pltpu.VMEM((subs, lats, depth, plan.genes), F32),
        pltpu.VMEM((max(1, subs - 1), lats, depth, plan.genes), F32),
        pltpu.VMEM((lats, lats, depth, plan.genes), jnp.int16),
        pltpu.VMEM((lats, depth, plan.genes), F32),
        pltpu.VMEM((share, 8, plan.points), F32),
        pltpu.VMEM((plan.points // 128, 128), F32),
        pltpu.VMEM((share, plan.points // 128, 128), jnp.int16),
        pltpu.VMEM((share, blocks, max(1, plan.cached), half, plan.tile), F32),
        pltpu.VMEM((max(1, far), share, half), sent),
        dma((9,)),
        dma((2,)),
        dma((2, 2, max(1, subs - 1))),
        dma((2, 2)),
        dma((2, 2)),
        dma((2, 2)),
        dma((2, 3, max(1, subs - 1, lats - 1), lats)),
        dma((2,)),
        dma((lats,)),
    ]
    return pl.pallas_call(
        functools.partial(body, plan),
        in_specs=[anywhere] * 9,
        out_specs=[anywhere] * 2,
        out_shape=[
            jax.ShapeDtypeStruct((subs, lats, depth, plan.genes), F32),
            jax.ShapeDtypeStruct((genes, share, plan.points // 128, 128), jnp.int16),
        ],
        scratch_shapes=scratch,
        compiler_params=pltpu.CompilerParams(
            collective_id=0, has_side_effects=True, vmem_limit_bytes=67043328
        ),
    )(*args)


def on_device(
    cell_index,
    coords_table,
    expr_table,
    inducing,
    ind_weights,
    lengthscale,
    variance,
    mixing,
    noise_prec,
):
    genes, lats, subs = (lax.axis_size(axis) for axis in ("gene", "lat", "sub"))
    latents, count = ind_weights.shape
    owners = math.gcd(genes, latents)
    split = genes // owners
    share = latents // owners
    plan = Plan(
        gene=genes,
        lat=lats,
        sub=subs,
        rows=cell_index.shape[0],
        table=coords_table.shape[1],
        lats=latents,
        count=count,
        genes=expr_table.shape[1],
        share=share,
        split=split,
        sliced=share % 8 != 0,
        scale=-1.0 / math.sqrt(cell_index.shape[0] * lats * subs),
    )
    if plan.sliced:
        place = lax.axis_index("gene")
        first, cut = place // split * share, lax.rem(place, split) * plan.points
        inducing = lax.dynamic_slice(inducing, (0, first, cut), (2, share, plan.points))
        ind_weights = lax.dynamic_slice(ind_weights, (first, cut), (share, plan.points))
    mix, codes = fused(
        plan,
        cell_index[None, :],
        coords_table,
        lengthscale[None, :],
        variance[None, :],
        expr_table,
        inducing,
        ind_weights,
        mixing,
        noise_prec[None, :],
    )
    grad_mixing, grad_inducing = lay(plan, mix, codes)
    return grad_mixing.reshape(mixing.shape), grad_inducing


def solution(mesh):
    in_specs = (
        P(("group", "lat", "sub")),
        P("group", ("lat", "sub")),
        P(("group", "lat", "sub"), "gene"),
        P("group", "lat", "sub"),
        P(("group", "lat"), "sub"),
        P(("group", "lat")),
        P(("group", "lat")),
        P("group", "gene"),
        P(("group", "gene")),
    )
    out_specs = (P("group", "gene"), P(("group", "lat"), "sub"))
    return jax.shard_map(
        on_device, mesh=mesh, in_specs=in_specs, out_specs=out_specs, check_vma=False
    )
```

```python
import functools
import math
from typing import NamedTuple

import jax
import jax.numpy as jnp
from jax import lax
from jax.experimental import pallas as pl
from jax.experimental.pallas import tpu as pltpu
from jax.sharding import PartitionSpec as P

F32 = jnp.float32
BF16 = jnp.bfloat16
DEPTH = 24
SPARE = 21
CENTER = 0.5
LOG2E = math.log2(math.e)
PACK = 20
CACHE = 44 * 2**20
LEFT = (0, 0, 1, 1, 0, 2)
RIGHT = (0, 1, 0, 1, 2, 0)


class Plan(NamedTuple):
    gene: int
    lat: int
    sub: int
    rows: int
    table: int
    lats: int
    count: int
    genes: int
    share: int
    split: int
    sliced: bool
    scale: float

    @property
    def blocks(self):
        return self.lat * self.sub

    @property
    def points(self):
        return self.count // self.split

    @property
    def owners(self):
        return self.gene // self.split

    @property
    def total(self):
        return self.lat * self.lats

    @property
    def half(self):
        return self.rows // 2

    @property
    def turned(self):
        return -(-3 * self.share // 8) * 8

    @property
    def tile(self):
        return min(256, self.points)

    @property
    def cached(self):
        return min(self.points // self.tile, CACHE // (self.share * self.blocks * self.half * self.tile * 4))

    @property
    def wide(self):
        return min(512, self.genes)


BIAS = 128
LEAST = 2.0**-120


def bit_rows(shape):
    row = lax.broadcasted_iota(jnp.int32, shape, 0)
    return row, row < 8


def code(value):
    top = jnp.maximum(jnp.max(jnp.abs(value), axis=0, keepdims=True), LEAST)
    power = jnp.floor(jnp.log(top) * LOG2E + 1e-5) + 1.0
    row, marked = bit_rows(value.shape)
    scaled = value * jnp.exp2(15.0 - power)
    fine = jnp.clip(jnp.floor(scaled + 0.5), -32767.0, 32767.0).astype(jnp.int32)
    coarse = jnp.clip(jnp.floor(scaled * 0.5 + 0.5), -16383.0, 16383.0).astype(jnp.int32) * 2
    place = jnp.where(marked, row, 0)
    bit = jnp.bitwise_and(jnp.right_shift(power.astype(jnp.int32) + BIAS, place), 1)
    return jnp.where(marked, coarse + bit, fine).astype(jnp.int16)


def decode(codes):
    codes = codes.astype(jnp.int32)
    row, marked = bit_rows(codes.shape)
    bit = jnp.where(marked, jnp.bitwise_and(codes, 1), 0)
    weight = jnp.left_shift(bit, jnp.where(marked, row, 0)).astype(F32)
    power = jnp.sum(weight, axis=0, keepdims=True) - float(BIAS)
    return (codes - bit).astype(F32) * jnp.exp2(power - 15.0)


def pieces(value):
    high = value.astype(BF16).astype(F32)
    rest = value - high
    middle = rest.astype(BF16).astype(F32)
    low = (rest - middle).astype(BF16).astype(F32)
    return high, middle, low


def point_features(plan, scale, points_ref, weight_ref, table_ref):
    step = min(512, plan.points)

    def part(i, carry):
        cols = pl.ds(pl.multiple_of(i * step, 128), step)
        x = points_ref[0, :, cols] - CENTER
        y = points_ref[1, :, cols] - CENTER
        px = pieces(x * (2.0 * scale))
        py = pieces(y * (2.0 * scale))
        ps = pieces(jnp.broadcast_to(-scale, x.shape))
        pn = pieces((x * x + y * y) * -scale)
        rows = [px[k] for k in RIGHT] + [py[k] for k in RIGHT] + [ps[k] for k in RIGHT]
        rows += list(pn) + [weight_ref[:, cols]] + [jnp.zeros_like(x)] * (DEPTH - SPARE - 1)
        for place, row in enumerate(rows):
            for lane in range(plan.share):
                table_ref[lane, place : place + 1, cols] = row[lane : lane + 1, :]
        return carry

    lax.fori_loop(0, plan.points // step, part, 0)


def cell_features(plan, block, xy_ref, side_ref, feat_ref):
    x = xy_ref[block, 0:1, :] - CENTER
    y = xy_ref[block, 1:2, :] - CENTER
    px, py, pn = pieces(x), pieces(y), pieces(x * x + y * y)
    rows = [px[k] for k in LEFT] + [py[k] for k in LEFT] + [pn[k] for k in LEFT]
    for place, row in enumerate(rows):
        side_ref[place : place + 1, :] = row
    place = pl.ds(pl.multiple_of(block * plan.rows, plan.rows), plan.rows)
    feat_ref[place, :] = side_ref[...].T[:, :DEPTH].astype(BF16)


def body(
    plan,
    index_hbm,
    coords_hbm,
    length_hbm,
    height_hbm,
    expr_hbm,
    points_hbm,
    weight_hbm,
    mixing_hbm,
    noise_hbm,
    mix_out,
    all_out,
    index_ref,
    coords_ref,
    length_ref,
    height_ref,
    expr_ref,
    points_ref,
    weight_ref,
    mixing_ref,
    noise_ref,
    pick_ref,
    xy_ref,
    side_ref,
    feat_ref,
    table_ref,
    total_ref,
    part_ref,
    near_ref,
    final_ref,
    latent_recv,
    latent_ref,
    side_lat_ref,
    seen_ref,
    cell_ref,
    chunk_ref,
    rs_ref,
    own_ref,
    lg_ref,
    lgside_ref,
    lgt_ref,
    wide_ref,
    mix_ref,
    mix_near,
    mix_all,
    mix_sum,
    sum_ref,
    row_ref,
    all_ref,
    cache_ref,
    far_ref,
    load_sem,
    xy_sem,
    near_sem,
    latent_sem,
    rs_sem,
    lg_sem,
    mix_sem,
    all_sem,
    keep_sem,
):
    genes, lats, subs, blocks = plan.gene, plan.lat, plan.sub, plan.blocks
    rows, half, share = plan.rows, plan.half, plan.share
    g, l, s = lax.axis_index("gene"), lax.axis_index("lat"), lax.axis_index("sub")
    owner, slab = g // plan.split, lax.rem(g, plan.split)
    me = l * subs + s

    def at(dg=0, dl=0, ds=0):
        return {"gene": lax.rem(g + dg, genes), "lat": lax.rem(l + dl, lats), "sub": lax.rem(s + ds, subs)}

    def send(src, dst, sems, k, device):
        return pltpu.make_async_remote_copy(
            src_ref=src,
            dst_ref=dst,
            send_sem=sems.at[(0, *k)],
            recv_sem=sems.at[(1, *k)],
            device_id=device,
            device_id_type=pl.DeviceIdType.MESH,
        )

    def drain(sems, k, sent, got):
        if sent is not None:
            pltpu.make_async_copy(sent, sent, sems.at[(0, *k)]).wait()
        pltpu.make_async_copy(got, got, sems.at[(1, *k)]).wait()

    if plan.sliced:
        points_src, weight_src = points_hbm, weight_hbm
    else:
        mine = pl.ds(pl.multiple_of(owner * share, 8), share)
        cut = pl.ds(pl.multiple_of(slab * plan.points, 128), plan.points)
        points_src, weight_src = points_hbm.at[:, mine, cut], weight_hbm.at[mine, cut]
    loads = [
        pltpu.make_async_copy(points_src, points_ref, load_sem.at[0]),
        pltpu.make_async_copy(weight_src, weight_ref, load_sem.at[1]),
        pltpu.make_async_copy(expr_hbm, expr_ref, load_sem.at[2]),
        pltpu.make_async_copy(mixing_hbm, mixing_ref, load_sem.at[3]),
        pltpu.make_async_copy(noise_hbm, noise_ref, load_sem.at[4]),
    ]
    small = [
        pltpu.make_async_copy(index_hbm, index_ref, load_sem.at[5]),
        pltpu.make_async_copy(coords_hbm, coords_ref, load_sem.at[6]),
        pltpu.make_async_copy(length_hbm, length_ref, load_sem.at[7]),
        pltpu.make_async_copy(height_hbm, height_ref, load_sem.at[8]),
    ]
    for load in small + loads[:2]:
        load.start()

    far = [(dg, dl, 0) for dg in range(genes) for dl in range(lats) if dg or dl]
    flat = [(0, dl, ds) for dl in range(lats) for ds in range(subs) if dl or ds]
    peers = sorted(set(far) | set(flat))
    barrier = pltpu.get_barrier_semaphore()
    for peer in peers:
        pl.semaphore_signal(barrier, inc=1, device_id=at(*peer), device_id_type=pl.DeviceIdType.MESH)

    for load in small:
        load.wait()
    pick = lax.broadcasted_iota(jnp.int32, (plan.table, rows), 0) == index_ref[...]
    pick_ref[...] = pick.astype(F32).astype(BF16)
    local = jnp.zeros((2, rows), F32)
    for piece in pieces(coords_ref[...]):
        local = local + jnp.dot(piece.astype(BF16), pick_ref[...], preferred_element_type=F32)
    xy_ref[me] = local
    side_ref[...] = jnp.zeros_like(side_ref)
    side_ref[18:21, :] = jnp.ones((3, rows), F32)
    cell_features(plan, me, xy_ref, side_ref, feat_ref)

    lane = lax.broadcasted_iota(jnp.int32, (share, plan.lats), 1)
    chosen = lane == lax.broadcasted_iota(jnp.int32, (share, plan.lats), 0) + owner * share
    length = jnp.sum(jnp.where(chosen, length_ref[...], 0.0), axis=1, keepdims=True)
    height = jnp.sum(jnp.where(chosen, height_ref[...], 0.0), axis=1, keepdims=True)
    loads[0].wait()
    loads[1].wait()
    for load in loads[2:]:
        load.start()
    point_features(plan, (0.5 * LOG2E) / (length * length), points_ref, weight_ref, table_ref)

    def ring(k):
        return lax.rem(me + k, blocks)

    def flush(part):
        for k in range(blocks):
            for j in range(share):
                row = jnp.sum(total_ref[j, 2 * k + part].T, axis=0, keepdims=True)
                part_ref[part, lax.rem(ring(k), subs), ring(k) // subs, j : j + 1, :] = row
        start(near_copies(part))

    def forward(units, stages=(), low=0, high=share, step=1):
        step = math.gcd(step, high - low) if high > low else 1

        def products(i, carry):
            for when, stage in stages:
                pl.when(i == (when - low) // step)(stage)
            for j in [low + i * step + d for d in range(step)]:
                for k, part in units:
                    place = pl.multiple_of(ring(k) * rows + part * half, half)
                    feat = feat_ref[pl.ds(place, half), :]
                    total = jnp.zeros((half, 128), F32)
                    for start in range(0, plan.points, plan.tile):
                        cols = slice(start, start + plan.tile)
                        value = jnp.exp2(
                            jnp.dot(feat, table_ref[j, :, cols].astype(BF16), preferred_element_type=F32)
                        )
                        if part == 1 and start // plan.tile < plan.cached:
                            cache_ref[j, k, start // plan.tile] = value
                        for first in range(0, plan.tile, 128):
                            w = table_ref[j, SPARE : SPARE + 1, start + first : start + first + 128]
                            total = total + value[:, first : first + 128] * w
                    total_ref[j, 2 * k + part] = total
            return carry

        lax.fori_loop(0, (high - low) // step, products, 0)

    def when(k):
        return k * share // 8

    forward([(0, 0)], step=4)

    pl.semaphore_wait(barrier, len(peers))
    for peer in flat:
        send(xy_ref.at[me], xy_ref.at[me], xy_sem, (), at(*peer)).start()
    forward([(0, 1)], high=when(4), step=4)
    for load in loads[2:]:
        load.wait()
    gene_tiles = [slice(first, first + plan.wide) for first in range(0, plan.genes, plan.wide)]
    for cols in gene_tiles:
        seen = lax.dot_general(
            pick_ref[...], expr_ref[:, cols], (((0,), (0,)), ((), ())), preferred_element_type=F32
        )
        seen_ref[:, cols] = seen.astype(BF16)
    if flat:
        others = xy_ref.at[pl.ds(0, blocks - 1)]
        drain(xy_sem, (), others, others)
    for k in range(1, blocks):
        cell_features(plan, ring(k), xy_ref, side_ref, feat_ref)

    def near_copies(part):
        return [
            send(part_ref.at[part, lax.rem(s + ds, subs)], near_ref.at[part, ds - 1], near_sem, (part, ds - 1), at(ds=ds))
            for ds in range(1, subs)
        ]

    def latent_copies(part):
        out = []
        for peer in far:
            target = at(*peer)
            out.append(
                send(final_ref.at[part, target["lat"]], latent_recv.at[part, g, l], latent_sem, (part,), target)
            )
        return out

    def rs_copies(part):
        out = []
        for dg in range(1, genes):
            target = at(dg=dg)
            source = chunk_ref.at[part, target["gene"] // plan.split]
            out.append(send(source, rs_ref.at[part, dg - 1], rs_sem, (part,), target))
        return out

    def lg_copies(part):
        out = []
        for peer in flat:
            target = at(*peer)
            out.append(send(own_ref.at[part, target["lat"]], lg_ref.at[part, me], lg_sem, (part,), target))
        return out

    def start(copies):
        for copy in copies:
            copy.start()

    def wait(copies):
        for copy in copies:
            copy.wait()

    def sum_near(part):
        wait(near_copies(part))
        value = part_ref[part, s]
        for ds in range(1, subs):
            value = value + near_ref[part, ds - 1]
        value = value * height[None]
        final_ref[part] = value.astype(final_ref.dtype)
        start(latent_copies(part))
        pltpu.make_async_copy(final_ref.at[part, l], latent_recv.at[part, g, l], latent_sem.at[1, part]).start()

    def middle(part):
        drain(latent_sem, (part,), far_ref if far else None, latent_recv.at[part])
        for lat in range(lats):
            for own in range(plan.owners):
                first = own * plan.split
                value = latent_recv[part, first, lat].astype(F32)
                for other in range(1, plan.split):
                    value = value + latent_recv[part, first + other, lat].astype(F32)
                base = lat * plan.lats + own * share
                side_lat_ref[base : base + share, :] = value
        cells = slice(part * half, (part + 1) * half)
        latent_ref[:, cells] = side_lat_ref[...].astype(BF16)
        turned = side_lat_ref[...].T.astype(BF16)
        cell = jnp.zeros((plan.total, half), F32)
        for cols in gene_tiles:
            mixing = mixing_ref[:, cols]
            predicted = jnp.dot(turned, mixing, preferred_element_type=F32)
            weighted = (noise_ref[:, cols] * (seen_ref[cells, cols].astype(F32) - predicted)).astype(BF16)
            seen_ref[cells, cols] = weighted
            cell = cell + lax.dot_general(
                mixing, weighted, (((1,), (1,)), ((), ())), preferred_element_type=F32
            )
        cell_ref[...] = cell
        for own in range(plan.owners):
            for lat in range(lats):
                base = lat * plan.lats + own * share
                chunk_ref[part, own, lat] = plan.scale * cell_ref[base : base + share, :]
        start(rs_copies(part))

    def sum_gene(part):
        if genes > 1:
            drain(rs_sem, (part,), rs_ref.at[part], rs_ref.at[part])
        value = chunk_ref[part, owner]
        for dg in range(1, genes):
            value = value + rs_ref[part, dg - 1]
        own_ref[part] = value
        start(lg_copies(part))
        pltpu.make_async_copy(own_ref.at[part, l], lg_ref.at[part, me], lg_sem.at[1, part]).start()

    def turn(part):
        drain(lg_sem, (part,), lg_ref.at[part, pl.ds(0, blocks - 1)] if flat else None, lg_ref.at[part])
        for block in range(blocks):
            for p, piece in enumerate(pieces(lg_ref[part, block] * height)):
                lgside_ref[p * share : (p + 1) * share, :] = piece
            lgt_ref[block * half : (block + 1) * half, :] = (
                lgside_ref[...].T[:, : plan.turned].astype(BF16)
            )

    def mix_near_copies():
        return [
            send(mix_ref.at[lax.rem(s + ds, subs)], mix_near.at[ds - 1], mix_sem, (0, ds - 1, 0), at(ds=ds))
            for ds in range(1, subs)
        ]

    def mix_lat_copies(p):
        return [send(mix_all.at[l, p], mix_all.at[l, p], mix_sem, (1, dl - 1, p), at(dl=dl)) for dl in range(1, lats)]

    def mix_back_copies(p):
        return [send(mix_sum.at[p], mix_out.at[s, p], mix_sem, (2, ds - 1, p), at(ds=ds)) for ds in range(1, subs)]

    def mix_keep(p):
        return pltpu.make_async_copy(mix_sum.at[p], mix_out.at[s, p], keep_sem.at[p])

    def mix_part():
        depth = mix_ref.shape[2]
        for cols in gene_tiles:
            value = plan.scale * jnp.dot(latent_ref[...], seen_ref[:, cols], preferred_element_type=F32)
            for sub in range(subs):
                for p in range(lats):
                    base = (sub * lats + p) * depth
                    mix_ref[sub, p, :, cols] = value[base : base + depth, :]
        start(mix_near_copies())

    def mix_sub():
        wait(mix_near_copies())
        for p in range(lats):
            value = mix_ref[s, p]
            for ds in range(1, subs):
                value = value + mix_near[ds - 1, p]
            mix_all[l, p] = code(value)
            start(mix_lat_copies(p))

    def mix_lat(p):
        wait(mix_lat_copies(p))
        value = decode(mix_all[0, p])
        for lat in range(1, lats):
            value = value + decode(mix_all[lat, p])
        mix_sum[p] = value
        start(mix_back_copies(p))
        mix_keep(p).start()

    def gather_copies(j):
        return [
            send(all_ref.at[j], all_out.at[g, j], all_sem, (), at(dg=dg)) for dg in range(1, genes)
        ] + [pltpu.make_async_copy(all_ref.at[j], all_out.at[g, j], all_sem.at[1])]

    def backward(part, stages, step=1):
        step = math.gcd(step, share)

        def products(i, carry):
            for when, stage in stages:
                pl.when(i == when // step)(stage)
            for d in range(step):
                one(i * step + d, d)
            return carry

        def one(j, slot):
            row = lax.broadcasted_iota(jnp.int32, (plan.turned, 128), 0)
            select = (lax.rem(row, share) == j).astype(F32).astype(BF16)
            for k in range(blocks):
                place = pl.multiple_of(ring(k) * half, half)
                turned = lgt_ref[pl.ds(place, half), :]
                wide_ref[slot, k] = jnp.dot(turned, select, preferred_element_type=F32)
            tiles = list(range(plan.points // plan.tile))
            kept = tiles[: plan.cached] if part == 1 else []
            fresh = tiles[len(kept) :]
            lanes = plan.tile // 128
            held = [(t, f) for t in kept for f in range(lanes)]
            held_sums = [None] * len(held)
            packs = [range(i, min(i + PACK, len(held))) for i in range(0, len(held), PACK)]
            groups = [(pack, k, r) for pack in packs for k in range(blocks) for r in range(0, half, 8)]
            steps = len(fresh) * blocks
            pace = -(-len(groups) // max(1, steps))

            def settle(sums, t, f):
                r = t * lanes + f
                here = slice(r * 128, (r + 1) * 128)
                if part == 0:
                    sum_ref[j, :, here] = sums
                else:
                    row_ref[r : r + 1, :] = jnp.sum(sum_ref[j, :, here] + sums, axis=0, keepdims=True)

            def spend(groups):
                for pack, k, r in groups:
                    wide = wide_ref[slot, k, r : r + 8, :]
                    for i in pack:
                        t, f = held[i]
                        term = cache_ref[j, k, t, r : r + 8, f * 128 : (f + 1) * 128] * wide
                        held_sums[i] = term if held_sums[i] is None else held_sums[i] + term

            for t in fresh:
                points = table_ref[j, :, t * plan.tile : (t + 1) * plan.tile].astype(BF16)
                sums = [None] * lanes
                for k in range(blocks):
                    place = pl.multiple_of(ring(k) * rows + part * half, half)
                    value = jnp.exp2(
                        jnp.dot(feat_ref[pl.ds(place, half), :], points, preferred_element_type=F32)
                    )
                    for f in range(lanes):
                        term = value[:, f * 128 : (f + 1) * 128] * wide_ref[slot, k]
                        term = jnp.sum(term.reshape(half // 8, 8, 128), axis=0)
                        sums[f] = term if sums[f] is None else sums[f] + term
                    spend(groups[:pace])
                    groups = groups[pace:]
                for f in range(lanes):
                    settle(sums[f], t, f)
            spend(groups)
            for (t, f), sums in zip(held, held_sums):
                settle(sums, t, f)
            if part == 1:
                all_ref[j] = code(row_ref[...])
                start(gather_copies(j))

        lax.fori_loop(0, share // step, products, 0)

    forward([(k, 0) for k in range(1, blocks)], step=2)
    flush(0)
    forward([(0, 1)], low=when(4), high=when(6), step=2)
    sum_near(0)
    forward([(0, 1)], low=when(6), step=2)
    forward(
        [(k, 1) for k in range(1, blocks)],
        [(when(3), lambda: middle(0)), (when(7), lambda: sum_gene(0))],
    )
    flush(1)
    lgside_ref[...] = jnp.zeros_like(lgside_ref)
    turn(0)
    backward(
        0,
        [
            (when(0), lambda: sum_near(1)),
            (when(4), lambda: middle(1)),
            (when(4), mix_part),
            (when(6), lambda: sum_gene(1)),
            (when(6), mix_sub),
        ],
        step=2,
    )
    turn(1)
    early = max(1, lats // 2)

    def first_parts():
        for p in range(early):
            mix_lat(p)

    backward(1, [(when(6), first_parts)])
    for p in range(early, lats):
        mix_lat(p)

    drain(all_sem, (), all_out.at[pl.ds(0, genes - 1)] if genes > 1 else None, all_out)
    for p in range(lats):
        wait(mix_back_copies(p))
        mix_keep(p).wait()


def lay_body(plan, mix_hbm, all_hbm, mix_out, ind_out, mix_ref, all_ref, row_ref, ind_ref, in_sem, out_sem):
    subs, lats = mix_hbm.shape[:2]
    parts = [(sub, p) for sub in range(subs) for p in range(lats)]
    codes = pltpu.make_async_copy(all_hbm, all_ref, in_sem.at[len(parts)])
    mix_in = [
        pltpu.make_async_copy(mix_hbm.at[part], mix_ref.at[part], in_sem.at[i]) for i, part in enumerate(parts)
    ]
    mix_back = [
        pltpu.make_async_copy(mix_ref.at[part], mix_out.at[part], out_sem.at[i]) for i, part in enumerate(parts)
    ]
    codes.start()
    codes.wait()
    for copy in mix_in:
        copy.start()
    for owner in range(plan.owners):
        base = owner * plan.share
        for slab in range(plan.split):
            gene = owner * plan.split + slab
            for j in range(plan.share):
                row_ref[gene, j] = decode(all_ref[gene, j])
            for r in range(plan.points // 128):
                first = slab * plan.points + r * 128
                ind_ref[base : base + plan.share, first : first + 128] = row_ref[gene, :, r, :]
    ind_back = pltpu.make_async_copy(ind_ref, ind_out, out_sem.at[len(parts)])
    ind_back.start()
    for copy, back in zip(mix_in, mix_back):
        copy.wait()
        back.start()
    for back in mix_back + [ind_back]:
        back.wait()


def lay(plan, mix, codes):
    anywhere = pl.BlockSpec(memory_space=pl.ANY)
    return pl.pallas_call(
        functools.partial(lay_body, plan),
        in_specs=[anywhere] * 2,
        out_specs=[anywhere] * 2,
        out_shape=[
            jax.ShapeDtypeStruct(mix.shape, F32),
            jax.ShapeDtypeStruct((plan.lats, plan.count), F32),
        ],
        scratch_shapes=[
            pltpu.VMEM(mix.shape, F32),
            pltpu.VMEM(codes.shape, jnp.int16),
            pltpu.VMEM((plan.gene, plan.share, plan.points // 128, 128), F32),
            pltpu.VMEM((plan.lats, plan.count), F32),
            pltpu.SemaphoreType.DMA((plan.blocks + 1,)),
            pltpu.SemaphoreType.DMA((plan.blocks + 1,)),
        ],
        compiler_params=pltpu.CompilerParams(vmem_limit_bytes=60 * 2**20),
    )(mix, codes)


def fused(plan, *args):
    genes, lats, subs = plan.gene, plan.lat, plan.sub
    rows, half, share, blocks = plan.rows, plan.half, plan.share, plan.blocks
    depth = plan.total // (lats * subs)
    sent = BF16 if plan.split == 1 else F32
    dma = pltpu.SemaphoreType.DMA
    far = genes * lats - 1
    flat = blocks - 1
    anywhere = pl.BlockSpec(memory_space=pl.ANY)
    scratch = [
        pltpu.VMEM((1, rows), jnp.int32),
        pltpu.VMEM((2, plan.table), F32),
        pltpu.VMEM((1, plan.lats), F32),
        pltpu.VMEM((1, plan.lats), F32),
        pltpu.VMEM((plan.table, plan.genes), BF16),
        pltpu.VMEM((2, share, plan.points), F32),
        pltpu.VMEM((share, plan.points), F32),
        pltpu.VMEM((plan.total, plan.genes), BF16),
        pltpu.VMEM((1, plan.genes), F32),
        pltpu.VMEM((plan.table, rows), BF16),
        pltpu.VMEM((blocks, 2, rows), F32),
        pltpu.VMEM((128, rows), F32),
        pltpu.VMEM((blocks * rows, DEPTH), BF16),
        pltpu.VMEM((share, DEPTH, plan.points), F32),
        pltpu.VMEM((share, 2 * blocks, half, 128), F32),
        pltpu.VMEM((2, subs, lats, share, half), F32),
        pltpu.VMEM((2, max(1, subs - 1), lats, share, half), F32),
        pltpu.VMEM((2, lats, share, half), sent),
        pltpu.VMEM((2, genes, lats, share, half), sent),
        pltpu.VMEM((plan.total, rows), BF16),
        pltpu.VMEM((plan.total, half), F32),
        pltpu.VMEM((rows, plan.genes), BF16),
        pltpu.VMEM((plan.total, half), F32),
        pltpu.VMEM((2, plan.owners, lats, share, half), F32),
        pltpu.VMEM((2, max(1, genes - 1), lats, share, half), F32),
        pltpu.VMEM((2, lats, share, half), F32),
        pltpu.VMEM((2, blocks, share, half), F32),
        pltpu.VMEM((128, half), F32),
        pltpu.VMEM((blocks * half, plan.turned), BF16),
        pltpu.VMEM((2, blocks, half, 128), F32),
        pltpu.VMEM((subs, lats, depth, plan.genes), F32),
        pltpu.VMEM((max(1, subs - 1), lats, depth, plan.genes), F32),
        pltpu.VMEM((lats, lats, depth, plan.genes), jnp.int16),
        pltpu.VMEM((lats, depth, plan.genes), F32),
        pltpu.VMEM((share, 8, plan.points), F32),
        pltpu.VMEM((plan.points // 128, 128), F32),
        pltpu.VMEM((share, plan.points // 128, 128), jnp.int16),
        pltpu.VMEM((share, blocks, max(1, plan.cached), half, plan.tile), F32),
        pltpu.VMEM((max(1, far), share, half), sent),
        dma((9,)),
        dma((2,)),
        dma((2, 2, max(1, subs - 1))),
        dma((2, 2)),
        dma((2, 2)),
        dma((2, 2)),
        dma((2, 3, max(1, subs - 1, lats - 1), lats)),
        dma((2,)),
        dma((lats,)),
    ]
    return pl.pallas_call(
        functools.partial(body, plan),
        in_specs=[anywhere] * 9,
        out_specs=[anywhere] * 2,
        out_shape=[
            jax.ShapeDtypeStruct((subs, lats, depth, plan.genes), F32),
            jax.ShapeDtypeStruct((genes, share, plan.points // 128, 128), jnp.int16),
        ],
        scratch_shapes=scratch,
        compiler_params=pltpu.CompilerParams(
            collective_id=0, has_side_effects=True, vmem_limit_bytes=67043328
        ),
    )(*args)


def on_device(
    cell_index,
    coords_table,
    expr_table,
    inducing,
    ind_weights,
    lengthscale,
    variance,
    mixing,
    noise_prec,
):
    genes, lats, subs = (lax.axis_size(axis) for axis in ("gene", "lat", "sub"))
    latents, count = ind_weights.shape
    owners = math.gcd(genes, latents)
    split = genes // owners
    share = latents // owners
    plan = Plan(
        gene=genes,
        lat=lats,
        sub=subs,
        rows=cell_index.shape[0],
        table=coords_table.shape[1],
        lats=latents,
        count=count,
        genes=expr_table.shape[1],
        share=share,
        split=split,
        sliced=share % 8 != 0,
        scale=-1.0 / math.sqrt(cell_index.shape[0] * lats * subs),
    )
    if plan.sliced:
        place = lax.axis_index("gene")
        first, cut = place // split * share, lax.rem(place, split) * plan.points
        inducing = lax.dynamic_slice(inducing, (0, first, cut), (2, share, plan.points))
        ind_weights = lax.dynamic_slice(ind_weights, (first, cut), (share, plan.points))
    mix, codes = fused(
        plan,
        cell_index[None, :],
        coords_table,
        lengthscale[None, :],
        variance[None, :],
        expr_table,
        inducing,
        ind_weights,
        mixing,
        noise_prec[None, :],
    )
    grad_mixing, grad_inducing = lay(plan, mix, codes)
    return grad_mixing.reshape(mixing.shape), grad_inducing


def solution(mesh):
    in_specs = (
        P(("group", "lat", "sub")),
        P("group", ("lat", "sub")),
        P(("group", "lat", "sub"), "gene"),
        P("group", "lat", "sub"),
        P(("group", "lat"), "sub"),
        P(("group", "lat")),
        P(("group", "lat")),
        P("group", "gene"),
        P(("group", "gene")),
    )
    out_specs = (P("group", "gene"), P(("group", "lat"), "sub"))
    return jax.shard_map(
        on_device, mesh=mesh, in_specs=in_specs, out_specs=out_specs, check_vma=False
    )
```

```python
import functools
import math
from typing import NamedTuple

import jax
import jax.numpy as jnp
from jax import lax
from jax.experimental import pallas as pl
from jax.experimental.pallas import tpu as pltpu
from jax.sharding import PartitionSpec as P

F32 = jnp.float32
BF16 = jnp.bfloat16
DEPTH = 24
SPARE = 21
CENTER = 0.5
LOG2E = math.log2(math.e)
PACK = 20
CACHE = 44 * 2**20
LEFT = (0, 0, 1, 1, 0, 2)
RIGHT = (0, 1, 0, 1, 2, 0)


class Plan(NamedTuple):
    gene: int
    lat: int
    sub: int
    rows: int
    table: int
    lats: int
    count: int
    genes: int
    share: int
    split: int
    sliced: bool
    scale: float

    @property
    def blocks(self):
        return self.lat * self.sub

    @property
    def points(self):
        return self.count // self.split

    @property
    def owners(self):
        return self.gene // self.split

    @property
    def total(self):
        return self.lat * self.lats

    @property
    def half(self):
        return self.rows // 2

    @property
    def turned(self):
        return -(-3 * self.share // 8) * 8

    @property
    def tile(self):
        return min(256, self.points)

    @property
    def cached(self):
        return min(self.points // self.tile, CACHE // (self.share * self.blocks * self.half * self.tile * 4))

    @property
    def wide(self):
        return min(512, self.genes)


BIAS = 128
LEAST = 2.0**-120


def bit_rows(shape):
    row = lax.broadcasted_iota(jnp.int32, shape, 0)
    return row, row < 8


def code(value):
    top = jnp.maximum(jnp.max(jnp.abs(value), axis=0, keepdims=True), LEAST)
    power = jnp.floor(jnp.log(top) * LOG2E + 1e-5) + 1.0
    row, marked = bit_rows(value.shape)
    scaled = value * jnp.exp2(15.0 - power)
    fine = jnp.clip(jnp.floor(scaled + 0.5), -32767.0, 32767.0).astype(jnp.int32)
    coarse = jnp.clip(jnp.floor(scaled * 0.5 + 0.5), -16383.0, 16383.0).astype(jnp.int32) * 2
    place = jnp.where(marked, row, 0)
    bit = jnp.bitwise_and(jnp.right_shift(power.astype(jnp.int32) + BIAS, place), 1)
    return jnp.where(marked, coarse + bit, fine).astype(jnp.int16)


def decode(codes):
    codes = codes.astype(jnp.int32)
    row, marked = bit_rows(codes.shape)
    bit = jnp.where(marked, jnp.bitwise_and(codes, 1), 0)
    weight = jnp.left_shift(bit, jnp.where(marked, row, 0)).astype(F32)
    power = jnp.sum(weight, axis=0, keepdims=True) - float(BIAS)
    return (codes - bit).astype(F32) * jnp.exp2(power - 15.0)


def pieces(value):
    high = value.astype(BF16).astype(F32)
    rest = value - high
    middle = rest.astype(BF16).astype(F32)
    low = (rest - middle).astype(BF16).astype(F32)
    return high, middle, low


def point_features(plan, scale, points_ref, weight_ref, table_ref):
    step = min(512, plan.points)

    def part(i, carry):
        cols = pl.ds(pl.multiple_of(i * step, 128), step)
        x = points_ref[0, :, cols] - CENTER
        y = points_ref[1, :, cols] - CENTER
        px = pieces(x * (2.0 * scale))
        py = pieces(y * (2.0 * scale))
        ps = pieces(jnp.broadcast_to(-scale, x.shape))
        pn = pieces((x * x + y * y) * -scale)
        rows = [px[k] for k in RIGHT] + [py[k] for k in RIGHT] + [ps[k] for k in RIGHT]
        rows += list(pn) + [weight_ref[:, cols]] + [jnp.zeros_like(x)] * (DEPTH - SPARE - 1)
        for place, row in enumerate(rows):
            for lane in range(plan.share):
                table_ref[lane, place : place + 1, cols] = row[lane : lane + 1, :]
        return carry

    lax.fori_loop(0, plan.points // step, part, 0)


def cell_features(plan, block, xy_ref, side_ref, feat_ref):
    x = xy_ref[block, 0:1, :] - CENTER
    y = xy_ref[block, 1:2, :] - CENTER
    px, py, pn = pieces(x), pieces(y), pieces(x * x + y * y)
    rows = [px[k] for k in LEFT] + [py[k] for k in LEFT] + [pn[k] for k in LEFT]
    for place, row in enumerate(rows):
        side_ref[place : place + 1, :] = row
    place = pl.ds(pl.multiple_of(block * plan.rows, plan.rows), plan.rows)
    feat_ref[place, :] = side_ref[...].T[:, :DEPTH].astype(BF16)


def body(
    plan,
    index_hbm,
    coords_hbm,
    length_hbm,
    height_hbm,
    expr_hbm,
    points_hbm,
    weight_hbm,
    mixing_hbm,
    noise_hbm,
    mix_out,
    all_out,
    index_ref,
    coords_ref,
    length_ref,
    height_ref,
    expr_ref,
    points_ref,
    weight_ref,
    mixing_ref,
    noise_ref,
    pick_ref,
    xy_ref,
    side_ref,
    feat_ref,
    table_ref,
    total_ref,
    part_ref,
    near_ref,
    final_ref,
    latent_recv,
    latent_ref,
    side_lat_ref,
    seen_ref,
    cell_ref,
    chunk_ref,
    rs_ref,
    own_ref,
    lg_ref,
    lgside_ref,
    lgt_ref,
    wide_ref,
    mix_ref,
    mix_near,
    mix_all,
    mix_sum,
    sum_ref,
    row_ref,
    all_ref,
    cache_ref,
    far_ref,
    load_sem,
    xy_sem,
    near_sem,
    latent_sem,
    rs_sem,
    lg_sem,
    mix_sem,
    all_sem,
    keep_sem,
):
    genes, lats, subs, blocks = plan.gene, plan.lat, plan.sub, plan.blocks
    rows, half, share = plan.rows, plan.half, plan.share
    g, l, s = lax.axis_index("gene"), lax.axis_index("lat"), lax.axis_index("sub")
    owner, slab = g // plan.split, lax.rem(g, plan.split)
    me = l * subs + s

    def at(dg=0, dl=0, ds=0):
        return {"gene": lax.rem(g + dg, genes), "lat": lax.rem(l + dl, lats), "sub": lax.rem(s + ds, subs)}

    def send(src, dst, sems, k, device):
        return pltpu.make_async_remote_copy(
            src_ref=src,
            dst_ref=dst,
            send_sem=sems.at[(0, *k)],
            recv_sem=sems.at[(1, *k)],
            device_id=device,
            device_id_type=pl.DeviceIdType.MESH,
        )

    def drain(sems, k, sent, got):
        if sent is not None:
            pltpu.make_async_copy(sent, sent, sems.at[(0, *k)]).wait()
        pltpu.make_async_copy(got, got, sems.at[(1, *k)]).wait()

    if plan.sliced:
        points_src, weight_src = points_hbm, weight_hbm
    else:
        mine = pl.ds(pl.multiple_of(owner * share, 8), share)
        cut = pl.ds(pl.multiple_of(slab * plan.points, 128), plan.points)
        points_src, weight_src = points_hbm.at[:, mine, cut], weight_hbm.at[mine, cut]
    loads = [
        pltpu.make_async_copy(points_src, points_ref, load_sem.at[0]),
        pltpu.make_async_copy(weight_src, weight_ref, load_sem.at[1]),
        pltpu.make_async_copy(expr_hbm, expr_ref, load_sem.at[2]),
        pltpu.make_async_copy(mixing_hbm, mixing_ref, load_sem.at[3]),
        pltpu.make_async_copy(noise_hbm, noise_ref, load_sem.at[4]),
    ]
    small = [
        pltpu.make_async_copy(index_hbm, index_ref, load_sem.at[5]),
        pltpu.make_async_copy(coords_hbm, coords_ref, load_sem.at[6]),
        pltpu.make_async_copy(length_hbm, length_ref, load_sem.at[7]),
        pltpu.make_async_copy(height_hbm, height_ref, load_sem.at[8]),
    ]
    for load in small + loads[:2]:
        load.start()

    far = [(dg, dl, 0) for dg in range(genes) for dl in range(lats) if dg or dl]
    flat = [(0, dl, ds) for dl in range(lats) for ds in range(subs) if dl or ds]
    peers = sorted(set(far) | set(flat))
    barrier = pltpu.get_barrier_semaphore()
    for peer in peers:
        pl.semaphore_signal(barrier, inc=1, device_id=at(*peer), device_id_type=pl.DeviceIdType.MESH)

    for load in small:
        load.wait()
    pick = lax.broadcasted_iota(jnp.int32, (plan.table, rows), 0) == index_ref[...]
    pick_ref[...] = pick.astype(F32).astype(BF16)
    local = jnp.zeros((2, rows), F32)
    for piece in pieces(coords_ref[...]):
        local = local + jnp.dot(piece.astype(BF16), pick_ref[...], preferred_element_type=F32)
    xy_ref[me] = local
    side_ref[...] = jnp.zeros_like(side_ref)
    side_ref[18:21, :] = jnp.ones((3, rows), F32)
    cell_features(plan, me, xy_ref, side_ref, feat_ref)

    lane = lax.broadcasted_iota(jnp.int32, (share, plan.lats), 1)
    chosen = lane == lax.broadcasted_iota(jnp.int32, (share, plan.lats), 0) + owner * share
    length = jnp.sum(jnp.where(chosen, length_ref[...], 0.0), axis=1, keepdims=True)
    height = jnp.sum(jnp.where(chosen, height_ref[...], 0.0), axis=1, keepdims=True)
    loads[0].wait()
    loads[1].wait()
    for load in loads[2:]:
        load.start()
    point_features(plan, (0.5 * LOG2E) / (length * length), points_ref, weight_ref, table_ref)

    def ring(k):
        return lax.rem(me + k, blocks)

    def flush(part):
        for k in range(blocks):
            for j in range(share):
                row = jnp.sum(total_ref[j, 2 * k + part].T, axis=0, keepdims=True)
                part_ref[part, lax.rem(ring(k), subs), ring(k) // subs, j : j + 1, :] = row
        start(near_copies(part))

    def forward(units, stages=(), low=0, high=share, step=1):
        step = math.gcd(step, high - low) if high > low else 1

        def products(i, carry):
            for when, stage in stages:
                pl.when(i == (when - low) // step)(stage)
            for j in [low + i * step + d for d in range(step)]:
                for k, part in units:
                    place = pl.multiple_of(ring(k) * rows + part * half, half)
                    feat = feat_ref[pl.ds(place, half), :]
                    total = jnp.zeros((half, 128), F32)
                    for start in range(0, plan.points, plan.tile):
                        cols = slice(start, start + plan.tile)
                        value = jnp.exp2(
                            jnp.dot(feat, table_ref[j, :, cols].astype(BF16), preferred_element_type=F32)
                        )
                        if part == 1 and start // plan.tile < plan.cached:
                            cache_ref[j, k, start // plan.tile] = value
                        for first in range(0, plan.tile, 128):
                            w = table_ref[j, SPARE : SPARE + 1, start + first : start + first + 128]
                            total = total + value[:, first : first + 128] * w
                    total_ref[j, 2 * k + part] = total
            return carry

        lax.fori_loop(0, (high - low) // step, products, 0)

    def when(k):
        return k * share // 8

    forward([(0, 0)], step=4)

    pl.semaphore_wait(barrier, len(peers))
    for peer in flat:
        send(xy_ref.at[me], xy_ref.at[me], xy_sem, (), at(*peer)).start()
    forward([(0, 1)], high=when(4), step=4)
    for load in loads[2:]:
        load.wait()
    gene_tiles = [slice(first, first + plan.wide) for first in range(0, plan.genes, plan.wide)]
    for cols in gene_tiles:
        seen = lax.dot_general(
            pick_ref[...], expr_ref[:, cols], (((0,), (0,)), ((), ())), preferred_element_type=F32
        )
        seen_ref[:, cols] = seen.astype(BF16)
    if flat:
        others = xy_ref.at[pl.ds(0, blocks - 1)]
        drain(xy_sem, (), others, others)
    for k in range(1, blocks):
        cell_features(plan, ring(k), xy_ref, side_ref, feat_ref)

    def near_copies(part):
        return [
            send(part_ref.at[part, lax.rem(s + ds, subs)], near_ref.at[part, ds - 1], near_sem, (part, ds - 1), at(ds=ds))
            for ds in range(1, subs)
        ]

    def latent_copies(part):
        out = []
        for peer in far:
            target = at(*peer)
            out.append(
                send(final_ref.at[part, target["lat"]], latent_recv.at[part, g, l], latent_sem, (part,), target)
            )
        return out

    def rs_copies(part):
        out = []
        for dg in range(1, genes):
            target = at(dg=dg)
            source = chunk_ref.at[part, target["gene"] // plan.split]
            out.append(send(source, rs_ref.at[part, dg - 1], rs_sem, (part,), target))
        return out

    def lg_copies(part):
        out = []
        for peer in flat:
            target = at(*peer)
            out.append(send(own_ref.at[part, target["lat"]], lg_ref.at[part, me], lg_sem, (part,), target))
        return out

    def start(copies):
        for copy in copies:
            copy.start()

    def wait(copies):
        for copy in copies:
            copy.wait()

    def sum_near(part):
        wait(near_copies(part))
        value = part_ref[part, s]
        for ds in range(1, subs):
            value = value + near_ref[part, ds - 1]
        value = value * height[None]
        final_ref[part] = value.astype(final_ref.dtype)
        start(latent_copies(part))
        pltpu.make_async_copy(final_ref.at[part, l], latent_recv.at[part, g, l], latent_sem.at[1, part]).start()

    def middle(part):
        drain(latent_sem, (part,), far_ref if far else None, latent_recv.at[part])
        for lat in range(lats):
            for own in range(plan.owners):
                first = own * plan.split
                value = latent_recv[part, first, lat].astype(F32)
                for other in range(1, plan.split):
                    value = value + latent_recv[part, first + other, lat].astype(F32)
                base = lat * plan.lats + own * share
                side_lat_ref[base : base + share, :] = value
        cells = slice(part * half, (part + 1) * half)
        latent_ref[:, cells] = side_lat_ref[...].astype(BF16)
        turned = side_lat_ref[...].T.astype(BF16)
        cell = jnp.zeros((plan.total, half), F32)
        for cols in gene_tiles:
            mixing = mixing_ref[:, cols]
            predicted = jnp.dot(turned, mixing, preferred_element_type=F32)
            weighted = (noise_ref[:, cols] * (seen_ref[cells, cols].astype(F32) - predicted)).astype(BF16)
            seen_ref[cells, cols] = weighted
            cell = cell + lax.dot_general(
                mixing, weighted, (((1,), (1,)), ((), ())), preferred_element_type=F32
            )
        cell_ref[...] = cell
        for own in range(plan.owners):
            for lat in range(lats):
                base = lat * plan.lats + own * share
                chunk_ref[part, own, lat] = plan.scale * cell_ref[base : base + share, :]
        start(rs_copies(part))

    def sum_gene(part):
        if genes > 1:
            drain(rs_sem, (part,), rs_ref.at[part], rs_ref.at[part])
        value = chunk_ref[part, owner]
        for dg in range(1, genes):
            value = value + rs_ref[part, dg - 1]
        own_ref[part] = value
        start(lg_copies(part))
        pltpu.make_async_copy(own_ref.at[part, l], lg_ref.at[part, me], lg_sem.at[1, part]).start()

    def turn(part):
        drain(lg_sem, (part,), lg_ref.at[part, pl.ds(0, blocks - 1)] if flat else None, lg_ref.at[part])
        for block in range(blocks):
            for p, piece in enumerate(pieces(lg_ref[part, block] * height)):
                lgside_ref[p * share : (p + 1) * share, :] = piece
            lgt_ref[block * half : (block + 1) * half, :] = (
                lgside_ref[...].T[:, : plan.turned].astype(BF16)
            )

    def mix_near_copies():
        return [
            send(mix_ref.at[lax.rem(s + ds, subs)], mix_near.at[ds - 1], mix_sem, (0, ds - 1, 0), at(ds=ds))
            for ds in range(1, subs)
        ]

    def mix_lat_copies(p):
        return [send(mix_all.at[l, p], mix_all.at[l, p], mix_sem, (1, dl - 1, p), at(dl=dl)) for dl in range(1, lats)]

    def mix_back_copies(p):
        return [send(mix_sum.at[p], mix_out.at[s, p], mix_sem, (2, ds - 1, p), at(ds=ds)) for ds in range(1, subs)]

    def mix_keep(p):
        return pltpu.make_async_copy(mix_sum.at[p], mix_out.at[s, p], keep_sem.at[p])

    def mix_part():
        depth = mix_ref.shape[2]
        for cols in gene_tiles:
            value = plan.scale * jnp.dot(latent_ref[...], seen_ref[:, cols], preferred_element_type=F32)
            for sub in range(subs):
                for p in range(lats):
                    base = (sub * lats + p) * depth
                    mix_ref[sub, p, :, cols] = value[base : base + depth, :]
        start(mix_near_copies())

    def mix_sub():
        wait(mix_near_copies())
        for p in range(lats):
            value = mix_ref[s, p]
            for ds in range(1, subs):
                value = value + mix_near[ds - 1, p]
            mix_all[l, p] = code(value)
            start(mix_lat_copies(p))

    def mix_lat(p):
        wait(mix_lat_copies(p))
        value = decode(mix_all[0, p])
        for lat in range(1, lats):
            value = value + decode(mix_all[lat, p])
        mix_sum[p] = value
        start(mix_back_copies(p))
        mix_keep(p).start()

    def gather_copies(j):
        return [
            send(all_ref.at[j], all_out.at[g, j], all_sem, (), at(dg=dg)) for dg in range(1, genes)
        ] + [pltpu.make_async_copy(all_ref.at[j], all_out.at[g, j], all_sem.at[1])]

    def backward(part, stages, step=1):
        step = math.gcd(step, share)

        def products(i, carry):
            for when, stage in stages:
                pl.when(i == when // step)(stage)
            for d in range(step):
                one(i * step + d, d)
            return carry

        def one(j, slot):
            row = lax.broadcasted_iota(jnp.int32, (plan.turned, 128), 0)
            select = (lax.rem(row, share) == j).astype(F32).astype(BF16)
            for k in range(blocks):
                place = pl.multiple_of(ring(k) * half, half)
                turned = lgt_ref[pl.ds(place, half), :]
                wide_ref[slot, k] = jnp.dot(turned, select, preferred_element_type=F32)
            tiles = list(range(plan.points // plan.tile))
            kept = tiles[: plan.cached] if part == 1 else []
            fresh = tiles[len(kept) :]
            lanes = plan.tile // 128
            held = [(t, f) for t in kept for f in range(lanes)]
            held_sums = [None] * len(held)
            packs = [range(i, min(i + PACK, len(held))) for i in range(0, len(held), PACK)]
            groups = [(pack, k, r) for pack in packs for k in range(blocks) for r in range(0, half, 8)]
            steps = len(fresh) * blocks
            pace = -(-len(groups) // max(1, steps))

            def settle(sums, t, f):
                r = t * lanes + f
                here = slice(r * 128, (r + 1) * 128)
                if part == 0:
                    sum_ref[j, :, here] = sums
                else:
                    row_ref[r : r + 1, :] = jnp.sum(sum_ref[j, :, here] + sums, axis=0, keepdims=True)

            def spend(groups):
                for pack, k, r in groups:
                    wide = wide_ref[slot, k, r : r + 8, :]
                    for i in pack:
                        t, f = held[i]
                        term = cache_ref[j, k, t, r : r + 8, f * 128 : (f + 1) * 128] * wide
                        held_sums[i] = term if held_sums[i] is None else held_sums[i] + term

            for t in fresh:
                points = table_ref[j, :, t * plan.tile : (t + 1) * plan.tile].astype(BF16)
                sums = [None] * lanes
                for k in range(blocks):
                    place = pl.multiple_of(ring(k) * rows + part * half, half)
                    value = jnp.exp2(
                        jnp.dot(feat_ref[pl.ds(place, half), :], points, preferred_element_type=F32)
                    )
                    for f in range(lanes):
                        term = value[:, f * 128 : (f + 1) * 128] * wide_ref[slot, k]
                        term = jnp.sum(term.reshape(half // 8, 8, 128), axis=0)
                        sums[f] = term if sums[f] is None else sums[f] + term
                    spend(groups[:pace])
                    groups = groups[pace:]
                for f in range(lanes):
                    settle(sums[f], t, f)
            spend(groups)
            for (t, f), sums in zip(held, held_sums):
                settle(sums, t, f)
            if part == 1:
                all_ref[j] = code(row_ref[...])
                start(gather_copies(j))

        lax.fori_loop(0, share // step, products, 0)

    forward([(k, 0) for k in range(1, blocks)], step=2)
    flush(0)
    forward([(0, 1)], low=when(4), high=when(6), step=2)
    sum_near(0)
    forward([(0, 1)], low=when(6), step=2)
    forward(
        [(k, 1) for k in range(1, blocks)],
        [(when(3), lambda: middle(0)), (when(7), lambda: sum_gene(0))],
    )
    flush(1)
    lgside_ref[...] = jnp.zeros_like(lgside_ref)
    turn(0)
    backward(
        0,
        [
            (when(0), lambda: sum_near(1)),
            (when(4), lambda: middle(1)),
            (when(6), mix_part),
            (when(6), lambda: sum_gene(1)),
        ],
        step=2,
    )
    mix_sub()
    turn(1)
    early = max(1, lats // 2)

    def first_parts():
        for p in range(early):
            mix_lat(p)

    backward(1, [(when(6), first_parts)])
    for p in range(early, lats):
        mix_lat(p)

    drain(all_sem, (), all_out.at[pl.ds(0, genes - 1)] if genes > 1 else None, all_out)
    for p in range(lats):
        wait(mix_back_copies(p))
        mix_keep(p).wait()


def lay_body(plan, mix_hbm, all_hbm, mix_out, ind_out, mix_ref, all_ref, row_ref, ind_ref, in_sem, out_sem):
    subs, lats = mix_hbm.shape[:2]
    parts = [(sub, p) for sub in range(subs) for p in range(lats)]
    codes = pltpu.make_async_copy(all_hbm, all_ref, in_sem.at[len(parts)])
    mix_in = [
        pltpu.make_async_copy(mix_hbm.at[part], mix_ref.at[part], in_sem.at[i]) for i, part in enumerate(parts)
    ]
    mix_back = [
        pltpu.make_async_copy(mix_ref.at[part], mix_out.at[part], out_sem.at[i]) for i, part in enumerate(parts)
    ]
    for copy in [codes] + mix_in:
        copy.start()
    codes.wait()
    for owner in range(plan.owners):
        base = owner * plan.share
        for slab in range(plan.split):
            gene = owner * plan.split + slab
            for j in range(plan.share):
                row_ref[gene, j] = decode(all_ref[gene, j])
            for r in range(plan.points // 128):
                first = slab * plan.points + r * 128
                ind_ref[base : base + plan.share, first : first + 128] = row_ref[gene, :, r, :]
    ind_back = pltpu.make_async_copy(ind_ref, ind_out, out_sem.at[len(parts)])
    ind_back.start()
    for copy, back in zip(mix_in, mix_back):
        copy.wait()
        back.start()
    for back in mix_back + [ind_back]:
        back.wait()


def lay(plan, mix, codes):
    anywhere = pl.BlockSpec(memory_space=pl.ANY)
    return pl.pallas_call(
        functools.partial(lay_body, plan),
        in_specs=[anywhere] * 2,
        out_specs=[anywhere] * 2,
        out_shape=[
            jax.ShapeDtypeStruct(mix.shape, F32),
            jax.ShapeDtypeStruct((plan.lats, plan.count), F32),
        ],
        scratch_shapes=[
            pltpu.VMEM(mix.shape, F32),
            pltpu.VMEM(codes.shape, jnp.int16),
            pltpu.VMEM((plan.gene, plan.share, plan.points // 128, 128), F32),
            pltpu.VMEM((plan.lats, plan.count), F32),
            pltpu.SemaphoreType.DMA((plan.blocks + 1,)),
            pltpu.SemaphoreType.DMA((plan.blocks + 1,)),
        ],
        compiler_params=pltpu.CompilerParams(vmem_limit_bytes=60 * 2**20),
    )(mix, codes)


def fused(plan, *args):
    genes, lats, subs = plan.gene, plan.lat, plan.sub
    rows, half, share, blocks = plan.rows, plan.half, plan.share, plan.blocks
    depth = plan.total // (lats * subs)
    sent = BF16 if plan.split == 1 else F32
    dma = pltpu.SemaphoreType.DMA
    far = genes * lats - 1
    flat = blocks - 1
    anywhere = pl.BlockSpec(memory_space=pl.ANY)
    scratch = [
        pltpu.VMEM((1, rows), jnp.int32),
        pltpu.VMEM((2, plan.table), F32),
        pltpu.VMEM((1, plan.lats), F32),
        pltpu.VMEM((1, plan.lats), F32),
        pltpu.VMEM((plan.table, plan.genes), BF16),
        pltpu.VMEM((2, share, plan.points), F32),
        pltpu.VMEM((share, plan.points), F32),
        pltpu.VMEM((plan.total, plan.genes), BF16),
        pltpu.VMEM((1, plan.genes), F32),
        pltpu.VMEM((plan.table, rows), BF16),
        pltpu.VMEM((blocks, 2, rows), F32),
        pltpu.VMEM((128, rows), F32),
        pltpu.VMEM((blocks * rows, DEPTH), BF16),
        pltpu.VMEM((share, DEPTH, plan.points), F32),
        pltpu.VMEM((share, 2 * blocks, half, 128), F32),
        pltpu.VMEM((2, subs, lats, share, half), F32),
        pltpu.VMEM((2, max(1, subs - 1), lats, share, half), F32),
        pltpu.VMEM((2, lats, share, half), sent),
        pltpu.VMEM((2, genes, lats, share, half), sent),
        pltpu.VMEM((plan.total, rows), BF16),
        pltpu.VMEM((plan.total, half), F32),
        pltpu.VMEM((rows, plan.genes), BF16),
        pltpu.VMEM((plan.total, half), F32),
        pltpu.VMEM((2, plan.owners, lats, share, half), F32),
        pltpu.VMEM((2, max(1, genes - 1), lats, share, half), F32),
        pltpu.VMEM((2, lats, share, half), F32),
        pltpu.VMEM((2, blocks, share, half), F32),
        pltpu.VMEM((128, half), F32),
        pltpu.VMEM((blocks * half, plan.turned), BF16),
        pltpu.VMEM((2, blocks, half, 128), F32),
        pltpu.VMEM((subs, lats, depth, plan.genes), F32),
        pltpu.VMEM((max(1, subs - 1), lats, depth, plan.genes), F32),
        pltpu.VMEM((lats, lats, depth, plan.genes), jnp.int16),
        pltpu.VMEM((lats, depth, plan.genes), F32),
        pltpu.VMEM((share, 8, plan.points), F32),
        pltpu.VMEM((plan.points // 128, 128), F32),
        pltpu.VMEM((share, plan.points // 128, 128), jnp.int16),
        pltpu.VMEM((share, blocks, max(1, plan.cached), half, plan.tile), F32),
        pltpu.VMEM((max(1, far), share, half), sent),
        dma((9,)),
        dma((2,)),
        dma((2, 2, max(1, subs - 1))),
        dma((2, 2)),
        dma((2, 2)),
        dma((2, 2)),
        dma((2, 3, max(1, subs - 1, lats - 1), lats)),
        dma((2,)),
        dma((lats,)),
    ]
    return pl.pallas_call(
        functools.partial(body, plan),
        in_specs=[anywhere] * 9,
        out_specs=[anywhere] * 2,
        out_shape=[
            jax.ShapeDtypeStruct((subs, lats, depth, plan.genes), F32),
            jax.ShapeDtypeStruct((genes, share, plan.points // 128, 128), jnp.int16),
        ],
        scratch_shapes=scratch,
        compiler_params=pltpu.CompilerParams(
            collective_id=0, has_side_effects=True, vmem_limit_bytes=67043328
        ),
    )(*args)


def on_device(
    cell_index,
    coords_table,
    expr_table,
    inducing,
    ind_weights,
    lengthscale,
    variance,
    mixing,
    noise_prec,
):
    genes, lats, subs = (lax.axis_size(axis) for axis in ("gene", "lat", "sub"))
    latents, count = ind_weights.shape
    owners = math.gcd(genes, latents)
    split = genes // owners
    share = latents // owners
    plan = Plan(
        gene=genes,
        lat=lats,
        sub=subs,
        rows=cell_index.shape[0],
        table=coords_table.shape[1],
        lats=latents,
        count=count,
        genes=expr_table.shape[1],
        share=share,
        split=split,
        sliced=share % 8 != 0,
        scale=-1.0 / math.sqrt(cell_index.shape[0] * lats * subs),
    )
    if plan.sliced:
        place = lax.axis_index("gene")
        first, cut = place // split * share, lax.rem(place, split) * plan.points
        inducing = lax.dynamic_slice(inducing, (0, first, cut), (2, share, plan.points))
        ind_weights = lax.dynamic_slice(ind_weights, (first, cut), (share, plan.points))
    mix, codes = fused(
        plan,
        cell_index[None, :],
        coords_table,
        lengthscale[None, :],
        variance[None, :],
        expr_table,
        inducing,
        ind_weights,
        mixing,
        noise_prec[None, :],
    )
    grad_mixing, grad_inducing = lay(plan, mix, codes)
    return grad_mixing.reshape(mixing.shape), grad_inducing


def solution(mesh):
    in_specs = (
        P(("group", "lat", "sub")),
        P("group", ("lat", "sub")),
        P(("group", "lat", "sub"), "gene"),
        P("group", "lat", "sub"),
        P(("group", "lat"), "sub"),
        P(("group", "lat")),
        P(("group", "lat")),
        P("group", "gene"),
        P(("group", "gene")),
    )
    out_specs = (P("group", "gene"), P(("group", "lat"), "sub"))
    return jax.shard_map(
        on_device, mesh=mesh, in_specs=in_specs, out_specs=out_specs, check_vma=False
    )
```

```python
import functools
import math
from typing import NamedTuple

import jax
import jax.numpy as jnp
from jax import lax
from jax.experimental import pallas as pl
from jax.experimental.pallas import tpu as pltpu
from jax.sharding import PartitionSpec as P

F32 = jnp.float32
BF16 = jnp.bfloat16
DEPTH = 24
SPARE = 21
CENTER = 0.5
LOG2E = math.log2(math.e)
PACK = 20
CACHE = 40 * 2**20
LEFT = (0, 0, 1, 1, 0, 2)
RIGHT = (0, 1, 0, 1, 2, 0)


class Plan(NamedTuple):
    gene: int
    lat: int
    sub: int
    rows: int
    table: int
    lats: int
    count: int
    genes: int
    share: int
    split: int
    sliced: bool
    scale: float

    @property
    def blocks(self):
        return self.lat * self.sub

    @property
    def points(self):
        return self.count // self.split

    @property
    def owners(self):
        return self.gene // self.split

    @property
    def total(self):
        return self.lat * self.lats

    @property
    def half(self):
        return self.rows // 2

    @property
    def turned(self):
        return -(-3 * self.share // 8) * 8

    @property
    def tile(self):
        return min(256, self.points)

    @property
    def cached(self):
        return min(self.points // self.tile, CACHE // (self.share * self.blocks * self.half * self.tile * 4))

    @property
    def wide(self):
        return min(512, self.genes)


BIAS = 128
LEAST = 2.0**-120


def bit_rows(shape):
    row = lax.broadcasted_iota(jnp.int32, shape, 0)
    return row, row < 8


def code(value):
    top = jnp.maximum(jnp.max(jnp.abs(value), axis=0, keepdims=True), LEAST)
    power = jnp.floor(jnp.log(top) * LOG2E + 1e-5) + 1.0
    row, marked = bit_rows(value.shape)
    scaled = value * jnp.exp2(15.0 - power)
    fine = jnp.clip(jnp.floor(scaled + 0.5), -32767.0, 32767.0).astype(jnp.int32)
    coarse = jnp.clip(jnp.floor(scaled * 0.5 + 0.5), -16383.0, 16383.0).astype(jnp.int32) * 2
    place = jnp.where(marked, row, 0)
    bit = jnp.bitwise_and(jnp.right_shift(power.astype(jnp.int32) + BIAS, place), 1)
    return jnp.where(marked, coarse + bit, fine).astype(jnp.int16)


def decode(codes):
    codes = codes.astype(jnp.int32)
    row, marked = bit_rows(codes.shape)
    bit = jnp.where(marked, jnp.bitwise_and(codes, 1), 0)
    weight = jnp.left_shift(bit, jnp.where(marked, row, 0)).astype(F32)
    power = jnp.sum(weight, axis=0, keepdims=True) - float(BIAS)
    return (codes - bit).astype(F32) * jnp.exp2(power - 15.0)


def pieces(value):
    high = value.astype(BF16).astype(F32)
    rest = value - high
    middle = rest.astype(BF16).astype(F32)
    low = (rest - middle).astype(BF16).astype(F32)
    return high, middle, low


def point_features(plan, scale, points_ref, weight_ref, table_ref):
    step = min(512, plan.points)

    def part(i, carry):
        cols = pl.ds(pl.multiple_of(i * step, 128), step)
        x = points_ref[0, :, cols] - CENTER
        y = points_ref[1, :, cols] - CENTER
        px = pieces(x * (2.0 * scale))
        py = pieces(y * (2.0 * scale))
        ps = pieces(jnp.broadcast_to(-scale, x.shape))
        pn = pieces((x * x + y * y) * -scale)
        rows = [px[k] for k in RIGHT] + [py[k] for k in RIGHT] + [ps[k] for k in RIGHT]
        rows += list(pn) + [weight_ref[:, cols]] + [jnp.zeros_like(x)] * (DEPTH - SPARE - 1)
        for place, row in enumerate(rows):
            for lane in range(plan.share):
                table_ref[lane, place : place + 1, cols] = row[lane : lane + 1, :]
        return carry

    lax.fori_loop(0, plan.points // step, part, 0)


def cell_features(plan, block, xy_ref, side_ref, feat_ref):
    x = xy_ref[block, 0:1, :] - CENTER
    y = xy_ref[block, 1:2, :] - CENTER
    px, py, pn = pieces(x), pieces(y), pieces(x * x + y * y)
    rows = [px[k] for k in LEFT] + [py[k] for k in LEFT] + [pn[k] for k in LEFT]
    for place, row in enumerate(rows):
        side_ref[place : place + 1, :] = row
    place = pl.ds(pl.multiple_of(block * plan.rows, plan.rows), plan.rows)
    feat_ref[place, :] = side_ref[...].T[:, :DEPTH].astype(BF16)


def body(
    plan,
    index_hbm,
    coords_hbm,
    length_hbm,
    height_hbm,
    expr_hbm,
    points_hbm,
    weight_hbm,
    mixing_hbm,
    noise_hbm,
    mix_out,
    all_out,
    index_ref,
    coords_ref,
    length_ref,
    height_ref,
    expr_ref,
    points_ref,
    weight_ref,
    mixing_ref,
    noise_ref,
    pick_ref,
    xy_ref,
    side_ref,
    feat_ref,
    table_ref,
    total_ref,
    part_ref,
    near_ref,
    final_ref,
    latent_recv,
    latent_ref,
    side_lat_ref,
    seen_ref,
    cell_ref,
    chunk_ref,
    rs_ref,
    own_ref,
    lg_ref,
    lgside_ref,
    lgt_ref,
    wide_ref,
    mix_ref,
    mix_near,
    mix_all,
    mix_sum,
    sum_ref,
    row_ref,
    all_ref,
    cache_ref,
    far_ref,
    load_sem,
    xy_sem,
    near_sem,
    latent_sem,
    rs_sem,
    lg_sem,
    mix_sem,
    all_sem,
    keep_sem,
):
    genes, lats, subs, blocks = plan.gene, plan.lat, plan.sub, plan.blocks
    rows, half, share = plan.rows, plan.half, plan.share
    g, l, s = lax.axis_index("gene"), lax.axis_index("lat"), lax.axis_index("sub")
    owner, slab = g // plan.split, lax.rem(g, plan.split)
    me = l * subs + s

    def at(dg=0, dl=0, ds=0):
        return {"gene": lax.rem(g + dg, genes), "lat": lax.rem(l + dl, lats), "sub": lax.rem(s + ds, subs)}

    def send(src, dst, sems, k, device):
        return pltpu.make_async_remote_copy(
            src_ref=src,
            dst_ref=dst,
            send_sem=sems.at[(0, *k)],
            recv_sem=sems.at[(1, *k)],
            device_id=device,
            device_id_type=pl.DeviceIdType.MESH,
        )

    def drain(sems, k, sent, got):
        if sent is not None:
            pltpu.make_async_copy(sent, sent, sems.at[(0, *k)]).wait()
        pltpu.make_async_copy(got, got, sems.at[(1, *k)]).wait()

    if plan.sliced:
        points_src, weight_src = points_hbm, weight_hbm
    else:
        mine = pl.ds(pl.multiple_of(owner * share, 8), share)
        cut = pl.ds(pl.multiple_of(slab * plan.points, 128), plan.points)
        points_src, weight_src = points_hbm.at[:, mine, cut], weight_hbm.at[mine, cut]
    loads = [
        pltpu.make_async_copy(points_src, points_ref, load_sem.at[0]),
        pltpu.make_async_copy(weight_src, weight_ref, load_sem.at[1]),
        pltpu.make_async_copy(expr_hbm, expr_ref, load_sem.at[2]),
        pltpu.make_async_copy(mixing_hbm, mixing_ref, load_sem.at[3]),
        pltpu.make_async_copy(noise_hbm, noise_ref, load_sem.at[4]),
    ]
    small = [
        pltpu.make_async_copy(index_hbm, index_ref, load_sem.at[5]),
        pltpu.make_async_copy(coords_hbm, coords_ref, load_sem.at[6]),
        pltpu.make_async_copy(length_hbm, length_ref, load_sem.at[7]),
        pltpu.make_async_copy(height_hbm, height_ref, load_sem.at[8]),
    ]
    for load in small + loads[:2]:
        load.start()

    far = [(dg, dl, 0) for dg in range(genes) for dl in range(lats) if dg or dl]
    flat = [(0, dl, ds) for dl in range(lats) for ds in range(subs) if dl or ds]
    peers = sorted(set(far) | set(flat))
    barrier = pltpu.get_barrier_semaphore()
    for peer in peers:
        pl.semaphore_signal(barrier, inc=1, device_id=at(*peer), device_id_type=pl.DeviceIdType.MESH)

    for load in small:
        load.wait()
    pick = lax.broadcasted_iota(jnp.int32, (plan.table, rows), 0) == index_ref[...]
    pick_ref[...] = pick.astype(F32).astype(BF16)
    local = jnp.zeros((2, rows), F32)
    for piece in pieces(coords_ref[...]):
        local = local + jnp.dot(piece.astype(BF16), pick_ref[...], preferred_element_type=F32)
    xy_ref[me] = local
    side_ref[...] = jnp.zeros_like(side_ref)
    side_ref[18:21, :] = jnp.ones((3, rows), F32)
    cell_features(plan, me, xy_ref, side_ref, feat_ref)

    lane = lax.broadcasted_iota(jnp.int32, (share, plan.lats), 1)
    chosen = lane == lax.broadcasted_iota(jnp.int32, (share, plan.lats), 0) + owner * share
    length = jnp.sum(jnp.where(chosen, length_ref[...], 0.0), axis=1, keepdims=True)
    height = jnp.sum(jnp.where(chosen, height_ref[...], 0.0), axis=1, keepdims=True)
    loads[0].wait()
    loads[1].wait()
    for load in loads[2:]:
        load.start()
    point_features(plan, (0.5 * LOG2E) / (length * length), points_ref, weight_ref, table_ref)

    def ring(k):
        return lax.rem(me + k, blocks)

    def flush(part):
        for k in range(blocks):
            for j in range(share):
                row = jnp.sum(total_ref[j, 2 * k + part].T, axis=0, keepdims=True)
                part_ref[part, lax.rem(ring(k), subs), ring(k) // subs, j : j + 1, :] = row
        start(near_copies(part))

    def forward(units, stages=(), low=0, high=share, step=1):
        step = math.gcd(step, high - low) if high > low else 1

        def products(i, carry):
            for when, stage in stages:
                pl.when(i == (when - low) // step)(stage)
            for j in [low + i * step + d for d in range(step)]:
                for k, part in units:
                    place = pl.multiple_of(ring(k) * rows + part * half, half)
                    feat = feat_ref[pl.ds(place, half), :]
                    total = jnp.zeros((half, 128), F32)
                    for start in range(0, plan.points, plan.tile):
                        cols = slice(start, start + plan.tile)
                        value = jnp.exp2(
                            jnp.dot(feat, table_ref[j, :, cols].astype(BF16), preferred_element_type=F32)
                        )
                        if part == 1 and start // plan.tile < plan.cached:
                            cache_ref[j, k, start // plan.tile] = value
                        for first in range(0, plan.tile, 128):
                            w = table_ref[j, SPARE : SPARE + 1, start + first : start + first + 128]
                            total = total + value[:, first : first + 128] * w
                    total_ref[j, 2 * k + part] = total
            return carry

        lax.fori_loop(0, (high - low) // step, products, 0)

    def when(k):
        return k * share // 8

    forward([(0, 0)], step=4)

    pl.semaphore_wait(barrier, len(peers))
    for peer in flat:
        send(xy_ref.at[me], xy_ref.at[me], xy_sem, (), at(*peer)).start()
    forward([(0, 1)], high=when(4), step=4)
    for load in loads[2:]:
        load.wait()
    gene_tiles = [slice(first, first + plan.wide) for first in range(0, plan.genes, plan.wide)]
    for cols in gene_tiles:
        seen = lax.dot_general(
            pick_ref[...], expr_ref[:, cols], (((0,), (0,)), ((), ())), preferred_element_type=F32
        )
        seen_ref[:, cols] = seen.astype(BF16)
    if flat:
        others = xy_ref.at[pl.ds(0, blocks - 1)]
        drain(xy_sem, (), others, others)
    for k in range(1, blocks):
        cell_features(plan, ring(k), xy_ref, side_ref, feat_ref)

    def near_copies(part):
        return [
            send(part_ref.at[part, lax.rem(s + ds, subs)], near_ref.at[part, ds - 1], near_sem, (part, ds - 1), at(ds=ds))
            for ds in range(1, subs)
        ]

    def latent_copies(part):
        out = []
        for peer in far:
            target = at(*peer)
            out.append(
                send(final_ref.at[part, target["lat"]], latent_recv.at[part, g, l], latent_sem, (part,), target)
            )
        return out

    def rs_copies(part):
        out = []
        for dg in range(1, genes):
            target = at(dg=dg)
            source = chunk_ref.at[part, target["gene"] // plan.split]
            out.append(send(source, rs_ref.at[part, dg - 1], rs_sem, (part,), target))
        return out

    def lg_copies(part):
        out = []
        for peer in flat:
            target = at(*peer)
            out.append(send(own_ref.at[part, target["lat"]], lg_ref.at[part, me], lg_sem, (part,), target))
        return out

    def start(copies):
        for copy in copies:
            copy.start()

    def wait(copies):
        for copy in copies:
            copy.wait()

    def sum_near(part):
        wait(near_copies(part))
        value = part_ref[part, s]
        for ds in range(1, subs):
            value = value + near_ref[part, ds - 1]
        value = value * height[None]
        final_ref[part] = value.astype(final_ref.dtype)
        start(latent_copies(part))
        pltpu.make_async_copy(final_ref.at[part, l], latent_recv.at[part, g, l], latent_sem.at[1, part]).start()

    def middle(part):
        drain(latent_sem, (part,), far_ref if far else None, latent_recv.at[part])
        for lat in range(lats):
            for own in range(plan.owners):
                first = own * plan.split
                value = latent_recv[part, first, lat].astype(F32)
                for other in range(1, plan.split):
                    value = value + latent_recv[part, first + other, lat].astype(F32)
                base = lat * plan.lats + own * share
                side_lat_ref[base : base + share, :] = value
        cells = slice(part * half, (part + 1) * half)
        latent_ref[:, cells] = side_lat_ref[...].astype(BF16)
        turned = side_lat_ref[...].T.astype(BF16)
        cell = jnp.zeros((plan.total, half), F32)
        for cols in gene_tiles:
            mixing = mixing_ref[:, cols]
            predicted = jnp.dot(turned, mixing, preferred_element_type=F32)
            weighted = (noise_ref[:, cols] * (seen_ref[cells, cols].astype(F32) - predicted)).astype(BF16)
            seen_ref[cells, cols] = weighted
            cell = cell + lax.dot_general(
                mixing, weighted, (((1,), (1,)), ((), ())), preferred_element_type=F32
            )
        cell_ref[...] = cell
        for own in range(plan.owners):
            for lat in range(lats):
                base = lat * plan.lats + own * share
                chunk_ref[part, own, lat] = plan.scale * cell_ref[base : base + share, :]
        start(rs_copies(part))

    def sum_gene(part):
        if genes > 1:
            drain(rs_sem, (part,), rs_ref.at[part], rs_ref.at[part])
        value = chunk_ref[part, owner]
        for dg in range(1, genes):
            value = value + rs_ref[part, dg - 1]
        own_ref[part] = value
        start(lg_copies(part))
        pltpu.make_async_copy(own_ref.at[part, l], lg_ref.at[part, me], lg_sem.at[1, part]).start()

    def turn(part):
        drain(lg_sem, (part,), lg_ref.at[part, pl.ds(0, blocks - 1)] if flat else None, lg_ref.at[part])
        for block in range(blocks):
            for p, piece in enumerate(pieces(lg_ref[part, block] * height)):
                lgside_ref[p * share : (p + 1) * share, :] = piece
            lgt_ref[block * half : (block + 1) * half, :] = (
                lgside_ref[...].T[:, : plan.turned].astype(BF16)
            )

    def mix_near_copies():
        return [
            send(mix_ref.at[lax.rem(s + ds, subs)], mix_near.at[ds - 1], mix_sem, (0, ds - 1, 0), at(ds=ds))
            for ds in range(1, subs)
        ]

    def mix_lat_copies(p):
        return [send(mix_all.at[l, p], mix_all.at[l, p], mix_sem, (1, dl - 1, p), at(dl=dl)) for dl in range(1, lats)]

    def mix_back_copies(p):
        return [send(mix_sum.at[p], mix_out.at[s, p], mix_sem, (2, ds - 1, p), at(ds=ds)) for ds in range(1, subs)]

    def mix_keep(p):
        return pltpu.make_async_copy(mix_sum.at[p], mix_out.at[s, p], keep_sem.at[p])

    def mix_part():
        depth = mix_ref.shape[2]
        for cols in gene_tiles:
            value = plan.scale * jnp.dot(latent_ref[...], seen_ref[:, cols], preferred_element_type=F32)
            for sub in range(subs):
                for p in range(lats):
                    base = (sub * lats + p) * depth
                    mix_ref[sub, p, :, cols] = value[base : base + depth, :]
        start(mix_near_copies())

    def mix_sub():
        wait(mix_near_copies())
        for p in range(lats):
            value = mix_ref[s, p]
            for ds in range(1, subs):
                value = value + mix_near[ds - 1, p]
            mix_all[l, p] = code(value)
            start(mix_lat_copies(p))

    def mix_lat(p):
        wait(mix_lat_copies(p))
        value = decode(mix_all[0, p])
        for lat in range(1, lats):
            value = value + decode(mix_all[lat, p])
        mix_sum[p] = value
        start(mix_back_copies(p))
        mix_keep(p).start()

    def gather_copies(j):
        return [
            send(all_ref.at[j], all_out.at[g, j], all_sem, (), at(dg=dg)) for dg in range(1, genes)
        ] + [pltpu.make_async_copy(all_ref.at[j], all_out.at[g, j], all_sem.at[1])]

    def backward(part, stages, step=1):
        step = math.gcd(step, share)

        def products(i, carry):
            for when, stage in stages:
                pl.when(i == when // step)(stage)
            for d in range(step):
                one(i * step + d, d)
            return carry

        def one(j, slot):
            row = lax.broadcasted_iota(jnp.int32, (plan.turned, 128), 0)
            select = (lax.rem(row, share) == j).astype(F32).astype(BF16)
            for k in range(blocks):
                place = pl.multiple_of(ring(k) * half, half)
                turned = lgt_ref[pl.ds(place, half), :]
                wide_ref[slot, k] = jnp.dot(turned, select, preferred_element_type=F32)
            tiles = list(range(plan.points // plan.tile))
            kept = tiles[: plan.cached] if part == 1 else []
            fresh = tiles[len(kept) :]
            lanes = plan.tile // 128
            held = [(t, f) for t in kept for f in range(lanes)]
            held_sums = [None] * len(held)
            packs = [range(i, min(i + PACK, len(held))) for i in range(0, len(held), PACK)]
            groups = [(pack, k, r) for pack in packs for k in range(blocks) for r in range(0, half, 8)]
            steps = len(fresh) * blocks
            pace = -(-len(groups) // max(1, steps))

            def settle(sums, t, f):
                r = t * lanes + f
                here = slice(r * 128, (r + 1) * 128)
                if part == 0:
                    sum_ref[j, :, here] = sums
                else:
                    row_ref[r : r + 1, :] = jnp.sum(sum_ref[j, :, here] + sums, axis=0, keepdims=True)

            def spend(groups):
                for pack, k, r in groups:
                    wide = wide_ref[slot, k, r : r + 8, :]
                    for i in pack:
                        t, f = held[i]
                        term = cache_ref[j, k, t, r : r + 8, f * 128 : (f + 1) * 128] * wide
                        held_sums[i] = term if held_sums[i] is None else held_sums[i] + term

            for t in fresh:
                points = table_ref[j, :, t * plan.tile : (t + 1) * plan.tile].astype(BF16)
                sums = [None] * lanes
                for k in range(blocks):
                    place = pl.multiple_of(ring(k) * rows + part * half, half)
                    value = jnp.exp2(
                        jnp.dot(feat_ref[pl.ds(place, half), :], points, preferred_element_type=F32)
                    )
                    for f in range(lanes):
                        term = value[:, f * 128 : (f + 1) * 128] * wide_ref[slot, k]
                        term = jnp.sum(term.reshape(half // 8, 8, 128), axis=0)
                        sums[f] = term if sums[f] is None else sums[f] + term
                    spend(groups[:pace])
                    groups = groups[pace:]
                for f in range(lanes):
                    settle(sums[f], t, f)
            spend(groups)
            for (t, f), sums in zip(held, held_sums):
                settle(sums, t, f)
            if part == 1:
                all_ref[j] = code(row_ref[...])
                start(gather_copies(j))

        lax.fori_loop(0, share // step, products, 0)

    forward([(k, 0) for k in range(1, blocks)], step=2)
    flush(0)
    forward([(0, 1)], low=when(4), high=when(6), step=2)
    sum_near(0)
    forward([(0, 1)], low=when(6), step=2)
    others = [(k, 1) for k in range(1, blocks)]
    forward(others, high=when(3), step=3)
    middle(0)
    forward(others, low=when(3), high=when(7), step=4)
    sum_gene(0)
    forward(others, low=when(7))
    flush(1)
    lgside_ref[...] = jnp.zeros_like(lgside_ref)
    turn(0)
    backward(
        0,
        [
            (when(0), lambda: sum_near(1)),
            (when(4), lambda: middle(1)),
            (when(6), mix_part),
            (when(6), lambda: sum_gene(1)),
        ],
        step=2,
    )
    mix_sub()
    turn(1)
    early = max(1, lats // 2)

    def first_parts():
        for p in range(early):
            mix_lat(p)

    backward(1, [(when(6), first_parts)])
    for p in range(early, lats):
        mix_lat(p)

    drain(all_sem, (), all_out.at[pl.ds(0, genes - 1)] if genes > 1 else None, all_out)
    for p in range(lats):
        wait(mix_back_copies(p))
        mix_keep(p).wait()


def lay_body(plan, mix_hbm, all_hbm, mix_out, ind_out, mix_ref, all_ref, row_ref, ind_ref, in_sem, out_sem):
    subs, lats = mix_hbm.shape[:2]
    parts = [(sub, p) for sub in range(subs) for p in range(lats)]
    codes = pltpu.make_async_copy(all_hbm, all_ref, in_sem.at[len(parts)])
    mix_in = [
        pltpu.make_async_copy(mix_hbm.at[part], mix_ref.at[part], in_sem.at[i]) for i, part in enumerate(parts)
    ]
    mix_back = [
        pltpu.make_async_copy(mix_ref.at[part], mix_out.at[part], out_sem.at[i]) for i, part in enumerate(parts)
    ]
    for copy in [codes] + mix_in:
        copy.start()
    codes.wait()
    for owner in range(plan.owners):
        base = owner * plan.share
        for slab in range(plan.split):
            gene = owner * plan.split + slab
            for j in range(plan.share):
                row_ref[gene, j] = decode(all_ref[gene, j])
            for r in range(plan.points // 128):
                first = slab * plan.points + r * 128
                ind_ref[base : base + plan.share, first : first + 128] = row_ref[gene, :, r, :]
    ind_back = pltpu.make_async_copy(ind_ref, ind_out, out_sem.at[len(parts)])
    ind_back.start()
    for copy, back in zip(mix_in, mix_back):
        copy.wait()
        back.start()
    for back in mix_back + [ind_back]:
        back.wait()


def lay(plan, mix, codes):
    anywhere = pl.BlockSpec(memory_space=pl.ANY)
    return pl.pallas_call(
        functools.partial(lay_body, plan),
        in_specs=[anywhere] * 2,
        out_specs=[anywhere] * 2,
        out_shape=[
            jax.ShapeDtypeStruct(mix.shape, F32),
            jax.ShapeDtypeStruct((plan.lats, plan.count), F32),
        ],
        scratch_shapes=[
            pltpu.VMEM(mix.shape, F32),
            pltpu.VMEM(codes.shape, jnp.int16),
            pltpu.VMEM((plan.gene, plan.share, plan.points // 128, 128), F32),
            pltpu.VMEM((plan.lats, plan.count), F32),
            pltpu.SemaphoreType.DMA((plan.blocks + 1,)),
            pltpu.SemaphoreType.DMA((plan.blocks + 1,)),
        ],
        compiler_params=pltpu.CompilerParams(vmem_limit_bytes=60 * 2**20),
    )(mix, codes)


def fused(plan, *args):
    genes, lats, subs = plan.gene, plan.lat, plan.sub
    rows, half, share, blocks = plan.rows, plan.half, plan.share, plan.blocks
    depth = plan.total // (lats * subs)
    sent = BF16 if plan.split == 1 else F32
    dma = pltpu.SemaphoreType.DMA
    far = genes * lats - 1
    flat = blocks - 1
    anywhere = pl.BlockSpec(memory_space=pl.ANY)
    scratch = [
        pltpu.VMEM((1, rows), jnp.int32),
        pltpu.VMEM((2, plan.table), F32),
        pltpu.VMEM((1, plan.lats), F32),
        pltpu.VMEM((1, plan.lats), F32),
        pltpu.VMEM((plan.table, plan.genes), BF16),
        pltpu.VMEM((2, share, plan.points), F32),
        pltpu.VMEM((share, plan.points), F32),
        pltpu.VMEM((plan.total, plan.genes), BF16),
        pltpu.VMEM((1, plan.genes), F32),
        pltpu.VMEM((plan.table, rows), BF16),
        pltpu.VMEM((blocks, 2, rows), F32),
        pltpu.VMEM((128, rows), F32),
        pltpu.VMEM((blocks * rows, DEPTH), BF16),
        pltpu.VMEM((share, DEPTH, plan.points), F32),
        pltpu.VMEM((share, 2 * blocks, half, 128), F32),
        pltpu.VMEM((2, subs, lats, share, half), F32),
        pltpu.VMEM((2, max(1, subs - 1), lats, share, half), F32),
        pltpu.VMEM((2, lats, share, half), sent),
        pltpu.VMEM((2, genes, lats, share, half), sent),
        pltpu.VMEM((plan.total, rows), BF16),
        pltpu.VMEM((plan.total, half), F32),
        pltpu.VMEM((rows, plan.genes), BF16),
        pltpu.VMEM((plan.total, half), F32),
        pltpu.VMEM((2, plan.owners, lats, share, half), F32),
        pltpu.VMEM((2, max(1, genes - 1), lats, share, half), F32),
        pltpu.VMEM((2, lats, share, half), F32),
        pltpu.VMEM((2, blocks, share, half), F32),
        pltpu.VMEM((128, half), F32),
        pltpu.VMEM((blocks * half, plan.turned), BF16),
        pltpu.VMEM((2, blocks, half, 128), F32),
        pltpu.VMEM((subs, lats, depth, plan.genes), F32),
        pltpu.VMEM((max(1, subs - 1), lats, depth, plan.genes), F32),
        pltpu.VMEM((lats, lats, depth, plan.genes), jnp.int16),
        pltpu.VMEM((lats, depth, plan.genes), F32),
        pltpu.VMEM((share, 8, plan.points), F32),
        pltpu.VMEM((plan.points // 128, 128), F32),
        pltpu.VMEM((share, plan.points // 128, 128), jnp.int16),
        pltpu.VMEM((share, blocks, max(1, plan.cached), half, plan.tile), F32),
        pltpu.VMEM((max(1, far), share, half), sent),
        dma((9,)),
        dma((2,)),
        dma((2, 2, max(1, subs - 1))),
        dma((2, 2)),
        dma((2, 2)),
        dma((2, 2)),
        dma((2, 3, max(1, subs - 1, lats - 1), lats)),
        dma((2,)),
        dma((lats,)),
    ]
    return pl.pallas_call(
        functools.partial(body, plan),
        in_specs=[anywhere] * 9,
        out_specs=[anywhere] * 2,
        out_shape=[
            jax.ShapeDtypeStruct((subs, lats, depth, plan.genes), F32),
            jax.ShapeDtypeStruct((genes, share, plan.points // 128, 128), jnp.int16),
        ],
        scratch_shapes=scratch,
        compiler_params=pltpu.CompilerParams(
            collective_id=0, has_side_effects=True, vmem_limit_bytes=67043328
        ),
    )(*args)


def on_device(
    cell_index,
    coords_table,
    expr_table,
    inducing,
    ind_weights,
    lengthscale,
    variance,
    mixing,
    noise_prec,
):
    genes, lats, subs = (lax.axis_size(axis) for axis in ("gene", "lat", "sub"))
    latents, count = ind_weights.shape
    owners = math.gcd(genes, latents)
    split = genes // owners
    share = latents // owners
    plan = Plan(
        gene=genes,
        lat=lats,
        sub=subs,
        rows=cell_index.shape[0],
        table=coords_table.shape[1],
        lats=latents,
        count=count,
        genes=expr_table.shape[1],
        share=share,
        split=split,
        sliced=share % 8 != 0,
        scale=-1.0 / math.sqrt(cell_index.shape[0] * lats * subs),
    )
    if plan.sliced:
        place = lax.axis_index("gene")
        first, cut = place // split * share, lax.rem(place, split) * plan.points
        inducing = lax.dynamic_slice(inducing, (0, first, cut), (2, share, plan.points))
        ind_weights = lax.dynamic_slice(ind_weights, (first, cut), (share, plan.points))
    mix, codes = fused(
        plan,
        cell_index[None, :],
        coords_table,
        lengthscale[None, :],
        variance[None, :],
        expr_table,
        inducing,
        ind_weights,
        mixing,
        noise_prec[None, :],
    )
    grad_mixing, grad_inducing = lay(plan, mix, codes)
    return grad_mixing.reshape(mixing.shape), grad_inducing


def solution(mesh):
    in_specs = (
        P(("group", "lat", "sub")),
        P("group", ("lat", "sub")),
        P(("group", "lat", "sub"), "gene"),
        P("group", "lat", "sub"),
        P(("group", "lat"), "sub"),
        P(("group", "lat")),
        P(("group", "lat")),
        P("group", "gene"),
        P(("group", "gene")),
    )
    out_specs = (P("group", "gene"), P(("group", "lat"), "sub"))
    return jax.shard_map(
        on_device, mesh=mesh, in_specs=in_specs, out_specs=out_specs, check_vma=False
    )
```
